32 devices in a mesh: dp: 8 (over z, y), seq: 4 (over x, core).
Axes of the slice: x: 2, y: 2, z: 4, core: 2. Of those that a mesh axis runs over, the one named last changes fastest.
Arguments:
- block_input: bfloat16 [8, 512, 1024], P('dp', 'seq'), may hold values from -6 to 6
- in_weight: bfloat16 [1024, 4384], P(('dp', 'seq')), may hold values from -0.1875 to 0.1875
- out_weight: bfloat16 [2048, 1024], P(None, ('dp', 'seq')), may hold values from -0.125 to 0.125
- pre_gain: bfloat16 [1024], P(('dp', 'seq')), may hold values from 0.099609375 to 1.8984375
- norm_gain: bfloat16 [2048], P(('dp', 'seq')), may hold values from 0.099609375 to 1.8984375
- conv_weight: bfloat16 [4, 2304], P(None, ('dp', 'seq')), may hold values from -3 to 3
- conv_bias: bfloat16 [2304], P(('dp', 'seq')), may hold values from -1.5 to 1.5
- dt_bias: float32 [32], replicated, may hold values from -11 to -2, as said below
- decay_log: float32 [32], replicated, may hold values from 0 to 1
- skip_gain: float32 [32], replicated, may hold values from 0.5 to 1.5
- cotangent: bfloat16 [8, 512, 1024], P('dp', 'seq'), may hold values from -6 to 6
Outputs:
- block_output: bfloat16 [8, 512, 1024], P('dp', 'seq')
- input_grad: float32 [8, 512, 1024], P('dp', 'seq')
- in_weight_grad: float32 [1024, 4384], P(('dp', 'seq'))
- out_weight_grad: float32 [2048, 1024], P(None, ('dp', 'seq'))
- pre_gain_grad: float32 [1024], P(('dp', 'seq'))
- norm_gain_grad: float32 [2048], P(('dp', 'seq'))
- conv_weight_grad: float32 [4, 2304], P(None, ('dp', 'seq'))
- conv_bias_grad: float32 [2304], P(('dp', 'seq'))
- dt_bias_grad: float32 [32], replicated
- decay_log_grad: float32 [32], replicated
- skip_gain_grad: float32 [32], replicated
The draws below stay inside these ranges and needn't reach their ends.
Inputs may be any that keep to these rules, and one draw needn't show every extreme that they name: `dt_bias`: each head's bias is a float between -11 and -2.
All inputs are finite; a program needn't handle non-finite values.
Results may differ from the reference program's by a relative error of at most 0.0067.
Values may be sent and summed in bfloat16 or wider, within the bound.
A program may use at most 256 MiB of HBM per device.

```python
import jax
import jax.numpy as jnp
from jax import lax

D = 1024
HEADS = 32
HEAD_DIM = 64
STATE = 128
CONV = 4
GROUP = 128
INNER = 2048
CONV_CH = 2304
PROJ = 4384
SEQS = 8
LENGTH = 512


def draw_dt_bias(key, part):
    key_order, key_slow, key_fast = jax.random.split(jax.random.fold_in(key, 11), 3)
    order = jax.random.permutation(key_order, HEADS)
    slow_count = HEADS // 2
    slow_values = jnp.log(jax.random.uniform(key_slow, (HEADS,), jnp.float32, 0.05, 0.3) / LENGTH)
    fast_values = jax.random.uniform(key_fast, (HEADS,), jnp.float32, -4.0, -2.5)
    return jnp.where(order < slow_count, slow_values, fast_values).astype(jnp.float32)


def with_spikes(entries, stream_key, source, target, shards_of, factor):
    owner, partner = [(jnp.arange(entries.shape[dim]) // (entries.shape[dim] // shards_of)).reshape([-1 if axis == dim else 1 for axis in range(entries.ndim)]) for dim in (source, target)]
    chosen = jax.random.permutation(stream_key, shards_of)[partner]
    strong = (owner == chosen) | (owner == (partner + shards_of // 2) % shards_of)
    return jnp.where(strong, factor * entries, entries)


def levels(rng, dims, cuts, least, high):
    factor_of = 1.0
    for dim, parts in cuts:
        steps = jax.random.uniform(jax.random.fold_in(jax.random.fold_in(rng, 6), dim), (parts,), jnp.float32, least / len(cuts), high / len(cuts))
        factor_of = factor_of * jnp.repeat(jnp.exp(steps), dims[dim] // parts).reshape((-1,) + (1,) * (len(dims) - 1 - dim))
    return factor_of


def scatter_about(own_key, extent, scale, reach, cuts=(), dtype=jnp.bfloat16):
    factor_of = levels(own_key, extent, cuts, -0.22, 0.18) if cuts else 1.0
    entries = jax.random.normal(own_key, extent, jnp.float32) * scale * factor_of
    return jnp.minimum(jnp.maximum(entries, -reach), reach).astype(dtype)


def heavy_noise(stream_key, shape, scale, most, pieces, heavy, kind=jnp.bfloat16):
    array = scale * jax.random.normal(stream_key, shape, jnp.float32)
    if pieces:
        array = array * levels(stream_key, shape, pieces, -0.22, 0.18)
    return jnp.clip(with_spikes(array, jax.random.fold_in(stream_key, 3), *heavy), -most, most).astype(kind)


def setup_inputs(seed: int = 0) -> dict:
    arg_keys = jax.random.split(jax.random.key(seed), 12)
    return {
        "block_input": heavy_noise(arg_keys[0], (SEQS, LENGTH, D), 1.0, 6.0, ((0, 8), (1, 4)), (0, 2, 8, 2.0)),
        "in_weight": scatter_about(arg_keys[1], (D, PROJ), D ** -0.5, 0.1875, ((0, 32),)),
        "out_weight": scatter_about(arg_keys[2], (INNER, D), INNER ** -0.5, 0.125, ((1, 32),)),
        "pre_gain": jnp.clip(1.0 + 0.18 * jax.random.normal(arg_keys[3], (D,), jnp.float32), 0.099609375, 1.8984375).astype(jnp.bfloat16),
        "norm_gain": jnp.clip(1.0 + 0.18 * jax.random.normal(arg_keys[4], (INNER,), jnp.float32), 0.099609375, 1.8984375).astype(jnp.bfloat16),
        "conv_weight": scatter_about(arg_keys[5], (CONV, CONV_CH), CONV ** -0.5, 3.0, ((1, 32),)),
        "conv_bias": scatter_about(arg_keys[6], (CONV_CH,), 0.3, 1.5, ((0, 32),)),
        "dt_bias": draw_dt_bias(jax.random.fold_in(arg_keys[11], 71), 0),
        "decay_log": jnp.clip(jax.random.uniform(arg_keys[8], (HEADS,), jnp.float32, 0.0, 1.0), 0.0, 1.0),
        "skip_gain": jnp.clip(jax.random.uniform(arg_keys[9], (HEADS,), jnp.float32, 0.5, 1.5), 0.5, 1.5),
        "cotangent": heavy_noise(arg_keys[10], (SEQS, LENGTH, D), 1.0, 6.0, ((0, 8), (1, 4)), (0, 2, 8, 2.0)),
    }


epsilon = 1e-05
highest = lax.Precision.HIGHEST

def convolve(padded, conv_weight, conv_bias):
    taps = conv_weight.shape[0]
    length = padded.shape[-2] - taps + 1
    total = conv_bias
    for index in range(taps):
        total = total + conv_weight[index] * lax.slice_in_dim(padded, index, index + length, axis=padded.ndim - 2)
    return total

def front(projected, rim, conv_weight, conv_bias, dt_bias, decay_log):
    gate_raw = projected[..., :INNER]
    conv_in = projected[..., INNER:INNER + CONV_CH]
    dt_raw = projected[..., INNER + CONV_CH:]
    padded = jnp.concatenate([rim, conv_in], axis=-2)
    conv_out = jax.nn.silu(convolve(padded, conv_weight, conv_bias))
    values = conv_out[..., :INNER]
    in_map = conv_out[..., INNER:INNER + STATE]
    out_map = conv_out[..., INNER + STATE:]
    step = jax.nn.softplus(dt_raw + dt_bias)
    return (gate_raw, values, in_map, out_map, step)

def group_state(values, in_map, step, cumulative):
    weights_end = jnp.exp(cumulative[-1][None, :] - cumulative) * step
    state = jnp.einsum('shp,sn->hpn', values * weights_end[:, :, None], in_map, precision=highest)
    return (state, jnp.exp(cumulative[-1]))

def group_output(values, in_map, out_map, step, cumulative, carried, skip_gain):
    length = values.shape[0]
    scores = jnp.dot(out_map, in_map.T, precision=highest)
    causal = jnp.arange(length)[:, None] >= jnp.arange(length)[None, :]
    spread = cumulative[:, None, :] - cumulative[None, :, :]
    decay = jnp.exp(jnp.where(causal[:, :, None], spread, -10000.0))
    mixing = scores[:, :, None] * decay * step[None, :, :]
    inner_part = jnp.einsum('tsh,shp->thp', mixing, values, precision=highest)
    carried_part = jnp.einsum('tn,hpn->thp', out_map, carried, precision=highest) * jnp.exp(cumulative)[:, :, None]
    return inner_part + carried_part + skip_gain[None, :, None] * values

def gate_norm(ssd_out, gate_raw, norm_gain):
    gated = ssd_out * jax.nn.silu(gate_raw)
    inverse = lax.rsqrt(lax.optimization_barrier(jnp.mean(gated * gated, axis=-1, keepdims=True)) + epsilon)
    return gated * inverse * norm_gain

def middle(projected, conv_weight, conv_bias, dt_bias, decay_log, skip_gain, norm_gain):
    length = projected.shape[0]
    rim = jnp.zeros((CONV - 1, CONV_CH), jnp.float32)
    gate_raw, values, in_map, out_map, step = front(projected, rim, conv_weight, conv_bias, dt_bias, decay_log)
    groups = length // GROUP
    values = values.reshape(groups, GROUP, HEADS, HEAD_DIM)
    in_map = in_map.reshape(groups, GROUP, STATE)
    out_map = out_map.reshape(groups, GROUP, STATE)
    step = step.reshape(groups, GROUP, HEADS)
    cumulative = jnp.cumsum(step * -jnp.exp(decay_log), axis=1)
    states, decays = jax.vmap(group_state)(values, in_map, step, cumulative)

    def carry_step(carry, pair):
        decay_now, state_now = pair
        return (decay_now[:, None, None] * carry + state_now, carry)
    start = jnp.zeros((HEADS, HEAD_DIM, STATE), jnp.float32)
    unused, carried = lax.scan(carry_step, start, (decays, states))
    ssd_out = jax.vmap(group_output, in_axes=(0, 0, 0, 0, 0, 0, None))(values, in_map, out_map, step, cumulative, carried, skip_gain)
    return gate_norm(ssd_out.reshape(length, INNER), gate_raw, norm_gain)

def reference(block_input, in_weight, out_weight, pre_gain, norm_gain, conv_weight, conv_bias, dt_bias, decay_log, skip_gain, cotangent):
    pre_float = pre_gain.astype(jnp.float32)
    norm_float = norm_gain.astype(jnp.float32)
    conv_w_float = conv_weight.astype(jnp.float32)
    conv_b_float = conv_bias.astype(jnp.float32)

    def one_sequence(totals, pair):
        block, grad_out = pair
        inputs = block.astype(jnp.float32)
        inv_pre = lax.rsqrt(lax.optimization_barrier(jnp.mean(inputs * inputs, axis=-1, keepdims=True)) + epsilon)
        normed = (inputs * inv_pre * pre_float).astype(jnp.bfloat16)
        projected = jnp.dot(normed, in_weight, preferred_element_type=jnp.float32)
        mixed_float, pullback = jax.vjp(middle, projected, conv_w_float, conv_b_float, dt_bias, decay_log, skip_gain, norm_float)
        mixed = mixed_float.astype(jnp.bfloat16)
        output = (inputs + jnp.dot(mixed, out_weight, preferred_element_type=jnp.float32)).astype(jnp.bfloat16)
        mixed_grad = jnp.dot(grad_out, out_weight.T, preferred_element_type=jnp.float32)
        out_w_grad = jnp.dot(mixed.T, grad_out, preferred_element_type=jnp.float32)
        proj_float, conv_w_grad, conv_b_grad, dt_grad, decay_grad, skip_grad, norm_grad = pullback(mixed_grad)
        proj_grad = proj_float.astype(jnp.bfloat16)
        in_w_grad = jnp.dot(normed.T, proj_grad, preferred_element_type=jnp.float32)
        normed_grad = jnp.dot(proj_grad, in_weight.T, preferred_element_type=jnp.float32)
        pre_grad = lax.optimization_barrier(jnp.sum(normed_grad * inputs * inv_pre, axis=0))
        scaled = normed_grad * pre_float
        unit = inputs * inv_pre
        input_grad = inv_pre * (scaled - unit * lax.optimization_barrier(jnp.mean(scaled * unit, axis=-1, keepdims=True))) + grad_out.astype(jnp.float32)
        terms = (in_w_grad, out_w_grad, pre_grad, norm_grad, conv_w_grad, conv_b_grad, dt_grad, decay_grad, skip_grad)
        totals = tuple((total + term for total, term in zip(totals, terms)))
        return (totals, (output, input_grad))
    zeros = (jnp.zeros((D, PROJ), jnp.float32), jnp.zeros((INNER, D), jnp.float32), jnp.zeros((D,), jnp.float32), jnp.zeros((INNER,), jnp.float32), jnp.zeros((CONV, CONV_CH), jnp.float32), jnp.zeros((CONV_CH,), jnp.float32), jnp.zeros((HEADS,), jnp.float32), jnp.zeros((HEADS,), jnp.float32), jnp.zeros((HEADS,), jnp.float32))
    totals, stacked = lax.scan(one_sequence, zeros, (block_input, cotangent))
    return (stacked[0], stacked[1], totals[0], totals[1], totals[2], totals[3], totals[4], totals[5], totals[6], totals[7], totals[8])
```

```python
import functools

import jax
import jax.numpy as jnp
from jax import lax
from jax.experimental import pallas as pl
from jax.experimental.pallas import tpu as pltpu
from jax.sharding import PartitionSpec as P

HEADS = 32
HEAD_DIM = 64
STATE = 128
CONV = 4
GROUP = 128
INNER = 2048
CONV_CH = 2304
LANES = 128
MAPS = CONV_CH - INNER
SHARED = MAPS + LANES


epsilon = 1e-05
highest = lax.Precision.HIGH
bf16 = jnp.bfloat16
f32 = jnp.float32


def at(start, size, multiple):
    return pl.ds(start if isinstance(start, int) else pl.multiple_of(start, multiple), size)


def remote(src, dst, send, recv, device):
    return pltpu.make_async_remote_copy(
        src_ref=src,
        dst_ref=dst,
        send_sem=send,
        recv_sem=recv,
        device_id=device,
        device_id_type=pl.DeviceIdType.MESH,
    )


class Site:
    def __init__(self, dp, seq, send, recv, own):
        self.nz, self.ns = dp // 2, seq
        self.d, self.s = lax.axis_index("dp"), lax.axis_index("seq")
        self.y, self.z = lax.rem(self.d, 2), self.d // 2
        self.owner = self.d * seq + self.s
        self.send, self.recv, self.own = send, recv, own
        self.used, self.used_own = 0, 0
        self.pending = []

    def group(self, k):
        return (self.d, lax.rem(self.s + k, self.ns))

    def column(self, k):
        return (lax.rem(self.z + k, self.nz) * 2 + self.y, self.s)

    def across(self):
        return (self.z * 2 + 1 - self.y, self.s)

    def take(self, count):
        self.used += count
        return self.used - count

    def copy(self, src, dst, slot, device):
        return remote(src, dst, self.send.at[slot], self.recv.at[slot], device)

    def greet(self):
        barrier = pltpu.get_barrier_semaphore()
        partners = [self.group(k) for k in range(1, self.ns)]
        partners += [self.column(k) for k in range(1, self.nz)] + [self.across()]
        for partner in partners:
            pl.semaphore_signal(
                barrier, inc=1, device_id=partner, device_id_type=pl.DeviceIdType.MESH
            )
        pl.semaphore_wait(barrier, len(partners))


class GroupCopy:
    def __init__(self, site, source, dest, local):
        self.site, self.source, self.dest, self.local = site, source, dest, local
        self.base = site.take(site.ns - 1)
        if local:
            self.own = site.used_own
            site.used_own += 1
        site.pending.append(self.drain)

    def own_copy(self):
        site = self.site
        return pltpu.make_async_copy(self.source(site.s), self.dest(0), site.own.at[self.own])

    def copy(self, k):
        site = self.site
        member = lax.rem(site.s + k, site.ns)
        return site.copy(self.source(member), self.dest(k), self.base + k - 1, site.group(k))

    def start(self):
        for k in range(1, self.site.ns):
            self.copy(k).start()
        if self.local:
            self.own_copy().start()

    def wait(self):
        if self.local:
            self.own_copy().wait()
        for k in range(1, self.site.ns):
            self.copy(k).wait_recv()

    def drain(self):
        for k in range(1, self.site.ns):
            self.copy(k).wait_send()


class Spread:
    def __init__(self, site, buf, rows, source):
        self.site, self.buf, self.rows, self.source = site, buf, rows, source
        self.block_rows = site.ns * rows
        self.members = GroupCopy(
            site, source, lambda k: buf.at[at(site.owner * rows, rows, rows)], True
        )
        self.z0, self.y0 = site.take(site.nz - 1), site.take(site.nz)
        site.pending.append(self.drain)

    def block(self, d):
        return self.buf.at[at(d * self.block_rows, self.block_rows, self.block_rows)]

    def z_copy(self, k):
        site = self.site
        block = self.block(site.d)
        return site.copy(block, block, self.z0 + k - 1, site.column(k))

    def y_copy(self, k):
        site = self.site
        block = self.block(lax.rem(site.z + site.nz - k, site.nz) * 2 + site.y)
        return site.copy(block, block, self.y0 + k, site.across())

    def begin(self):
        self.members.wait()
        for k in range(1, self.site.nz):
            self.z_copy(k).start()
        self.y_copy(0).start()

    def forward(self, k):
        self.z_copy(k).wait_recv()
        self.y_copy(k).start()

    def finish(self):
        for k in range(self.site.nz):
            self.y_copy(k).wait_recv()

    def drain(self):
        for k in range(1, self.site.nz):
            self.z_copy(k).wait_send()
        for k in range(self.site.nz):
            self.y_copy(k).wait_send()


class Fold:
    def __init__(self, site, grad, rows, ybox, zout, zbox, total, final):
        self.site, self.grad, self.rows = site, grad, rows
        self.block_rows = site.ns * rows
        self.ybox, self.zout, self.zbox, self.total, self.final = ybox, zout, zbox, total, final
        self.y0, self.z0 = site.take(site.nz), site.take(site.nz - 1)
        self.members = GroupCopy(
            site,
            lambda q: total.at[at(q * rows, rows, rows)],
            lambda k: final.at[site.s],
            False,
        )
        site.pending.append(self.drain)

    def level(self, k):
        return lax.rem(self.site.z + k, self.site.nz)

    def rows_of(self, d):
        return at(d * self.block_rows, self.block_rows, self.block_rows)

    def mine(self, k):
        return self.rows_of(self.level(k) * 2 + self.site.y)

    def other(self, k):
        return self.rows_of(self.level(k) * 2 + 1 - self.site.y)

    def y_copy(self, k):
        site = self.site
        return site.copy(
            self.grad.at[self.other(k)], self.ybox.at[k], self.y0 + k, site.across()
        )

    def z_copy(self, k):
        site = self.site
        return site.copy(
            self.zout.at[k - 1], self.zbox.at[k - 1], self.z0 + k - 1, site.column(k)
        )

    def forward(self, k):
        self.y_copy(k).wait_recv()
        pair = self.grad[self.mine(k)].astype(f32) + self.ybox[k].astype(f32)
        self.zout[k - 1] = pair.astype(self.zout.dtype)
        self.z_copy(k).start()

    def finish(self):
        site = self.site
        self.y_copy(0).wait_recv()
        total = self.grad[self.mine(0)].astype(f32) + self.ybox[0].astype(f32)
        for k in range(1, site.nz):
            self.z_copy(k).wait_recv()
            total = total + self.zbox[k - 1].astype(f32)
        self.total[...] = total.astype(self.total.dtype)
        self.members.start()
        self.final[site.s] = self.total[at(site.s * self.rows, self.rows, self.rows)]

    def drain(self):
        for k in range(self.site.nz):
            self.y_copy(k).wait_send()
        for k in range(1, self.site.nz):
            self.z_copy(k).wait_send()


def dot(a, b):
    return jnp.dot(a, b, preferred_element_type=f32)


def dot_nt(a, b):
    return lax.dot_general(a, b, (((1,), (1,)), ((), ())), preferred_element_type=f32)


def split(value, parts):
    pieces = []
    for _ in range(parts - 1):
        pieces.append(value.astype(bf16))
        value = value - pieces[-1].astype(f32)
    return pieces + [value.astype(bf16)]


def exact(product, value, onehot, parts):
    total = None
    for piece in split(value, parts)[::-1]:
        term = product(piece, onehot)
        total = term if total is None else total + term
    return total


def wide(product, a, b, passes):
    if passes == 1:
        return product(a.astype(bf16), b.astype(bf16))
    (a_hi, a_lo), (b_hi, b_lo) = split(a, 2), split(b, 2)
    total = product(a_hi, b_lo)
    if passes == 3:
        total = total + product(a_lo, b_hi)
    return total + product(a_hi, b_hi)


def mm(a, b, passes=3):
    return wide(dot, a, b, passes)


def mm_nt(a, b, passes=3):
    return wide(dot_nt, a, b, passes)


def iota(shape, axis):
    return lax.broadcasted_iota(jnp.int32, shape, axis)


def sigmoid(value):
    return 1.0 / (1.0 + jnp.exp(-value))


def softplus(value):
    small = jnp.exp(-jnp.abs(value))
    series = small * (1.0 - small * (0.5 - small * (1 / 3 - small * (0.25 - small * 0.2))))
    return jnp.maximum(value, 0.0) + jnp.where(small < 0.03, series, jnp.log(1.0 + small))


def rows_sum(value):
    return jnp.sum(value, axis=0, keepdims=True)


def lanes_sum(value):
    return jnp.sum(value, axis=1, keepdims=True)


class Table:
    def __init__(self, owners, channel, size):
        count = channel.shape[1]
        first = iota((owners, count), 0) * size
        place = channel - first
        self.mask = (place >= 0) & (place < size)
        spot = jnp.sum(jnp.where(self.mask, place.astype(f32), 0.0), axis=0, keepdims=True)
        self.onehot = (iota((LANES, count), 0).astype(f32) == spot).astype(f32).astype(bf16)

    def row(self, blocks):
        return rows_sum(jnp.where(self.mask, dot(blocks.astype(bf16), self.onehot), 0.0))

    def blocks(self, row):
        return exact(dot_nt, jnp.where(self.mask, row, 0.0), self.onehot, 3)


def scratch_plan(dp, seq, length, width, rows):
    nz, owners, tokens = dp // 2, dp * seq, seq * length
    w = INNER // seq
    cw, groups, block = w + MAPS, tokens // GROUP, seq * rows
    plan = dict(
        XF=((tokens, width), bf16),
        CF=((tokens, width), bf16),
        WV=((width, w), bf16),
        WS=((width, SHARED), bf16),
        WG=((width, w), bf16),
        WO=((width, w), bf16),
        SM=((owners, 8, LANES), f32),
        XN=((tokens, width), bf16),
        NT=((width, tokens), bf16),
        CT=((width, tokens), bf16),
        INV=((tokens, LANES), f32),
        GA=((8, width), f32),
        NG=((8, w), f32),
        CW=((8, cw), f32),
        EM=((LANES, w), bf16),
        CI=((8 + tokens, cw), f32),
        PRE=((tokens, cw), f32),
        DT=((tokens, LANES), f32),
        CAR=((groups, STATE, w), f32),
        RUN=((STATE, w), f32),
        SSD=((tokens, w), f32),
        GR=((tokens, w), f32),
        GT=((tokens, w), f32),
        MG=((tokens, w), f32),
        ST=((8, tokens), f32),
        EX=((seq - 1, 8, tokens), f32),
        MX=((tokens, w), bf16),
        PG=((tokens, w), bf16),
        DY=((tokens, w), f32),
        PV=((tokens, w), bf16),
        PS=((tokens, SHARED), bf16),
        DP=((tokens + 8, cw), f32),
        OP=((tokens, width), bf16),
        OB=((seq - 1, length, width), bf16),
        NP=((tokens, width), bf16),
        NB=((seq - 1, length, width), bf16),
        CACC=((8, cw), f32),
        NACC=((8, w), f32),
        HACC=((8, LANES), f32),
        PACC=((8, width), f32),
    )
    for name, columns in (("O", w), ("G", w), ("V", w), ("S", SHARED)):
        plan["G" + name] = ((width, columns), bf16)
        plan["Y" + name] = ((nz, block, columns), bf16)
        plan["A" + name] = ((nz - 1, block, columns), bf16)
        plan["Z" + name] = ((nz - 1, block, columns), bf16)
        plan["T" + name] = ((block, columns), bf16)
        plan["F" + name] = ((seq, rows, columns), bf16)
    tile = (8, LANES)
    plan["GM"] = ((owners,) + tile, f32)
    plan["YM"] = ((nz, seq) + tile, f32)
    plan["AM"] = ((nz - 1, seq) + tile, f32)
    plan["ZM"] = ((nz - 1, seq) + tile, f32)
    plan["TM"] = ((seq,) + tile, f32)
    plan["FM"] = ((seq, 1) + tile, f32)
    return plan


def fused_kernel(dp, seq, names, sems, *refs):
    x_ref, cot_ref, inw_ref, sh_ref, outt_ref, small_ref, heads_ref = refs[:7]
    block_ref, ingrad_ref, inshare_ref, outshare_ref, smallout_ref = refs[7:12]
    b = dict(zip(names, refs[12 : 12 + len(names)]))
    send, recv, own = refs[12 + len(names) :]
    site = Site(dp, seq, send, recv, own)
    nz, owners = dp // 2, dp * seq
    length, width = x_ref.shape
    rows = inw_ref.shape[0]
    tokens = seq * length
    groups = tokens // GROUP
    w = INNER // seq
    cw = w + MAPS
    pairs = w // LANES
    block_rows = seq * rows
    s = site.s

    def tok(g):
        return at(g * GROUP, GROUP, GROUP)

    def each_group(body):
        lax.fori_loop(0, groups, lambda g, c: (body(g), c)[1], 0)

    def columns(base):
        return lambda q: inw_ref.at[:, at(base + q * w, w, LANES)]

    sm = Spread(site, b["SM"], 1, lambda q: small_ref)
    wv = Spread(site, b["WV"], rows, columns(INNER))
    ws = Spread(site, b["WS"], rows, lambda q: sh_ref.at[q])
    wg = Spread(site, b["WG"], rows, columns(0))
    wo = Spread(site, b["WO"], rows, lambda q: outt_ref.at[:, at(q * w, w, LANES)])
    mine = at(s * length, length, length)
    xg = GroupCopy(site, lambda q: x_ref, lambda k: b["XF"].at[mine], True)
    cg = GroupCopy(site, lambda q: cot_ref, lambda k: b["CF"].at[mine], True)
    stat = GroupCopy(site, lambda q: b["ST"], lambda k: b["EX"].at[k - 1], False)

    def slices(name):
        return lambda q: b[name].at[at(q * length, length, length)]

    outs = GroupCopy(site, slices("OP"), lambda k: b["OB"].at[k - 1], False)
    grads = GroupCopy(site, slices("NP"), lambda k: b["NB"].at[k - 1], False)
    fo, fg, fv, fs = (
        Fold(site, b["G" + n], rows, b["Y" + n], b["A" + n], b["Z" + n], b["T" + n], b["F" + n])
        for n in "OGVS"
    )
    fm = Fold(site, b["GM"], 1, b["YM"], b["AM"], b["ZM"], b["TM"], b["FM"])
    assert site.used == sems[0] and site.used_own == sems[1]

    site.greet()
    for item in (sm.members, wv.members, ws.members, xg):
        item.start()
    for item in (sm, wv, ws):
        item.begin()
    for item in (wg.members, wo.members, cg):
        item.start()
    head = lax.div(iota((LANES, w), 1), HEAD_DIM)
    b["EM"][...] = (iota((LANES, w), 0) == head).astype(f32).astype(bf16)
    for name in ("CACC", "NACC", "HACC", "PACC"):
        b[name][...] = jnp.zeros_like(b[name])
    b["CI"][pl.ds(0, 8), :] = jnp.zeros((8, cw), f32)
    b["DP"][pl.ds(tokens, 8), :] = jnp.zeros((8, cw), f32)
    xg.wait()

    def norm_scale(g):
        value = b["XF"][tok(g), :].astype(f32)
        inverse = lax.rsqrt(lanes_sum(value * value) / width + epsilon)
        b["INV"][tok(g), :] = jnp.broadcast_to(inverse, (GROUP, LANES))

    each_group(norm_scale)
    for k in range(1, nz):
        for item in (sm, wv, ws):
            item.forward(k)
    for item in (wg, wo):
        item.begin()
    sm.finish()

    lane = iota((1, width), 1)
    pre_table = lambda: Table(owners, lane, width // owners)
    norm_table = lambda: Table(owners, iota((1, w), 1) + s * w, INNER // owners)

    def conv_table():
        place = iota((1, cw), 1)
        channel = jnp.where(place < w, place + s * w, place - w + INNER)
        return Table(owners, channel, CONV_CH // owners)

    b["GA"][pl.ds(0, 1), :] = pre_table().row(b["SM"][:, 0, :])
    b["NG"][pl.ds(0, 1), :] = norm_table().row(b["SM"][:, 1, :])
    taps = conv_table()
    for k in range(CONV + 1):
        b["CW"][pl.ds(k, 1), :] = taps.row(b["SM"][:, 2 + k, :])

    def flip(source, target):
        def body(g):
            for c in range(0, width, LANES):
                part = b[source][tok(g), pl.ds(c, LANES)].astype(f32)
                b[target][pl.ds(c, LANES), tok(g)] = part.T.astype(bf16)

        each_group(body)

    def normalise(g):
        value = b["XF"][tok(g), :].astype(f32) * b["INV"][tok(g), pl.ds(0, 1)]
        b["XN"][tok(g), :] = (value * b["GA"][pl.ds(0, 1), :]).astype(bf16)

    each_group(normalise)
    flip("XN", "NT")
    wv.finish()
    ws.finish()

    def project(g):
        normed = b["XN"][tok(g), :]
        here = at(g * GROUP + 8, GROUP, 8)
        shared = dot(normed, b["WS"][...])
        b["CI"][here, pl.ds(0, w)] = dot(normed, b["WV"][...])
        b["CI"][here, pl.ds(w, MAPS)] = shared[:, :MAPS]
        b["DT"][tok(g), :] = shared[:, MAPS:]
        window = b["CI"][at(g * GROUP, GROUP + 8, 8), :]
        total = jnp.broadcast_to(b["CW"][pl.ds(CONV, 1), :], (GROUP, cw))
        for k in range(CONV):
            shift = 8 - (CONV - 1) + k
            total = total + b["CW"][pl.ds(k, 1), :] * window[shift : shift + GROUP]
        b["PRE"][tok(g), :] = total

    each_group(project)

    causal = iota((GROUP, GROUP), 0) >= iota((GROUP, GROUP), 1)
    low_half = iota((1, LANES), 1) < HEAD_DIM

    def expand(value):
        return exact(dot, value, b["EM"][...], 2)

    def per_head(value):
        return exact(dot_nt, value, b["EM"][...], 2)

    def halves(value):
        return jnp.concatenate(
            (jnp.where(low_half, value, 0.0), jnp.where(low_half, 0.0, value)), axis=0
        )

    def front(g):
        pre = b["PRE"][tok(g), :]
        out = pre * sigmoid(pre)
        bias, rate = heads_ref[pl.ds(0, 1), :], heads_ref[pl.ds(1, 1), :]
        raw = b["DT"][tok(g), :] + bias
        step = softplus(raw)
        lower = causal.astype(f32).astype(bf16)
        pieces = split(step * rate, 3)
        cumulative = dot(lower, pieces[2]) + dot(lower, pieces[1]) + dot(lower, pieces[0])
        return out[:, :w], out[:, w : w + STATE], out[:, w + STATE :], raw, step, cumulative

    def decays(cumulative, turned, j, backward):
        column = cumulative[:, j : j + 1]
        row = turned[j : j + 1, :]
        if backward:
            upper = iota((GROUP, GROUP), 0) <= iota((GROUP, GROUP), 1)
            return jnp.exp(jnp.where(upper, row - column, -10000.0))
        return jnp.exp(jnp.where(causal, column - row, -10000.0))

    b["RUN"][...] = jnp.zeros_like(b["RUN"])

    def ssd_forward(g):
        values, in_map, out_map, raw, step, cumulative = front(g)
        turned = cumulative.T
        last = cumulative[GROUP - 1 :, :]
        grown = jnp.exp(cumulative)
        grown_wide = expand(grown)
        carried = b["RUN"][...]
        b["CAR"][g] = carried
        scores = mm_nt(out_map, in_map)
        weighted = values * expand(step)
        skip = exact(dot, heads_ref[...], b["EM"][...], 3)[2:3, :]
        rest = mm(out_map, carried) * grown_wide + skip * values
        for p in range(pairs):
            part = slice(p * LANES, (p + 1) * LANES)
            mixing = jnp.concatenate(
                [scores * decays(cumulative, turned, 2 * p + i, False) for i in range(2)], axis=1
            )
            inner = mm(mixing, halves(weighted[:, part]))
            b["SSD"][tok(g), part] = inner + rest[:, part]
        ends = expand(jnp.exp(last - cumulative) * step)
        state = mm(in_map.T, values * ends)
        b["RUN"][...] = carried * grown_wide[GROUP - 1 :, :] + state

    def between(items, g):
        @pl.when(g < nz - 1)
        def _():
            for item in items:
                item.forward(g + 1)

    def later(items):
        for k in range(groups + 1, nz):
            for item in items:
                item.forward(k)

    def ssd_step(g):
        ssd_forward(g)
        between((wg, wo), g)

    each_group(ssd_step)
    later((wg, wo))
    cg.wait()
    wg.finish()
    wo.finish()

    norm_gain = lambda: b["NG"][pl.ds(0, 1), :]

    def gate(g):
        raw = dot(b["XN"][tok(g), :], b["WG"][...])
        gated = b["SSD"][tok(g), :] * (raw * sigmoid(raw))
        mixed_grad = dot(b["CF"][tok(g), :], b["WO"][...])
        b["GR"][tok(g), :] = raw
        b["GT"][tok(g), :] = gated
        b["MG"][tok(g), :] = mixed_grad
        squares = lanes_sum(gated * gated)
        cross = lanes_sum(mixed_grad * norm_gain() * gated)
        both = jnp.where(iota((GROUP, LANES), 1) < 4, squares, cross)
        b["ST"][:, tok(g)] = both.T[:8, :]

    each_group(gate)
    stat.start()
    flip("CF", "CT")
    stat.wait()

    def gate_back(g):
        sums = b["ST"][:, tok(g)]
        for k in range(seq - 1):
            sums = sums + b["EX"][k, :, tok(g)]
        sums = jnp.concatenate([sums] * (LANES // 8), axis=0).T
        squares, cross = sums[:, 0:1], sums[:, 4:5]
        inverse = lax.rsqrt(squares / INNER + epsilon)
        gated, mixed_grad, raw = b["GT"][tok(g), :], b["MG"][tok(g), :], b["GR"][tok(g), :]
        unit = gated * inverse
        b["MX"][tok(g), :] = (unit * norm_gain()).astype(bf16)
        b["NACC"][pl.ds(0, 1), :] += rows_sum(mixed_grad * unit)
        gated_grad = inverse * (mixed_grad * norm_gain() - unit * (inverse * cross / INNER))
        sig = sigmoid(raw)
        b["DY"][tok(g), :] = gated_grad * (raw * sig)
        slope = sig * (1.0 + raw * (1.0 - sig))
        b["PG"][tok(g), :] = (gated_grad * b["SSD"][tok(g), :] * slope).astype(bf16)

    each_group(gate_back)

    def weight_grad(fold, left, right):
        def block(rows_here):
            fold.grad[rows_here] = dot(b[left][rows_here], b[right][...]).astype(bf16)

        def away(i, carry):
            k = lax.rem(i + 1, nz)
            block(fold.other(k))
            fold.y_copy(k).start()
            return carry

        def home(i, carry):
            block(fold.mine(lax.rem(i + 1, nz)))
            return carry

        lax.fori_loop(0, nz, away, 0)
        lax.fori_loop(0, nz, home, 0)

    weight_grad(fo, "CT", "MX")
    weight_grad(fg, "NT", "PG")

    def out_product(g):
        b["OP"][tok(g), :] = dot_nt(b["MX"][tok(g), :], b["WO"][...]).astype(bf16)

    each_group(out_product)
    outs.start()

    b["RUN"][...] = jnp.zeros_like(b["RUN"])

    def ssd_backward(g):
        values, in_map, out_map, raw, step, cumulative = front(g)
        turned = cumulative.T
        last = cumulative[GROUP - 1 :, :]
        grown_wide = expand(jnp.exp(cumulative))
        step_wide = expand(step)
        weighted = values * step_wide
        skip = exact(dot, heads_ref[...], b["EM"][...], 3)[2:3, :]
        out_grad = b["DY"][tok(g), :]
        ssd = b["SSD"][tok(g), :]
        carried, after = b["CAR"][g], b["RUN"][...]
        rate = heads_ref[pl.ds(1, 1), :]

        b["NACC"][pl.ds(1, 1), :] += rows_sum(out_grad * values)
        cumul_grad = per_head(out_grad * (ssd - skip * values))
        grown_grad = out_grad * grown_wide
        ends = jnp.exp(last - cumulative)
        ends_wide = expand(ends * step)
        out_map_grad = mm_nt(grown_grad, carried)
        scaled_grad = mm(in_map, after)
        in_map_grad = mm_nt(values * ends_wide, after)
        ends_grad = per_head(scaled_grad * values)
        step_grad = ends_grad * ends
        ends_cumul = ends_grad * ends * step
        cumul_grad = cumul_grad - ends_cumul
        decay_sum = rows_sum(after * carried)
        decay_grad = per_head(jnp.broadcast_to(decay_sum, (8, w)))[0:1, :] * jnp.exp(last)
        last_grad = rows_sum(ends_cumul) + decay_grad
        b["RUN"][...] = mm(out_map.T, grown_grad) + after * grown_wide[GROUP - 1 :, :]
        scores_turned = mm_nt(in_map, out_map)
        scores_grad = jnp.zeros((GROUP, GROUP), f32)
        value_grads, step_parts = [], []
        for p in range(pairs):
            part = slice(p * LANES, (p + 1) * LANES)
            grads_here = halves(out_grad[:, part])
            mixing = jnp.concatenate(
                [scores_turned * decays(cumulative, turned, 2 * p + i, True) for i in range(2)],
                axis=1,
            )
            inner = mm(mixing, grads_here)
            step_parts.append(inner * values[:, part])
            value_grads.append(inner * step_wide[:, part])
            mixing_grad = mm_nt(grads_here, weighted[:, part])
            for i in range(2):
                scores_grad = scores_grad + (
                    decays(cumulative, turned, 2 * p + i, False)
                    * mixing_grad[i * GROUP : (i + 1) * GROUP]
                )
        inner_step = per_head(jnp.concatenate(step_parts, axis=1))
        step_grad = step_grad + inner_step
        cumul_grad = cumul_grad - inner_step * step
        values_grad = (
            jnp.concatenate(value_grads, axis=1) + scaled_grad * ends_wide + skip * out_grad
        )
        out_map_grad = out_map_grad + mm(scores_grad, in_map)
        in_map_grad = in_map_grad + mm(scores_grad.T, out_map)
        at_last = iota((GROUP, LANES), 0) == GROUP - 1
        cumul_grad = cumul_grad + jnp.where(at_last, last_grad, 0.0)
        upper = (iota((GROUP, GROUP), 0) <= iota((GROUP, GROUP), 1)).astype(f32).astype(bf16)
        pieces = split(cumul_grad, 3)
        rated_grad = dot(upper, pieces[2]) + dot(upper, pieces[1]) + dot(upper, pieces[0])
        step_grad = step_grad + rated_grad * rate
        b["HACC"][pl.ds(1, 1), :] += rows_sum(rated_grad * step * rate)
        raw_grad = step_grad * sigmoid(raw)
        b["HACC"][pl.ds(0, 1), :] += rows_sum(raw_grad)
        pre = b["PRE"][tok(g), :]
        sig = sigmoid(pre)
        conv_grad = jnp.concatenate((values_grad, in_map_grad, out_map_grad), axis=1)
        pre_grad = conv_grad * (sig * (1.0 + pre * (1.0 - sig)))
        b["DP"][tok(g), :] = pre_grad
        before = b["CI"][at(g * GROUP, GROUP + 8, 8), :]
        following = jnp.concatenate((pre_grad, b["DP"][at(g * GROUP + GROUP, 8, 8), :]), axis=0)
        total = None
        for k in range(CONV):
            shift = 8 - (CONV - 1) + k
            b["CACC"][pl.ds(k, 1), :] += rows_sum(pre_grad * before[shift : shift + GROUP])
            back = CONV - 1 - k
            term = b["CW"][pl.ds(k, 1), :] * following[back : back + GROUP]
            total = term if total is None else total + term
        b["CACC"][pl.ds(CONV, 1), :] += rows_sum(pre_grad)
        b["PV"][tok(g), :] = total[:, :w].astype(bf16)
        b["PS"][tok(g), :] = jnp.concatenate((total[:, w:], raw_grad), axis=1).astype(bf16)

    def ssd_back_step(g):
        ssd_backward(groups - 1 - g)
        between((fo, fg), g)

    each_group(ssd_back_step)
    later((fo, fg))

    weight_grad(fv, "NT", "PV")
    weight_grad(fs, "NT", "PS")

    def normed_grad(g):
        total = (
            dot_nt(b["PV"][tok(g), :], b["WV"][...])
            + dot_nt(b["PG"][tok(g), :], b["WG"][...])
            + dot_nt(b["PS"][tok(g), :], b["WS"][...])
        )
        b["NP"][tok(g), :] = total.astype(bf16)
        unit = b["XF"][tok(g), :].astype(f32) * b["INV"][tok(g), pl.ds(0, 1)]
        b["PACC"][pl.ds(0, 1), :] += rows_sum(total * unit)

    each_group(normed_grad)
    grads.start()
    b["GM"][:, 0, :] = pre_table().blocks(b["PACC"][pl.ds(0, 1), :])
    b["GM"][:, 1, :] = norm_table().blocks(b["NACC"][pl.ds(0, 1), :])
    taps = conv_table()
    for k in range(CONV + 1):
        b["GM"][:, 2 + k, :] = taps.blocks(b["CACC"][pl.ds(k, 1), :])
    skip_grad = per_head(jnp.broadcast_to(b["NACC"][pl.ds(1, 1), :], (8, w)))
    heads_here = w // HEAD_DIM
    total = jnp.zeros((8, LANES), f32)
    kinds = (b["HACC"][pl.ds(0, 1), :], b["HACC"][pl.ds(1, 1), :], skip_grad[0:1, :])
    for i, row in enumerate(kinds):
        place = iota((LANES, LANES), 1) - s * heads_here - i * HEADS
        source = iota((LANES, LANES), 0)
        move = ((place == source) & (source < heads_here)).astype(f32).astype(bf16)
        total = total + exact(dot, jnp.broadcast_to(row, (8, LANES)), move, 3)
    b["GM"][:, 7, :] = jnp.broadcast_to(total[0:1, :], (owners, LANES))
    for k in range(1, nz):
        fm.y_copy(k).start()
    fm.y_copy(0).start()

    for k in range(1, nz):
        for item in (fv, fs, fm):
            item.forward(k)
    fo.finish()
    fg.finish()
    outs.wait()
    total = x_ref[...].astype(f32) + b["OP"][mine, :].astype(f32)
    for k in range(seq - 1):
        total = total + b["OB"][k].astype(f32)
    block_ref[...] = total.astype(bf16)
    grads.wait()
    total = b["NP"][mine, :].astype(f32)
    for k in range(seq - 1):
        total = total + b["NB"][k].astype(f32)
    scaled = total * b["GA"][pl.ds(0, 1), :]
    inverse = b["INV"][mine, pl.ds(0, 1)]
    unit = x_ref[...].astype(f32) * inverse
    mean = lanes_sum(scaled * unit) / width
    ingrad_ref[...] = inverse * (scaled - unit * mean) + cot_ref[...].astype(f32)
    for item in (fv, fs, fm):
        item.finish()
    for item in (fo, fg, fv, fs, fm):
        item.members.wait()
    shared = None
    for q in range(seq):
        outshare_ref[:, pl.ds(q * w, w)] = b["FO"][q].astype(f32)
        inshare_ref[:, pl.ds(q * w, w)] = b["FG"][q].astype(f32)
        inshare_ref[:, pl.ds(INNER + q * w, w)] = b["FV"][q].astype(f32)
        part = b["FS"][q].astype(f32)
        maps = part[:, :MAPS]
        shared = maps if shared is None else shared + maps
        first = INNER + CONV_CH + q * heads_here
        inshare_ref[:, pl.ds(first, heads_here)] = part[:, MAPS : MAPS + heads_here]
        small = b["FM"][q]
        smalls = small if q == 0 else smalls + small
    inshare_ref[:, pl.ds(INNER + INNER, MAPS)] = shared
    smallout_ref[...] = smalls
    for drain in site.pending:
        drain()


def fused(x, cot, in_weight, shared, out_t, small, heads, dp, seq):
    length, width = x.shape
    rows, proj = in_weight.shape
    nz = dp // 2
    plan = scratch_plan(dp, seq, length, width, rows)
    names = tuple(plan)
    per_spread, per_fold = (seq - 1) + (nz - 1) + nz, nz + (nz - 1) + (seq - 1)
    sems = (5 * per_spread + 5 * (seq - 1) + 5 * per_fold, 7)
    vmem = pl.BlockSpec(memory_space=pltpu.VMEM)
    return pl.pallas_call(
        functools.partial(fused_kernel, dp, seq, names, sems),
        out_shape=[
            jax.ShapeDtypeStruct((length, width), bf16),
            jax.ShapeDtypeStruct((length, width), f32),
            jax.ShapeDtypeStruct((rows, proj), f32),
            jax.ShapeDtypeStruct((rows, INNER), f32),
            jax.ShapeDtypeStruct((1, 8, LANES), f32),
        ],
        in_specs=[vmem] * 7,
        out_specs=[vmem] * 5,
        scratch_shapes=[pltpu.VMEM(*plan[name]) for name in names]
        + [
            pltpu.SemaphoreType.DMA((sems[0],)),
            pltpu.SemaphoreType.DMA((sems[0],)),
            pltpu.SemaphoreType.DMA((sems[1],)),
        ],
        compiler_params=pltpu.CompilerParams(
            collective_id=0, has_side_effects=True, vmem_limit_bytes=58 * 2**20
        ),
    )(x, cot, in_weight, shared, out_t, small, heads)


def fits(dp, seq, block_input, in_weight):
    seq_dev, length, width = block_input.shape
    rows = in_weight.shape[0]
    owners = dp * seq
    return (
        seq_dev == 1
        and dp % 2 == 0
        and dp >= 4
        and seq > 1
        and length % GROUP == 0
        and rows % 16 == 0
        and INNER % (seq * LANES) == 0
        and INNER % owners == 0
        and CONV_CH % owners == 0
        and CONV_CH // owners <= LANES
        and dp // 2 <= seq * length // GROUP + 1
    )


def lane_row(value):
    value = value.reshape(1, -1).astype(f32)
    return jnp.pad(value, ((0, 0), (0, LANES - value.shape[1])))


def on_device_fused(
    block_input,
    in_weight,
    out_weight,
    pre_gain,
    norm_gain,
    conv_weight,
    conv_bias,
    dt_bias,
    decay_log,
    skip_gain,
    cotangent,
):
    dp, seq = lax.axis_size("dp"), lax.axis_size("seq")
    here = HEADS // seq
    rows = in_weight.shape[0]
    maps, steps = in_weight[:, INNER + INNER : INNER + CONV_CH], in_weight[:, INNER + CONV_CH :]
    filler = jnp.zeros((rows, LANES - here), in_weight.dtype)
    shared = jnp.stack(
        [
            jnp.concatenate((maps, steps[:, q * here : (q + 1) * here], filler), axis=1)
            for q in range(seq)
        ]
    )
    small = jnp.concatenate(
        [lane_row(pre_gain), lane_row(norm_gain)]
        + [lane_row(conv_weight[k]) for k in range(CONV)]
        + [lane_row(conv_bias), jnp.zeros((1, LANES), f32)]
    )[None]
    own = jnp.stack((dt_bias, -jnp.exp(decay_log), skip_gain))
    own = lax.dynamic_slice_in_dim(own, lax.axis_index("seq") * here, here, axis=1)
    own = jnp.pad(own, ((0, 5), (0, LANES - here)))
    block, in_grad, in_share, out_share, smalls = fused(
        block_input[0],
        cotangent[0],
        in_weight,
        shared,
        out_weight.T,
        small,
        own,
        dp,
        seq,
    )
    smalls = smalls[0]
    return (
        block[None],
        in_grad[None],
        in_share,
        out_share.T,
        smalls[0, : pre_gain.size],
        smalls[1, : norm_gain.size],
        smalls[2 : 2 + CONV, : conv_bias.size],
        smalls[2 + CONV, : conv_bias.size],
        smalls[7, :HEADS],
        smalls[7, HEADS : 2 * HEADS],
        smalls[7, 2 * HEADS : 3 * HEADS],
    )


def from_behind(value, axis, steps):
    count = lax.axis_size(axis)
    leading, last = (max(0, -steps), min(count, count - steps))
    return lax.ppermute(value, axis, [(source, source + steps) for source in range(leading, last)])


def convolve(padded, conv_weight, conv_bias):
    taps = conv_weight.shape[0]
    length = padded.shape[-2] - taps + 1
    total = conv_bias
    for index in range(taps):
        total = total + conv_weight[index] * lax.slice_in_dim(
            padded, index, index + length, axis=padded.ndim - 2
        )
    return total


def running_sum(value):
    length = value.shape[1]
    lower = (jnp.arange(length)[:, None] >= jnp.arange(length)[None, :]).astype(value.dtype)
    return jnp.einsum("ts,bsh->bth", lower, value, precision=lax.Precision.HIGHEST)


def carry_scan(state, decay, axis, sign):
    count = lax.axis_size(axis)
    within, within_decay = state, decay
    entering, entering_decay = None, None
    width = 1
    while width < count:
        moved = from_behind(within.astype(jnp.bfloat16), axis, sign * width).astype(jnp.float32)
        last = 2 * width >= count
        if not last or entering is None:
            moved_decay = from_behind(within_decay, axis, sign * width)
        if entering is None:
            entering, entering_decay = moved, moved_decay
        else:
            entering = entering + entering_decay[:, :, None, None] * moved
            if not last:
                entering_decay = entering_decay * moved_decay
        if not last:
            within = within + within_decay[:, :, None, None] * moved
            within_decay = within_decay * moved_decay
        width *= 2
    return jnp.zeros_like(state) if entering is None else entering


def front_fn(tail, rim, conv_weight, conv_bias, dt_bias, decay_log):
    conv_in = tail[..., :CONV_CH]
    dt_raw = tail[..., CONV_CH:]
    padded = jnp.concatenate([rim, conv_in], axis=-2)
    conv_out = jax.nn.silu(convolve(padded, conv_weight, conv_bias))
    leading = conv_out.shape[:-1]
    values = conv_out[..., :INNER].reshape(leading + (HEADS, HEAD_DIM))
    in_map = conv_out[..., INNER : INNER + STATE]
    out_map = conv_out[..., INNER + STATE :]
    step = jax.nn.softplus(dt_raw + dt_bias)
    cumulative = running_sum(step * -jnp.exp(decay_log))
    return (values, in_map, out_map, step, cumulative)


def group_state(values, in_map, step, cumulative):
    weights_end = jnp.exp(cumulative[-1][None, :] - cumulative) * step
    state = jnp.einsum("shp,sn->hpn", values * weights_end[:, :, None], in_map, precision=highest)
    return (state, jnp.exp(cumulative[-1]))


def group_output(values, in_map, out_map, step, cumulative, carried, skip_gain):
    length = values.shape[0]
    scores = jnp.dot(out_map, in_map.T, precision=highest)
    causal = jnp.arange(length)[:, None] >= jnp.arange(length)[None, :]
    spread = cumulative[:, None, :] - cumulative[None, :, :]
    decay = jnp.exp(jnp.where(causal[:, :, None], spread, -10000.0))
    mixing = scores[:, :, None] * decay * step[None, :, :]
    inner_part = jnp.einsum("tsh,shp->thp", mixing, values, precision=highest)
    carried_part = (
        jnp.einsum("tn,hpn->thp", out_map, carried, precision=highest)
        * jnp.exp(cumulative)[:, :, None]
    )
    return inner_part + carried_part + skip_gain[None, :, None] * values


def state_fn(values, in_map, step, cumulative):
    return jax.vmap(group_state)(values, in_map, step, cumulative)


def out_fn(values, in_map, out_map, step, cumulative, gate_raw, carried, skip_gain, norm_gain):
    ssd_out = jax.vmap(group_output, in_axes=(0, 0, 0, 0, 0, 0, None))(
        values, in_map, out_map, step, cumulative, carried, skip_gain
    )
    ssd_out = ssd_out.reshape(gate_raw.shape)
    gated = ssd_out * jax.nn.silu(gate_raw)
    inverse = lax.rsqrt(jnp.mean(gated * gated, axis=-1, keepdims=True) + epsilon)
    return gated * inverse * norm_gain


def by_rows(grad, owners):
    return grad.reshape(owners, -1)


def by_columns(grad, owners):
    rows = grad.shape[0]
    return jnp.transpose(grad.reshape(rows, owners, -1), (1, 0, 2)).reshape(owners, -1)


def on_device(
    block_input,
    in_weight,
    out_weight,
    pre_gain,
    norm_gain,
    conv_weight,
    conv_bias,
    dt_bias,
    decay_log,
    skip_gain,
    cotangent,
):
    seq_dev, length, width = block_input.shape
    dp, seq = lax.axis_size("dp"), lax.axis_size("seq")
    owners = dp * seq
    both = ("dp", "seq")
    if fits(dp, seq, block_input, in_weight):
        return on_device_fused(
            block_input,
            in_weight,
            out_weight,
            pre_gain,
            norm_gain,
            conv_weight,
            conv_bias,
            dt_bias,
            decay_log,
            skip_gain,
            cotangent,
        )
    small_parts = (pre_gain, norm_gain, conv_weight.reshape(-1), conv_bias)
    small_sizes = [part.size for part in small_parts]
    small = jnp.concatenate(small_parts)
    in_full = lax.all_gather(in_weight, both, axis=0, tiled=True)
    gate_w, tail_w = in_full[:, :INNER], in_full[:, INNER:]
    out_t = lax.all_gather(out_weight.T, both, axis=0, tiled=True)
    small_all = lax.all_gather(small, both, axis=0)
    pieces, start = [], 0
    for size in small_sizes:
        pieces.append(small_all[:, start : start + size])
        start += size
    pre_full, norm_full, conv_b_full = (pieces[i].reshape(-1) for i in (0, 1, 3))
    conv_w_full = jnp.transpose(pieces[2].reshape(owners, CONV, -1), (1, 0, 2)).reshape(CONV, -1)
    pre_float = pre_full.astype(jnp.float32)
    norm_float = norm_full.astype(jnp.float32)
    inputs = block_input.astype(jnp.float32)
    inv_pre = lax.rsqrt(jnp.mean(inputs * inputs, axis=-1, keepdims=True) + epsilon)
    normed = (inputs * inv_pre * pre_float).astype(jnp.bfloat16)
    flat_normed = normed.reshape(seq_dev * length, width)
    gate_raw = jnp.dot(flat_normed, gate_w, preferred_element_type=jnp.float32).reshape(
        seq_dev, length, -1
    )
    tail = jnp.dot(flat_normed, tail_w, preferred_element_type=jnp.float32).reshape(
        seq_dev, length, -1
    )
    conv_in = tail[:, length - (CONV - 1) :, :CONV_CH]
    rim = from_behind(conv_in, "seq", 1)
    front_out, front_pull = jax.vjp(
        front_fn,
        tail,
        rim,
        conv_w_full.astype(jnp.float32),
        conv_b_full.astype(jnp.float32),
        dt_bias,
        decay_log,
    )
    values, in_map, out_map, step, cumulative = front_out
    state_out, state_pull = jax.vjp(state_fn, values, in_map, step, cumulative)
    state, decay = state_out
    carried = carry_scan(state, decay, "seq", 1)
    mixed_float, out_pull = jax.vjp(
        out_fn, values, in_map, out_map, step, cumulative, gate_raw, carried, skip_gain, norm_float
    )
    mixed = mixed_float.astype(jnp.bfloat16)
    flat_mixed = mixed.reshape(seq_dev * length, INNER)
    block_output = (
        inputs
        + jnp.dot(flat_mixed, out_t.T, preferred_element_type=jnp.float32).reshape(
            seq_dev, length, width
        )
    ).astype(jnp.bfloat16)
    flat_grad = cotangent.reshape(seq_dev * length, width)
    mixed_grad = jnp.dot(flat_grad, out_t, preferred_element_type=jnp.float32).reshape(
        seq_dev, length, INNER
    )
    out_w_grad = jnp.dot(flat_grad.T, flat_mixed, preferred_element_type=jnp.float32)
    (
        values_a,
        in_map_a,
        out_map_grad,
        step_a,
        cumul_a,
        gate_grad,
        local_grad,
        skip_grad,
        norm_grad,
    ) = out_pull(mixed_grad)

    later_grad = carry_scan(local_grad, decay, "seq", -1)
    decay_grad = jnp.sum(later_grad * carried, axis=(2, 3))
    values_b, in_map_b, step_b, cumul_b = state_pull((later_grad, decay_grad))
    front_grads = front_pull(
        (
            values_a + values_b,
            in_map_a + in_map_b,
            out_map_grad,
            step_a + step_b,
            cumul_a + cumul_b,
        )
    )
    tail_float, rim_grad, conv_w_grad, conv_b_grad, dt_grad, decay_log_grad = front_grads
    returned = from_behind(rim_grad, "seq", -1)
    tail_float = tail_float + jnp.pad(returned, ((0, 0), (length - (CONV - 1), 0), (0, HEADS)))
    tail_grad = tail_float.astype(jnp.bfloat16).reshape(seq_dev * length, -1)
    gate_grad = gate_grad.astype(jnp.bfloat16).reshape(seq_dev * length, -1)
    gate_w_grad = jnp.dot(flat_normed.T, gate_grad, preferred_element_type=jnp.float32)
    tail_w_grad = jnp.dot(flat_normed.T, tail_grad, preferred_element_type=jnp.float32)
    normed_grad = (
        jnp.dot(gate_grad, gate_w.T, preferred_element_type=jnp.float32)
        + jnp.dot(tail_grad, tail_w.T, preferred_element_type=jnp.float32)
    ).reshape(seq_dev, length, width)
    pre_grad = jnp.sum(normed_grad * inputs * inv_pre, axis=(0, 1))
    scaled = normed_grad * pre_float
    unit = inputs * inv_pre
    input_grad = inv_pre * (
        scaled - unit * jnp.mean(scaled * unit, axis=-1, keepdims=True)
    ) + cotangent.astype(jnp.float32)
    small_grads = jnp.concatenate(
        (
            by_rows(pre_grad, owners),
            by_rows(norm_grad, owners),
            by_columns(conv_w_grad, owners),
            by_rows(conv_b_grad, owners),
        ),
        axis=1,
    )
    heads = jnp.concatenate((dt_grad, decay_log_grad, skip_grad))
    scatter = functools.partial(
        lax.psum_scatter, axis_name=both, scatter_dimension=0, tiled=True
    )
    in_share = scatter(jnp.concatenate((gate_w_grad, tail_w_grad), axis=1))
    out_share = scatter(out_w_grad).T
    small_share = scatter(small_grads)[0]
    heads = lax.psum(heads, both)
    shares, start = [], 0
    for size in small_sizes:
        shares.append(small_share[start : start + size])
        start += size
    pre_share, norm_share, conv_w_share, conv_b_share = shares
    conv_w_share = conv_w_share.reshape(CONV, -1)
    heads_total = (heads[:HEADS], heads[HEADS : 2 * HEADS], heads[2 * HEADS :])
    return (
        block_output,
        input_grad,
        in_share,
        out_share,
        pre_share,
        norm_share,
        conv_w_share,
        conv_b_share,
        heads_total[0],
        heads_total[1],
        heads_total[2],
    )


def solution(mesh):
    in_specs = (
        P("dp", "seq", None),
        P(("dp", "seq"), None),
        P(None, ("dp", "seq")),
        P(("dp", "seq")),
        P(("dp", "seq")),
        P(None, ("dp", "seq")),
        P(("dp", "seq")),
        P(),
        P(),
        P(),
        P("dp", "seq", None),
    )
    out_specs = (
        P("dp", "seq", None),
        P("dp", "seq", None),
        P(("dp", "seq"), None),
        P(None, ("dp", "seq")),
        P(("dp", "seq")),
        P(("dp", "seq")),
        P(None, ("dp", "seq")),
        P(("dp", "seq")),
        P(),
        P(),
        P(),
    )
    return jax.shard_map(
        on_device, mesh=mesh, in_specs=in_specs, out_specs=out_specs, check_vma=False
    )
```

```python
import functools

import jax
import jax.numpy as jnp
from jax import lax
from jax.experimental import pallas as pl
from jax.experimental.pallas import tpu as pltpu
from jax.sharding import PartitionSpec as P

HEADS = 32
HEAD_DIM = 64
STATE = 128
CONV = 4
GROUP = 128
INNER = 2048
CONV_CH = 2304
LANES = 128
MAPS = CONV_CH - INNER
SHARED = MAPS + LANES


epsilon = 1e-05
highest = lax.Precision.HIGH
bf16 = jnp.bfloat16
f32 = jnp.float32


def at(start, size, multiple):
    return pl.ds(start if isinstance(start, int) else pl.multiple_of(start, multiple), size)


def remote(src, dst, send, recv, device):
    return pltpu.make_async_remote_copy(
        src_ref=src,
        dst_ref=dst,
        send_sem=send,
        recv_sem=recv,
        device_id=device,
        device_id_type=pl.DeviceIdType.MESH,
    )


class Site:
    def __init__(self, dp, seq, send, recv, own):
        self.nz, self.ns = dp // 2, seq
        self.d, self.s = lax.axis_index("dp"), lax.axis_index("seq")
        far, level = lax.rem(self.d, 2), self.d // 2
        self.dp, self.half = dp, dp // 2
        self.place = level + far * (dp - 1 - 2 * level)
        self.owner = self.d * seq + self.s
        self.send, self.recv, self.own = send, recv, own
        self.used, self.used_own = 0, 0
        self.pending = []

    def group(self, k):
        return (self.d, lax.rem(self.s + k, self.ns))

    def ring(self, offset):
        place = lax.rem(self.place + offset + 2 * self.dp, self.dp)
        far = place // self.nz
        level = place + far * (self.dp - 1 - 2 * place)
        return level * 2 + far

    def beside(self, way):
        return (self.ring(way), self.s)

    def take(self, count):
        self.used += count
        return self.used - count

    def copy(self, src, dst, slot, device):
        return remote(src, dst, self.send.at[slot], self.recv.at[slot], device)

    def greet(self):
        barrier = pltpu.get_barrier_semaphore()
        partners = [self.group(k) for k in range(1, self.ns)]
        partners += [self.beside(1), self.beside(-1)]
        for partner in partners:
            pl.semaphore_signal(
                barrier, inc=1, device_id=partner, device_id_type=pl.DeviceIdType.MESH
            )
        pl.semaphore_wait(barrier, len(partners))


class GroupCopy:
    def __init__(self, site, source, dest, local):
        self.site, self.source, self.dest, self.local = site, source, dest, local
        self.base = site.take(site.ns - 1)
        if local:
            self.own = site.used_own
            site.used_own += 1
        site.pending.append(self.drain)

    def own_copy(self):
        site = self.site
        return pltpu.make_async_copy(self.source(site.s), self.dest(0), site.own.at[self.own])

    def copy(self, k):
        site = self.site
        member = lax.rem(site.s + k, site.ns)
        return site.copy(self.source(member), self.dest(k), self.base + k - 1, site.group(k))

    def start(self):
        for k in range(1, self.site.ns):
            self.copy(k).start()
        if self.local:
            self.own_copy().start()

    def wait(self):
        if self.local:
            self.own_copy().wait()
        for k in range(1, self.site.ns):
            self.copy(k).wait_recv()

    def drain(self):
        for k in range(1, self.site.ns):
            self.copy(k).wait_send()


class Spread:
    def __init__(self, site, buf, rows, source):
        self.site, self.buf, self.rows, self.source = site, buf, rows, source
        self.block_rows = site.ns * rows
        self.members = GroupCopy(
            site, source, lambda k: buf.at[at(site.owner * rows, rows, rows)], True
        )
        self.base = {way: site.take(site.half) for way in (1, -1)}
        site.pending.append(self.drain)

    def copy(self, way, hop):
        site, size = self.site, self.block_rows
        start = site.ring(way * (1 - hop)) * size
        if hop == site.half:
            size = size // 2
            start = start if way > 0 else start + size
        block = self.buf.at[at(start, size, size)]
        return site.copy(block, block, self.base[way] + hop - 1, site.beside(way))

    def begin(self):
        self.members.wait()
        for way in (1, -1):
            self.copy(way, 1).start()

    def forward(self, hop):
        for way in (1, -1):
            self.copy(way, hop).wait_recv()
            self.copy(way, hop + 1).start()

    def finish(self):
        for way in (1, -1):
            self.copy(way, self.site.half).wait_recv()

    def drain(self):
        for way in (1, -1):
            for hop in range(1, self.site.half + 1):
                self.copy(way, hop).wait_send()


class Fold:
    def __init__(self, site, grad, rows, boxes, sums, total, final):
        self.site, self.grad, self.rows = site, grad, rows
        self.block_rows = site.ns * rows
        self.boxes, self.sums = dict(zip((1, -1), boxes)), dict(zip((1, -1), sums))
        self.total, self.final = total, final
        self.base = {way: site.take(site.half) for way in (1, -1)}
        self.members = GroupCopy(
            site,
            lambda q: total.at[at(q * rows, rows, rows)],
            lambda k: final.at[site.s],
            False,
        )
        site.pending.append(self.drain)

    def block(self, offset):
        return at(self.site.ring(offset) * self.block_rows, self.block_rows, self.block_rows)

    def copy(self, way, hop):
        site, size = self.site, self.block_rows // 2
        if hop == 1:
            shift = 0 if way > 0 else size
            source = self.grad.at[at(site.ring(way * site.half) * 2 * size + shift, size, size)]
            dest = self.boxes[way].at[0, pl.ds(shift, size)]
        else:
            source, dest = self.sums[way].at[hop - 2], self.boxes[way].at[hop - 1]
        return site.copy(source, dest, self.base[way] + hop - 1, site.beside(way))

    def begin(self):
        for way in (1, -1):
            self.copy(way, 1).start()

    def forward(self, hop):
        site, size = self.site, self.block_rows // 2
        for way in (1, -1):
            self.copy(way, hop).wait_recv()
            kept = self.grad[self.block(way * (site.half - hop))]
            box, sums = self.boxes[way], self.sums[way]
            if hop == 1:
                near, far = (slice(0, size), slice(size, None))[::way]
                both = kept[near].astype(f32) + box[0, near].astype(f32)
                sums[0, near] = both.astype(sums.dtype)
                sums[0, far] = kept[far]
            else:
                both = kept.astype(f32) + box[hop - 1].astype(f32)
                sums[hop - 1] = both.astype(sums.dtype)
            self.copy(way, hop + 1).start()

    def finish(self):
        site = self.site
        total = self.grad[self.block(0)].astype(f32)
        for way in (1, -1):
            self.copy(way, site.half).wait_recv()
            total = total + self.boxes[way][site.half - 1].astype(f32)
        self.total[...] = total.astype(self.total.dtype)
        self.members.start()
        self.final[site.s] = self.total[at(site.s * self.rows, self.rows, self.rows)]

    def drain(self):
        for way in (1, -1):
            for hop in range(1, self.site.half + 1):
                self.copy(way, hop).wait_send()


def dot(a, b):
    return jnp.dot(a, b, preferred_element_type=f32)


def dot_nt(a, b):
    return lax.dot_general(a, b, (((1,), (1,)), ((), ())), preferred_element_type=f32)


def split(value, parts):
    pieces = []
    for _ in range(parts - 1):
        pieces.append(value.astype(bf16))
        value = value - pieces[-1].astype(f32)
    return pieces + [value.astype(bf16)]


def exact(product, value, onehot, parts):
    total = None
    for piece in split(value, parts)[::-1]:
        term = product(piece, onehot)
        total = term if total is None else total + term
    return total


def wide(product, a, b, passes):
    if passes == 1:
        return product(a.astype(bf16), b.astype(bf16))
    (a_hi, a_lo), (b_hi, b_lo) = split(a, 2), split(b, 2)
    total = product(a_hi, b_lo)
    if passes == 3:
        total = total + product(a_lo, b_hi)
    return total + product(a_hi, b_hi)


def mm(a, b, passes=3):
    return wide(dot, a, b, passes)


def mm_nt(a, b, passes=3):
    return wide(dot_nt, a, b, passes)


def iota(shape, axis):
    return lax.broadcasted_iota(jnp.int32, shape, axis)


def sigmoid(value):
    return 1.0 / (1.0 + jnp.exp(-value))


def softplus(value):
    small = jnp.exp(-jnp.abs(value))
    series = small * (1.0 - small * (0.5 - small * (1 / 3 - small * (0.25 - small * 0.2))))
    return jnp.maximum(value, 0.0) + jnp.where(small < 0.03, series, jnp.log(1.0 + small))


def rows_sum(value):
    return jnp.sum(value, axis=0, keepdims=True)


def lanes_sum(value):
    return jnp.sum(value, axis=1, keepdims=True)


class Table:
    def __init__(self, owners, channel, size):
        count = channel.shape[1]
        first = iota((owners, count), 0) * size
        place = channel - first
        self.mask = (place >= 0) & (place < size)
        spot = jnp.sum(jnp.where(self.mask, place.astype(f32), 0.0), axis=0, keepdims=True)
        self.onehot = (iota((LANES, count), 0).astype(f32) == spot).astype(f32).astype(bf16)

    def row(self, blocks):
        return rows_sum(jnp.where(self.mask, dot(blocks.astype(bf16), self.onehot), 0.0))

    def blocks(self, row):
        return exact(dot_nt, jnp.where(self.mask, row, 0.0), self.onehot, 3)


def scratch_plan(dp, seq, length, width, rows):
    nz, owners, tokens = dp // 2, dp * seq, seq * length
    w = INNER // seq
    cw, groups, block = w + MAPS, tokens // GROUP, seq * rows
    plan = dict(
        XF=((tokens, width), bf16),
        CF=((tokens, width), bf16),
        WV=((width, w), bf16),
        WS=((width, SHARED), bf16),
        WG=((width, w), bf16),
        WO=((width, w), bf16),
        SM=((owners, 8, LANES), f32),
        XN=((tokens, width), bf16),
        NT=((width, tokens), bf16),
        CT=((width, tokens), bf16),
        INV=((tokens, LANES), f32),
        GA=((8, width), f32),
        NG=((8, w), f32),
        CW=((8, cw), f32),
        EM=((LANES, w), bf16),
        CI=((8 + tokens, cw), f32),
        PRE=((tokens, cw), f32),
        DT=((tokens, LANES), f32),
        CAR=((groups, STATE, w), f32),
        RUN=((STATE, w), f32),
        SSD=((tokens, w), f32),
        GR=((tokens, w), f32),
        GT=((tokens, w), f32),
        MG=((tokens, w), f32),
        ST=((8, tokens), f32),
        EX=((seq - 1, 8, tokens), f32),
        MX=((tokens, w), bf16),
        PG=((tokens, w), bf16),
        DY=((tokens, w), f32),
        PV=((tokens, w), bf16),
        PS=((tokens, SHARED), bf16),
        DP=((tokens + 8, cw), f32),
        OP=((tokens, width), bf16),
        OB=((seq - 1, length, width), bf16),
        NP=((tokens, width), bf16),
        NB=((seq - 1, length, width), bf16),
        CACC=((8, cw), f32),
        NACC=((8, w), f32),
        HACC=((8, LANES), f32),
        PACC=((8, width), f32),
    )
    for name, columns in (("O", w), ("G", w), ("V", w), ("S", SHARED)):
        plan["G" + name] = ((width, columns), bf16)
        for way in "RL":
            plan["Y" + way + name] = ((nz, block, columns), bf16)
            plan["A" + way + name] = ((nz - 1, block, columns), bf16)
        plan["T" + name] = ((block, columns), bf16)
        plan["F" + name] = ((seq, rows, columns), bf16)
    tile = (8, LANES)
    plan["GM"] = ((owners,) + tile, f32)
    for way in "RL":
        plan["Y" + way + "M"] = ((nz, seq) + tile, f32)
        plan["A" + way + "M"] = ((nz - 1, seq) + tile, f32)
    plan["TM"] = ((seq,) + tile, f32)
    plan["FM"] = ((seq, 1) + tile, f32)
    return plan


def fused_kernel(dp, seq, names, sems, *refs):
    x_ref, cot_ref, inw_ref, sh_ref, outt_ref, small_ref, heads_ref = refs[:7]
    block_ref, ingrad_ref, inshare_ref, outshare_ref, smallout_ref = refs[7:12]
    b = dict(zip(names, refs[12 : 12 + len(names)]))
    send, recv, own = refs[12 + len(names) :]
    site = Site(dp, seq, send, recv, own)
    nz, owners = dp // 2, dp * seq
    length, width = x_ref.shape
    rows = inw_ref.shape[0]
    tokens = seq * length
    groups = tokens // GROUP
    w = INNER // seq
    cw = w + MAPS
    pairs = w // LANES
    block_rows = seq * rows
    s = site.s

    def tok(g):
        return at(g * GROUP, GROUP, GROUP)

    def each_group(body):
        lax.fori_loop(0, groups, lambda g, c: (body(g), c)[1], 0)

    def columns(base):
        return lambda q: inw_ref.at[:, at(base + q * w, w, LANES)]

    sm = Spread(site, b["SM"], 1, lambda q: small_ref)
    wv = Spread(site, b["WV"], rows, columns(INNER))
    ws = Spread(site, b["WS"], rows, lambda q: sh_ref.at[q])
    wg = Spread(site, b["WG"], rows, columns(0))
    wo = Spread(site, b["WO"], rows, lambda q: outt_ref.at[:, at(q * w, w, LANES)])
    mine = at(s * length, length, length)
    xg = GroupCopy(site, lambda q: x_ref, lambda k: b["XF"].at[mine], True)
    cg = GroupCopy(site, lambda q: cot_ref, lambda k: b["CF"].at[mine], True)
    stat = GroupCopy(site, lambda q: b["ST"], lambda k: b["EX"].at[k - 1], False)

    def slices(name):
        return lambda q: b[name].at[at(q * length, length, length)]

    outs = GroupCopy(site, slices("OP"), lambda k: b["OB"].at[k - 1], False)
    grads = GroupCopy(site, slices("NP"), lambda k: b["NB"].at[k - 1], False)
    fo, fg, fv, fs, fm = (
        Fold(
            site,
            b["G" + n],
            1 if n == "M" else rows,
            (b["YR" + n], b["YL" + n]),
            (b["AR" + n], b["AL" + n]),
            b["T" + n],
            b["F" + n],
        )
        for n in "OGVSM"
    )
    assert site.used == sems[0] and site.used_own == sems[1]

    site.greet()
    for item in (sm.members, wv.members, ws.members):
        item.start()
    for item in (sm, wv, ws):
        item.begin()
    for item in (xg, wg.members, wo.members):
        item.start()
    head = lax.div(iota((LANES, w), 1), HEAD_DIM)
    b["EM"][...] = (iota((LANES, w), 0) == head).astype(f32).astype(bf16)
    for name in ("CACC", "NACC", "HACC", "PACC"):
        b[name][...] = jnp.zeros_like(b[name])
    b["CI"][pl.ds(0, 8), :] = jnp.zeros((8, cw), f32)
    b["DP"][pl.ds(tokens, 8), :] = jnp.zeros((8, cw), f32)

    def norm_scale(g):
        value = b["XF"][tok(g), :].astype(f32)
        inverse = lax.rsqrt(lanes_sum(value * value) / width + epsilon)
        b["INV"][tok(g), :] = jnp.broadcast_to(inverse, (GROUP, LANES))

    def forward(items, hop):
        for item in items:
            item.forward(hop)

    forward((sm, wv, ws), 1)
    wg.begin()
    for hop in range(2, nz):
        forward((sm, wv, ws), hop)
    wo.begin()
    xg.wait()
    cg.start()
    each_group(norm_scale)
    sm.finish()

    lane = iota((1, width), 1)
    pre_table = lambda: Table(owners, lane, width // owners)
    norm_table = lambda: Table(owners, iota((1, w), 1) + s * w, INNER // owners)

    def conv_table():
        place = iota((1, cw), 1)
        channel = jnp.where(place < w, place + s * w, place - w + INNER)
        return Table(owners, channel, CONV_CH // owners)

    b["GA"][pl.ds(0, 1), :] = pre_table().row(b["SM"][:, 0, :])
    b["NG"][pl.ds(0, 1), :] = norm_table().row(b["SM"][:, 1, :])
    taps = conv_table()
    for k in range(CONV + 1):
        b["CW"][pl.ds(k, 1), :] = taps.row(b["SM"][:, 2 + k, :])

    def flip(source, target):
        def body(g):
            for c in range(0, width, LANES):
                part = b[source][tok(g), pl.ds(c, LANES)].astype(f32)
                b[target][pl.ds(c, LANES), tok(g)] = part.T.astype(bf16)

        each_group(body)

    def normalise(g):
        value = b["XF"][tok(g), :].astype(f32) * b["INV"][tok(g), pl.ds(0, 1)]
        b["XN"][tok(g), :] = (value * b["GA"][pl.ds(0, 1), :]).astype(bf16)

    each_group(normalise)
    flip("XN", "NT")
    wv.finish()
    ws.finish()

    def project(g):
        normed = b["XN"][tok(g), :]
        here = at(g * GROUP + 8, GROUP, 8)
        shared = dot(normed, b["WS"][...])
        b["CI"][here, pl.ds(0, w)] = dot(normed, b["WV"][...])
        b["CI"][here, pl.ds(w, MAPS)] = shared[:, :MAPS]
        b["DT"][tok(g), :] = shared[:, MAPS:]
        window = b["CI"][at(g * GROUP, GROUP + 8, 8), :]
        total = jnp.broadcast_to(b["CW"][pl.ds(CONV, 1), :], (GROUP, cw))
        for k in range(CONV):
            shift = 8 - (CONV - 1) + k
            total = total + b["CW"][pl.ds(k, 1), :] * window[shift : shift + GROUP]
        b["PRE"][tok(g), :] = total

    each_group(project)

    causal = iota((GROUP, GROUP), 0) >= iota((GROUP, GROUP), 1)
    low_half = iota((1, LANES), 1) < HEAD_DIM

    def expand(value):
        return exact(dot, value, b["EM"][...], 2)

    def per_head(value):
        return exact(dot_nt, value, b["EM"][...], 2)

    def halves(value):
        return jnp.concatenate(
            (jnp.where(low_half, value, 0.0), jnp.where(low_half, 0.0, value)), axis=0
        )

    def front(g):
        pre = b["PRE"][tok(g), :]
        out = pre * sigmoid(pre)
        bias, rate = heads_ref[pl.ds(0, 1), :], heads_ref[pl.ds(1, 1), :]
        raw = b["DT"][tok(g), :] + bias
        step = softplus(raw)
        lower = causal.astype(f32).astype(bf16)
        pieces = split(step * rate, 3)
        cumulative = dot(lower, pieces[2]) + dot(lower, pieces[1]) + dot(lower, pieces[0])
        return out[:, :w], out[:, w : w + STATE], out[:, w + STATE :], raw, step, cumulative

    def decays(cumulative, turned, j, backward):
        column = cumulative[:, j : j + 1]
        row = turned[j : j + 1, :]
        if backward:
            upper = iota((GROUP, GROUP), 0) <= iota((GROUP, GROUP), 1)
            return jnp.exp(jnp.where(upper, row - column, -10000.0))
        return jnp.exp(jnp.where(causal, column - row, -10000.0))

    b["RUN"][...] = jnp.zeros_like(b["RUN"])

    def ssd_forward(g):
        values, in_map, out_map, raw, step, cumulative = front(g)
        turned = cumulative.T
        last = cumulative[GROUP - 1 :, :]
        grown = jnp.exp(cumulative)
        grown_wide = expand(grown)
        carried = b["RUN"][...]
        b["CAR"][g] = carried
        scores = mm_nt(out_map, in_map)
        weighted = values * expand(step)
        skip = exact(dot, heads_ref[...], b["EM"][...], 3)[2:3, :]
        rest = mm(out_map, carried) * grown_wide + skip * values
        for p in range(pairs):
            part = slice(p * LANES, (p + 1) * LANES)
            mixing = jnp.concatenate(
                [scores * decays(cumulative, turned, 2 * p + i, False) for i in range(2)], axis=1
            )
            inner = mm(mixing, halves(weighted[:, part]))
            b["SSD"][tok(g), part] = inner + rest[:, part]
        ends = expand(jnp.exp(last - cumulative) * step)
        state = mm(in_map.T, values * ends)
        b["RUN"][...] = carried * grown_wide[GROUP - 1 :, :] + state

    def between(items, g):
        for hop in range(1, nz):

            @pl.when(g == min(hop, groups) - 1)
            def _(hop=hop):
                forward(items, hop)

    def ssd_step(g):
        ssd_forward(g)
        between((wg, wo), g)

    each_group(ssd_step)
    cg.wait()
    wg.finish()
    wo.finish()

    norm_gain = lambda: b["NG"][pl.ds(0, 1), :]

    def gate(g):
        raw = dot(b["XN"][tok(g), :], b["WG"][...])
        gated = b["SSD"][tok(g), :] * (raw * sigmoid(raw))
        mixed_grad = dot(b["CF"][tok(g), :], b["WO"][...])
        b["GR"][tok(g), :] = raw
        b["GT"][tok(g), :] = gated
        b["MG"][tok(g), :] = mixed_grad
        squares = lanes_sum(gated * gated)
        cross = lanes_sum(mixed_grad * norm_gain() * gated)
        both = jnp.where(iota((GROUP, LANES), 1) < 4, squares, cross)
        b["ST"][:, tok(g)] = both.T[:8, :]

    each_group(gate)
    stat.start()
    flip("CF", "CT")
    stat.wait()

    def gate_back(g):
        sums = b["ST"][:, tok(g)]
        for k in range(seq - 1):
            sums = sums + b["EX"][k, :, tok(g)]
        sums = jnp.concatenate([sums] * (LANES // 8), axis=0).T
        squares, cross = sums[:, 0:1], sums[:, 4:5]
        inverse = lax.rsqrt(squares / INNER + epsilon)
        gated, mixed_grad, raw = b["GT"][tok(g), :], b["MG"][tok(g), :], b["GR"][tok(g), :]
        unit = gated * inverse
        b["MX"][tok(g), :] = (unit * norm_gain()).astype(bf16)
        b["NACC"][pl.ds(0, 1), :] += rows_sum(mixed_grad * unit)
        gated_grad = inverse * (mixed_grad * norm_gain() - unit * (inverse * cross / INNER))
        sig = sigmoid(raw)
        b["DY"][tok(g), :] = gated_grad * (raw * sig)
        slope = sig * (1.0 + raw * (1.0 - sig))
        b["PG"][tok(g), :] = (gated_grad * b["SSD"][tok(g), :] * slope).astype(bf16)

    each_group(gate_back)

    def weight_grad(fold, left, right):
        def block(rows_here):
            fold.grad[rows_here] = dot(b[left][rows_here], b[right][...]).astype(bf16)

        def offset(i):
            farther = nz - (i + 1) // 2
            return farther * (2 * lax.rem(i, 2) - 1)

        def each(i, carry):
            block(fold.block(offset(i)))
            return carry

        block(fold.block(nz))
        fold.begin()
        lax.fori_loop(1, dp, each, 0)

    weight_grad(fo, "CT", "MX")
    weight_grad(fg, "NT", "PG")

    def out_product(g):
        b["OP"][tok(g), :] = dot_nt(b["MX"][tok(g), :], b["WO"][...]).astype(bf16)

    each_group(out_product)
    outs.start()

    b["RUN"][...] = jnp.zeros_like(b["RUN"])

    def ssd_backward(g):
        values, in_map, out_map, raw, step, cumulative = front(g)
        turned = cumulative.T
        last = cumulative[GROUP - 1 :, :]
        grown_wide = expand(jnp.exp(cumulative))
        step_wide = expand(step)
        weighted = values * step_wide
        skip = exact(dot, heads_ref[...], b["EM"][...], 3)[2:3, :]
        out_grad = b["DY"][tok(g), :]
        ssd = b["SSD"][tok(g), :]
        carried, after = b["CAR"][g], b["RUN"][...]
        rate = heads_ref[pl.ds(1, 1), :]

        b["NACC"][pl.ds(1, 1), :] += rows_sum(out_grad * values)
        cumul_grad = per_head(out_grad * (ssd - skip * values))
        grown_grad = out_grad * grown_wide
        ends = jnp.exp(last - cumulative)
        ends_wide = expand(ends * step)
        out_map_grad = mm_nt(grown_grad, carried)
        scaled_grad = mm(in_map, after)
        in_map_grad = mm_nt(values * ends_wide, after)
        ends_grad = per_head(scaled_grad * values)
        step_grad = ends_grad * ends
        ends_cumul = ends_grad * ends * step
        cumul_grad = cumul_grad - ends_cumul
        decay_sum = rows_sum(after * carried)
        decay_grad = per_head(jnp.broadcast_to(decay_sum, (8, w)))[0:1, :] * jnp.exp(last)
        last_grad = rows_sum(ends_cumul) + decay_grad
        b["RUN"][...] = mm(out_map.T, grown_grad) + after * grown_wide[GROUP - 1 :, :]
        scores_turned = mm_nt(in_map, out_map)
        scores_grad = jnp.zeros((GROUP, GROUP), f32)
        value_grads, step_parts = [], []
        for p in range(pairs):
            part = slice(p * LANES, (p + 1) * LANES)
            grads_here = halves(out_grad[:, part])
            mixing = jnp.concatenate(
                [scores_turned * decays(cumulative, turned, 2 * p + i, True) for i in range(2)],
                axis=1,
            )
            inner = mm(mixing, grads_here)
            step_parts.append(inner * values[:, part])
            value_grads.append(inner * step_wide[:, part])
            mixing_grad = mm_nt(grads_here, weighted[:, part])
            for i in range(2):
                scores_grad = scores_grad + (
                    decays(cumulative, turned, 2 * p + i, False)
                    * mixing_grad[i * GROUP : (i + 1) * GROUP]
                )
        inner_step = per_head(jnp.concatenate(step_parts, axis=1))
        step_grad = step_grad + inner_step
        cumul_grad = cumul_grad - inner_step * step
        values_grad = (
            jnp.concatenate(value_grads, axis=1) + scaled_grad * ends_wide + skip * out_grad
        )
        out_map_grad = out_map_grad + mm(scores_grad, in_map)
        in_map_grad = in_map_grad + mm(scores_grad.T, out_map)
        at_last = iota((GROUP, LANES), 0) == GROUP - 1
        cumul_grad = cumul_grad + jnp.where(at_last, last_grad, 0.0)
        upper = (iota((GROUP, GROUP), 0) <= iota((GROUP, GROUP), 1)).astype(f32).astype(bf16)
        pieces = split(cumul_grad, 3)
        rated_grad = dot(upper, pieces[2]) + dot(upper, pieces[1]) + dot(upper, pieces[0])
        step_grad = step_grad + rated_grad * rate
        b["HACC"][pl.ds(1, 1), :] += rows_sum(rated_grad * step * rate)
        raw_grad = step_grad * sigmoid(raw)
        b["HACC"][pl.ds(0, 1), :] += rows_sum(raw_grad)
        pre = b["PRE"][tok(g), :]
        sig = sigmoid(pre)
        conv_grad = jnp.concatenate((values_grad, in_map_grad, out_map_grad), axis=1)
        pre_grad = conv_grad * (sig * (1.0 + pre * (1.0 - sig)))
        b["DP"][tok(g), :] = pre_grad
        before = b["CI"][at(g * GROUP, GROUP + 8, 8), :]
        following = jnp.concatenate((pre_grad, b["DP"][at(g * GROUP + GROUP, 8, 8), :]), axis=0)
        total = None
        for k in range(CONV):
            shift = 8 - (CONV - 1) + k
            b["CACC"][pl.ds(k, 1), :] += rows_sum(pre_grad * before[shift : shift + GROUP])
            back = CONV - 1 - k
            term = b["CW"][pl.ds(k, 1), :] * following[back : back + GROUP]
            total = term if total is None else total + term
        b["CACC"][pl.ds(CONV, 1), :] += rows_sum(pre_grad)
        b["PV"][tok(g), :] = total[:, :w].astype(bf16)
        b["PS"][tok(g), :] = jnp.concatenate((total[:, w:], raw_grad), axis=1).astype(bf16)

    def ssd_back_step(g):
        ssd_backward(groups - 1 - g)
        between((fo, fg), g)

    each_group(ssd_back_step)

    weight_grad(fv, "NT", "PV")
    weight_grad(fs, "NT", "PS")

    def normed_grad(g):
        total = (
            dot_nt(b["PV"][tok(g), :], b["WV"][...])
            + dot_nt(b["PG"][tok(g), :], b["WG"][...])
            + dot_nt(b["PS"][tok(g), :], b["WS"][...])
        )
        b["NP"][tok(g), :] = total.astype(bf16)
        unit = b["XF"][tok(g), :].astype(f32) * b["INV"][tok(g), pl.ds(0, 1)]
        b["PACC"][pl.ds(0, 1), :] += rows_sum(total * unit)

    each_group(normed_grad)
    grads.start()
    b["GM"][:, 0, :] = pre_table().blocks(b["PACC"][pl.ds(0, 1), :])
    b["GM"][:, 1, :] = norm_table().blocks(b["NACC"][pl.ds(0, 1), :])
    taps = conv_table()
    for k in range(CONV + 1):
        b["GM"][:, 2 + k, :] = taps.blocks(b["CACC"][pl.ds(k, 1), :])
    skip_grad = per_head(jnp.broadcast_to(b["NACC"][pl.ds(1, 1), :], (8, w)))
    heads_here = w // HEAD_DIM
    total = jnp.zeros((8, LANES), f32)
    kinds = (b["HACC"][pl.ds(0, 1), :], b["HACC"][pl.ds(1, 1), :], skip_grad[0:1, :])
    for i, row in enumerate(kinds):
        place = iota((LANES, LANES), 1) - s * heads_here - i * HEADS
        source = iota((LANES, LANES), 0)
        move = ((place == source) & (source < heads_here)).astype(f32).astype(bf16)
        total = total + exact(dot, jnp.broadcast_to(row, (8, LANES)), move, 3)
    b["GM"][:, 7, :] = jnp.broadcast_to(total[0:1, :], (owners, LANES))
    fm.begin()
    fo.finish()
    fg.finish()
    for hop in range(1, nz):
        forward((fv, fs, fm), hop)
    outs.wait()
    total = x_ref[...].astype(f32) + b["OP"][mine, :].astype(f32)
    for k in range(seq - 1):
        total = total + b["OB"][k].astype(f32)
    block_ref[...] = total.astype(bf16)
    grads.wait()
    total = b["NP"][mine, :].astype(f32)
    for k in range(seq - 1):
        total = total + b["NB"][k].astype(f32)
    scaled = total * b["GA"][pl.ds(0, 1), :]
    inverse = b["INV"][mine, pl.ds(0, 1)]
    unit = x_ref[...].astype(f32) * inverse
    mean = lanes_sum(scaled * unit) / width
    ingrad_ref[...] = inverse * (scaled - unit * mean) + cot_ref[...].astype(f32)
    for item in (fv, fs, fm):
        item.finish()
    for item in (fo, fg, fv, fs, fm):
        item.members.wait()
    shared = None
    for q in range(seq):
        outshare_ref[:, pl.ds(q * w, w)] = b["FO"][q].astype(f32)
        inshare_ref[:, pl.ds(q * w, w)] = b["FG"][q].astype(f32)
        inshare_ref[:, pl.ds(INNER + q * w, w)] = b["FV"][q].astype(f32)
        part = b["FS"][q].astype(f32)
        maps = part[:, :MAPS]
        shared = maps if shared is None else shared + maps
        first = INNER + CONV_CH + q * heads_here
        inshare_ref[:, pl.ds(first, heads_here)] = part[:, MAPS : MAPS + heads_here]
        small = b["FM"][q]
        smalls = small if q == 0 else smalls + small
    inshare_ref[:, pl.ds(INNER + INNER, MAPS)] = shared
    smallout_ref[...] = smalls
    for drain in site.pending:
        drain()


def fused(x, cot, in_weight, shared, out_t, small, heads, dp, seq):
    length, width = x.shape
    rows, proj = in_weight.shape
    plan = scratch_plan(dp, seq, length, width, rows)
    names = tuple(plan)
    sems = (10 * (seq - 1 + dp) + 5 * (seq - 1), 7)
    vmem = pl.BlockSpec(memory_space=pltpu.VMEM)
    return pl.pallas_call(
        functools.partial(fused_kernel, dp, seq, names, sems),
        out_shape=[
            jax.ShapeDtypeStruct((length, width), bf16),
            jax.ShapeDtypeStruct((length, width), f32),
            jax.ShapeDtypeStruct((rows, proj), f32),
            jax.ShapeDtypeStruct((rows, INNER), f32),
            jax.ShapeDtypeStruct((1, 8, LANES), f32),
        ],
        in_specs=[vmem] * 7,
        out_specs=[vmem] * 5,
        scratch_shapes=[pltpu.VMEM(*plan[name]) for name in names]
        + [
            pltpu.SemaphoreType.DMA((sems[0],)),
            pltpu.SemaphoreType.DMA((sems[0],)),
            pltpu.SemaphoreType.DMA((sems[1],)),
        ],
        compiler_params=pltpu.CompilerParams(
            collective_id=0, has_side_effects=True, vmem_limit_bytes=58 * 2**20
        ),
    )(x, cot, in_weight, shared, out_t, small, heads)


def fits(dp, seq, block_input, in_weight):
    seq_dev, length, width = block_input.shape
    rows = in_weight.shape[0]
    owners = dp * seq
    return (
        seq_dev == 1
        and dp % 2 == 0
        and dp >= 4
        and seq > 1
        and length % GROUP == 0
        and rows % 16 == 0
        and INNER % (seq * LANES) == 0
        and INNER % owners == 0
        and CONV_CH % owners == 0
        and CONV_CH // owners <= LANES
        and dp // 2 <= seq * length // GROUP + 1
    )


def lane_row(value):
    value = value.reshape(1, -1).astype(f32)
    return jnp.pad(value, ((0, 0), (0, LANES - value.shape[1])))


def on_device_fused(
    block_input,
    in_weight,
    out_weight,
    pre_gain,
    norm_gain,
    conv_weight,
    conv_bias,
    dt_bias,
    decay_log,
    skip_gain,
    cotangent,
):
    dp, seq = lax.axis_size("dp"), lax.axis_size("seq")
    here = HEADS // seq
    rows = in_weight.shape[0]
    maps, steps = in_weight[:, INNER + INNER : INNER + CONV_CH], in_weight[:, INNER + CONV_CH :]
    filler = jnp.zeros((rows, LANES - here), in_weight.dtype)
    shared = jnp.stack(
        [
            jnp.concatenate((maps, steps[:, q * here : (q + 1) * here], filler), axis=1)
            for q in range(seq)
        ]
    )
    small = jnp.concatenate(
        [lane_row(pre_gain), lane_row(norm_gain)]
        + [lane_row(conv_weight[k]) for k in range(CONV)]
        + [lane_row(conv_bias), jnp.zeros((1, LANES), f32)]
    )[None]
    own = jnp.stack((dt_bias, -jnp.exp(decay_log), skip_gain))
    own = lax.dynamic_slice_in_dim(own, lax.axis_index("seq") * here, here, axis=1)
    own = jnp.pad(own, ((0, 5), (0, LANES - here)))
    block, in_grad, in_share, out_share, smalls = fused(
        block_input[0],
        cotangent[0],
        in_weight,
        shared,
        out_weight.T,
        small,
        own,
        dp,
        seq,
    )
    smalls = smalls[0]
    return (
        block[None],
        in_grad[None],
        in_share,
        out_share.T,
        smalls[0, : pre_gain.size],
        smalls[1, : norm_gain.size],
        smalls[2 : 2 + CONV, : conv_bias.size],
        smalls[2 + CONV, : conv_bias.size],
        smalls[7, :HEADS],
        smalls[7, HEADS : 2 * HEADS],
        smalls[7, 2 * HEADS : 3 * HEADS],
    )


def from_behind(value, axis, steps):
    count = lax.axis_size(axis)
    leading, last = (max(0, -steps), min(count, count - steps))
    return lax.ppermute(value, axis, [(source, source + steps) for source in range(leading, last)])


def convolve(padded, conv_weight, conv_bias):
    taps = conv_weight.shape[0]
    length = padded.shape[-2] - taps + 1
    total = conv_bias
    for index in range(taps):
        total = total + conv_weight[index] * lax.slice_in_dim(
            padded, index, index + length, axis=padded.ndim - 2
        )
    return total


def running_sum(value):
    length = value.shape[1]
    lower = (jnp.arange(length)[:, None] >= jnp.arange(length)[None, :]).astype(value.dtype)
    return jnp.einsum("ts,bsh->bth", lower, value, precision=lax.Precision.HIGHEST)


def carry_scan(state, decay, axis, sign):
    count = lax.axis_size(axis)
    within, within_decay = state, decay
    entering, entering_decay = None, None
    width = 1
    while width < count:
        moved = from_behind(within.astype(jnp.bfloat16), axis, sign * width).astype(jnp.float32)
        last = 2 * width >= count
        if not last or entering is None:
            moved_decay = from_behind(within_decay, axis, sign * width)
        if entering is None:
            entering, entering_decay = moved, moved_decay
        else:
            entering = entering + entering_decay[:, :, None, None] * moved
            if not last:
                entering_decay = entering_decay * moved_decay
        if not last:
            within = within + within_decay[:, :, None, None] * moved
            within_decay = within_decay * moved_decay
        width *= 2
    return jnp.zeros_like(state) if entering is None else entering


def front_fn(tail, rim, conv_weight, conv_bias, dt_bias, decay_log):
    conv_in = tail[..., :CONV_CH]
    dt_raw = tail[..., CONV_CH:]
    padded = jnp.concatenate([rim, conv_in], axis=-2)
    conv_out = jax.nn.silu(convolve(padded, conv_weight, conv_bias))
    leading = conv_out.shape[:-1]
    values = conv_out[..., :INNER].reshape(leading + (HEADS, HEAD_DIM))
    in_map = conv_out[..., INNER : INNER + STATE]
    out_map = conv_out[..., INNER + STATE :]
    step = jax.nn.softplus(dt_raw + dt_bias)
    cumulative = running_sum(step * -jnp.exp(decay_log))
    return (values, in_map, out_map, step, cumulative)


def group_state(values, in_map, step, cumulative):
    weights_end = jnp.exp(cumulative[-1][None, :] - cumulative) * step
    state = jnp.einsum("shp,sn->hpn", values * weights_end[:, :, None], in_map, precision=highest)
    return (state, jnp.exp(cumulative[-1]))


def group_output(values, in_map, out_map, step, cumulative, carried, skip_gain):
    length = values.shape[0]
    scores = jnp.dot(out_map, in_map.T, precision=highest)
    causal = jnp.arange(length)[:, None] >= jnp.arange(length)[None, :]
    spread = cumulative[:, None, :] - cumulative[None, :, :]
    decay = jnp.exp(jnp.where(causal[:, :, None], spread, -10000.0))
    mixing = scores[:, :, None] * decay * step[None, :, :]
    inner_part = jnp.einsum("tsh,shp->thp", mixing, values, precision=highest)
    carried_part = (
        jnp.einsum("tn,hpn->thp", out_map, carried, precision=highest)
        * jnp.exp(cumulative)[:, :, None]
    )
    return inner_part + carried_part + skip_gain[None, :, None] * values


def state_fn(values, in_map, step, cumulative):
    return jax.vmap(group_state)(values, in_map, step, cumulative)


def out_fn(values, in_map, out_map, step, cumulative, gate_raw, carried, skip_gain, norm_gain):
    ssd_out = jax.vmap(group_output, in_axes=(0, 0, 0, 0, 0, 0, None))(
        values, in_map, out_map, step, cumulative, carried, skip_gain
    )
    ssd_out = ssd_out.reshape(gate_raw.shape)
    gated = ssd_out * jax.nn.silu(gate_raw)
    inverse = lax.rsqrt(jnp.mean(gated * gated, axis=-1, keepdims=True) + epsilon)
    return gated * inverse * norm_gain


def by_rows(grad, owners):
    return grad.reshape(owners, -1)


def by_columns(grad, owners):
    rows = grad.shape[0]
    return jnp.transpose(grad.reshape(rows, owners, -1), (1, 0, 2)).reshape(owners, -1)


def on_device(
    block_input,
    in_weight,
    out_weight,
    pre_gain,
    norm_gain,
    conv_weight,
    conv_bias,
    dt_bias,
    decay_log,
    skip_gain,
    cotangent,
):
    seq_dev, length, width = block_input.shape
    dp, seq = lax.axis_size("dp"), lax.axis_size("seq")
    owners = dp * seq
    both = ("dp", "seq")
    if fits(dp, seq, block_input, in_weight):
        return on_device_fused(
            block_input,
            in_weight,
            out_weight,
            pre_gain,
            norm_gain,
            conv_weight,
            conv_bias,
            dt_bias,
            decay_log,
            skip_gain,
            cotangent,
        )
    small_parts = (pre_gain, norm_gain, conv_weight.reshape(-1), conv_bias)
    small_sizes = [part.size for part in small_parts]
    small = jnp.concatenate(small_parts)
    in_full = lax.all_gather(in_weight, both, axis=0, tiled=True)
    gate_w, tail_w = in_full[:, :INNER], in_full[:, INNER:]
    out_t = lax.all_gather(out_weight.T, both, axis=0, tiled=True)
    small_all = lax.all_gather(small, both, axis=0)
    pieces, start = [], 0
    for size in small_sizes:
        pieces.append(small_all[:, start : start + size])
        start += size
    pre_full, norm_full, conv_b_full = (pieces[i].reshape(-1) for i in (0, 1, 3))
    conv_w_full = jnp.transpose(pieces[2].reshape(owners, CONV, -1), (1, 0, 2)).reshape(CONV, -1)
    pre_float = pre_full.astype(jnp.float32)
    norm_float = norm_full.astype(jnp.float32)
    inputs = block_input.astype(jnp.float32)
    inv_pre = lax.rsqrt(jnp.mean(inputs * inputs, axis=-1, keepdims=True) + epsilon)
    normed = (inputs * inv_pre * pre_float).astype(jnp.bfloat16)
    flat_normed = normed.reshape(seq_dev * length, width)
    gate_raw = jnp.dot(flat_normed, gate_w, preferred_element_type=jnp.float32).reshape(
        seq_dev, length, -1
    )
    tail = jnp.dot(flat_normed, tail_w, preferred_element_type=jnp.float32).reshape(
        seq_dev, length, -1
    )
    conv_in = tail[:, length - (CONV - 1) :, :CONV_CH]
    rim = from_behind(conv_in, "seq", 1)
    front_out, front_pull = jax.vjp(
        front_fn,
        tail,
        rim,
        conv_w_full.astype(jnp.float32),
        conv_b_full.astype(jnp.float32),
        dt_bias,
        decay_log,
    )
    values, in_map, out_map, step, cumulative = front_out
    state_out, state_pull = jax.vjp(state_fn, values, in_map, step, cumulative)
    state, decay = state_out
    carried = carry_scan(state, decay, "seq", 1)
    mixed_float, out_pull = jax.vjp(
        out_fn, values, in_map, out_map, step, cumulative, gate_raw, carried, skip_gain, norm_float
    )
    mixed = mixed_float.astype(jnp.bfloat16)
    flat_mixed = mixed.reshape(seq_dev * length, INNER)
    block_output = (
        inputs
        + jnp.dot(flat_mixed, out_t.T, preferred_element_type=jnp.float32).reshape(
            seq_dev, length, width
        )
    ).astype(jnp.bfloat16)
    flat_grad = cotangent.reshape(seq_dev * length, width)
    mixed_grad = jnp.dot(flat_grad, out_t, preferred_element_type=jnp.float32).reshape(
        seq_dev, length, INNER
    )
    out_w_grad = jnp.dot(flat_grad.T, flat_mixed, preferred_element_type=jnp.float32)
    (
        values_a,
        in_map_a,
        out_map_grad,
        step_a,
        cumul_a,
        gate_grad,
        local_grad,
        skip_grad,
        norm_grad,
    ) = out_pull(mixed_grad)

    later_grad = carry_scan(local_grad, decay, "seq", -1)
    decay_grad = jnp.sum(later_grad * carried, axis=(2, 3))
    values_b, in_map_b, step_b, cumul_b = state_pull((later_grad, decay_grad))
    front_grads = front_pull(
        (
            values_a + values_b,
            in_map_a + in_map_b,
            out_map_grad,
            step_a + step_b,
            cumul_a + cumul_b,
        )
    )
    tail_float, rim_grad, conv_w_grad, conv_b_grad, dt_grad, decay_log_grad = front_grads
    returned = from_behind(rim_grad, "seq", -1)
    tail_float = tail_float + jnp.pad(returned, ((0, 0), (length - (CONV - 1), 0), (0, HEADS)))
    tail_grad = tail_float.astype(jnp.bfloat16).reshape(seq_dev * length, -1)
    gate_grad = gate_grad.astype(jnp.bfloat16).reshape(seq_dev * length, -1)
    gate_w_grad = jnp.dot(flat_normed.T, gate_grad, preferred_element_type=jnp.float32)
    tail_w_grad = jnp.dot(flat_normed.T, tail_grad, preferred_element_type=jnp.float32)
    normed_grad = (
        jnp.dot(gate_grad, gate_w.T, preferred_element_type=jnp.float32)
        + jnp.dot(tail_grad, tail_w.T, preferred_element_type=jnp.float32)
    ).reshape(seq_dev, length, width)
    pre_grad = jnp.sum(normed_grad * inputs * inv_pre, axis=(0, 1))
    scaled = normed_grad * pre_float
    unit = inputs * inv_pre
    input_grad = inv_pre * (
        scaled - unit * jnp.mean(scaled * unit, axis=-1, keepdims=True)
    ) + cotangent.astype(jnp.float32)
    small_grads = jnp.concatenate(
        (
            by_rows(pre_grad, owners),
            by_rows(norm_grad, owners),
            by_columns(conv_w_grad, owners),
            by_rows(conv_b_grad, owners),
        ),
        axis=1,
    )
    heads = jnp.concatenate((dt_grad, decay_log_grad, skip_grad))
    scatter = functools.partial(
        lax.psum_scatter, axis_name=both, scatter_dimension=0, tiled=True
    )
    in_share = scatter(jnp.concatenate((gate_w_grad, tail_w_grad), axis=1))
    out_share = scatter(out_w_grad).T
    small_share = scatter(small_grads)[0]
    heads = lax.psum(heads, both)
    shares, start = [], 0
    for size in small_sizes:
        shares.append(small_share[start : start + size])
        start += size
    pre_share, norm_share, conv_w_share, conv_b_share = shares
    conv_w_share = conv_w_share.reshape(CONV, -1)
    heads_total = (heads[:HEADS], heads[HEADS : 2 * HEADS], heads[2 * HEADS :])
    return (
        block_output,
        input_grad,
        in_share,
        out_share,
        pre_share,
        norm_share,
        conv_w_share,
        conv_b_share,
        heads_total[0],
        heads_total[1],
        heads_total[2],
    )


def solution(mesh):
    in_specs = (
        P("dp", "seq", None),
        P(("dp", "seq"), None),
        P(None, ("dp", "seq")),
        P(("dp", "seq")),
        P(("dp", "seq")),
        P(None, ("dp", "seq")),
        P(("dp", "seq")),
        P(),
        P(),
        P(),
        P("dp", "seq", None),
    )
    out_specs = (
        P("dp", "seq", None),
        P("dp", "seq", None),
        P(("dp", "seq"), None),
        P(None, ("dp", "seq")),
        P(("dp", "seq")),
        P(("dp", "seq")),
        P(None, ("dp", "seq")),
        P(("dp", "seq")),
        P(),
        P(),
        P(),
    )
    return jax.shard_map(
        on_device, mesh=mesh, in_specs=in_specs, out_specs=out_specs, check_vma=False
    )
```

```python
import functools

import jax
import jax.numpy as jnp
from jax import lax
from jax.experimental import pallas as pl
from jax.experimental.pallas import tpu as pltpu
from jax.sharding import PartitionSpec as P

HEADS = 32
HEAD_DIM = 64
STATE = 128
CONV = 4
GROUP = 128
INNER = 2048
CONV_CH = 2304
LANES = 128
MAPS = CONV_CH - INNER
SHARED = MAPS + LANES


epsilon = 1e-05
highest = lax.Precision.HIGH
bf16 = jnp.bfloat16
f32 = jnp.float32


def at(start, size, multiple):
    return pl.ds(start if isinstance(start, int) else pl.multiple_of(start, multiple), size)


def remote(src, dst, send, recv, device):
    return pltpu.make_async_remote_copy(
        src_ref=src,
        dst_ref=dst,
        send_sem=send,
        recv_sem=recv,
        device_id=device,
        device_id_type=pl.DeviceIdType.MESH,
    )


class Site:
    def __init__(self, dp, seq, send, recv, own):
        self.nz, self.ns = dp // 2, seq
        self.d, self.s = lax.axis_index("dp"), lax.axis_index("seq")
        far, level = lax.rem(self.d, 2), self.d // 2
        self.dp, self.half = dp, dp // 2
        self.place = level + far * (dp - 1 - 2 * level)
        self.owner = self.d * seq + self.s
        self.send, self.recv, self.own = send, recv, own
        self.used, self.used_own = 0, 0
        self.pending = []

    def group(self, k):
        return (self.d, lax.rem(self.s + k, self.ns))

    def ring(self, offset):
        place = lax.rem(self.place + offset + 2 * self.dp, self.dp)
        far = place // self.nz
        level = place + far * (self.dp - 1 - 2 * place)
        return level * 2 + far

    def beside(self, way):
        return (self.ring(way), self.s)

    def twin(self):
        return (self.d, self.s + 1 - 2 * lax.rem(self.s, 2))

    def take(self, count):
        self.used += count
        return self.used - count

    def copy(self, src, dst, slot, device):
        return remote(src, dst, self.send.at[slot], self.recv.at[slot], device)

    def greet(self):
        barrier = pltpu.get_barrier_semaphore()
        partners = [self.group(k) for k in range(1, self.ns)]
        partners += [self.beside(1), self.beside(-1)]
        for partner in partners:
            pl.semaphore_signal(
                barrier, inc=1, device_id=partner, device_id_type=pl.DeviceIdType.MESH
            )
        pl.semaphore_wait(barrier, len(partners))


class GroupCopy:
    def __init__(self, site, source, dest, local, wanted=None):
        self.site, self.source, self.dest, self.local = site, source, dest, local
        self.wanted = wanted
        self.base = site.take(site.ns - 1)
        if local:
            self.own = site.used_own
            site.used_own += 1
        site.pending.append(self.drain)

    def own_copy(self):
        site = self.site
        return pltpu.make_async_copy(self.source(site.s), self.dest(0), site.own.at[self.own])

    def copy(self, k):
        site = self.site
        member = lax.rem(site.s + k, site.ns)
        return site.copy(self.source(member), self.dest(k), self.base + k - 1, site.group(k))

    def each(self, act, sending):
        site = self.site
        for k in range(1, site.ns):
            if self.wanted is None:
                act(k)
                continue
            other = lax.rem(site.s + (k if sending else site.ns - k), site.ns)
            ends = (site.s, other) if sending else (other, site.s)
            pl.when(self.wanted(*ends))(functools.partial(act, k))

    def start(self):
        self.each(lambda k: self.copy(k).start(), True)
        if self.local:
            self.own_copy().start()

    def wait(self):
        if self.local:
            self.own_copy().wait()
        self.each(lambda k: self.copy(k).wait_recv(), False)

    def drain(self):
        self.each(lambda k: self.copy(k).wait_send(), True)


class Spread:
    def __init__(self, site, buf, rows, source, twins=False):
        self.site, self.buf, self.rows, self.source = site, buf, rows, source
        self.block_rows, self.twins = site.ns * rows, twins
        self.members = GroupCopy(
            site, source, lambda k: buf.at[at(site.owner * rows, rows, rows)], True
        )
        self.base = {way: site.take(site.half) for way in (1, -1)}
        self.twin_base = {way: site.take(site.half) for way in (1, -1)} if twins else None
        site.pending.append(self.drain)

    def block(self, way, offset, halved):
        size = self.block_rows
        start = self.site.ring(offset) * size
        if self.twins:
            size = size // 2
            start = start + lax.rem(self.site.s, 2) * size
        if halved:
            size = size // 2
            start = start if way > 0 else start + size
        return self.buf.at[at(start, size, size)]

    def copy(self, way, hop):
        site = self.site
        block = self.block(way, way * (1 - hop), hop == site.half)
        return site.copy(block, block, self.base[way] + hop - 1, site.beside(way))

    def twin_copy(self, way, hop):
        site = self.site
        block = self.block(way, -way * hop, hop == site.half)
        return site.copy(block, block, self.twin_base[way] + hop - 1, site.twin())

    def begin(self):
        self.members.wait()
        for way in (1, -1):
            self.copy(way, 1).start()

    def forward(self, hop):
        for way in (1, -1):
            self.copy(way, hop).wait_recv()
            self.copy(way, hop + 1).start()
            if self.twins:
                self.twin_copy(way, hop).start()

    def finish(self):
        last = self.site.half
        for way in (1, -1):
            self.copy(way, last).wait_recv()
            if self.twins:
                self.twin_copy(way, last).start()
        if self.twins:
            for way in (1, -1):
                for hop in range(1, last + 1):
                    self.twin_copy(way, hop).wait_recv()

    def drain(self):
        for way in (1, -1):
            for hop in range(1, self.site.half + 1):
                self.copy(way, hop).wait_send()
                if self.twins:
                    self.twin_copy(way, hop).wait_send()


class Fold:
    def __init__(self, site, grad, rows, boxes, sums, total, final, twins=False):
        self.site, self.grad, self.rows, self.twins = site, grad, rows, twins
        self.members_in = site.ns // 2 if twins else site.ns
        self.block_rows = self.members_in * rows
        self.boxes, self.sums = dict(zip((1, -1), boxes)), dict(zip((1, -1), sums))
        self.total, self.final = total, final
        self.base = {way: site.take(site.half) for way in (1, -1)}
        self.members = GroupCopy(
            site,
            lambda q: total.at[self.rows_for(q)],
            lambda k: final.at[site.s],
            False,
            (lambda a, q: lax.rem(a, 2) == q // self.members_in) if twins else None,
        )
        site.pending.append(self.drain)

    def rows_for(self, q):
        return at(lax.rem(q, self.members_in) * self.rows, self.rows, self.rows)

    def block(self, offset):
        return at(self.site.ring(offset) * self.block_rows, self.block_rows, self.block_rows)

    def copy(self, way, hop):
        site, size = self.site, self.block_rows // 2
        if hop == 1:
            shift = 0 if way > 0 else size
            source = self.grad.at[at(site.ring(way * site.half) * 2 * size + shift, size, size)]
            dest = self.boxes[way].at[0, pl.ds(shift, size)]
        else:
            source, dest = self.sums[way].at[hop - 2], self.boxes[way].at[hop - 1]
        return site.copy(source, dest, self.base[way] + hop - 1, site.beside(way))

    def begin(self):
        for way in (1, -1):
            self.copy(way, 1).start()

    def forward(self, hop):
        site, size = self.site, self.block_rows // 2
        for way in (1, -1):
            self.copy(way, hop).wait_recv()
            kept = self.grad[self.block(way * (site.half - hop))]
            box, sums = self.boxes[way], self.sums[way]
            if hop == 1:
                near, far = (slice(0, size), slice(size, None))[::way]
                both = kept[near].astype(f32) + box[0, near].astype(f32)
                sums[0, near] = both.astype(sums.dtype)
                sums[0, far] = kept[far]
            else:
                both = kept.astype(f32) + box[hop - 1].astype(f32)
                sums[hop - 1] = both.astype(sums.dtype)
            self.copy(way, hop + 1).start()

    def finish(self):
        site = self.site
        total = self.grad[self.block(0)].astype(f32)
        for way in (1, -1):
            self.copy(way, site.half).wait_recv()
            total = total + self.boxes[way][site.half - 1].astype(f32)
        self.total[...] = total.astype(self.total.dtype)
        self.members.start()
        self.final[site.s] = self.total[self.rows_for(site.s)]

    def drain(self):
        for way in (1, -1):
            for hop in range(1, self.site.half + 1):
                self.copy(way, hop).wait_send()


def dot(a, b):
    return jnp.dot(a, b, preferred_element_type=f32)


def dot_nt(a, b):
    return lax.dot_general(a, b, (((1,), (1,)), ((), ())), preferred_element_type=f32)


def split(value, parts):
    pieces = []
    for _ in range(parts - 1):
        pieces.append(value.astype(bf16))
        value = value - pieces[-1].astype(f32)
    return pieces + [value.astype(bf16)]


def exact(product, value, onehot, parts):
    total = None
    for piece in split(value, parts)[::-1]:
        term = product(piece, onehot)
        total = term if total is None else total + term
    return total


def wide(product, a, b, passes):
    if passes == 1:
        return product(a.astype(bf16), b.astype(bf16))
    (a_hi, a_lo), (b_hi, b_lo) = split(a, 2), split(b, 2)
    total = product(a_hi, b_lo)
    if passes == 3:
        total = total + product(a_lo, b_hi)
    return total + product(a_hi, b_hi)


def mm(a, b, passes=3):
    return wide(dot, a, b, passes)


def mm_nt(a, b, passes=3):
    return wide(dot_nt, a, b, passes)


def iota(shape, axis):
    return lax.broadcasted_iota(jnp.int32, shape, axis)


def sigmoid(value):
    return 1.0 / (1.0 + jnp.exp(-value))


def softplus(value):
    small = jnp.exp(-jnp.abs(value))
    series = small * (1.0 - small * (0.5 - small * (1 / 3 - small * (0.25 - small * 0.2))))
    return jnp.maximum(value, 0.0) + jnp.where(small < 0.03, series, jnp.log(1.0 + small))


def rows_sum(value):
    return jnp.sum(value, axis=0, keepdims=True)


def lanes_sum(value):
    return jnp.sum(value, axis=1, keepdims=True)


class Table:
    def __init__(self, owners, channel, size):
        count = channel.shape[1]
        first = iota((owners, count), 0) * size
        place = channel - first
        self.mask = (place >= 0) & (place < size)
        spot = jnp.sum(jnp.where(self.mask, place.astype(f32), 0.0), axis=0, keepdims=True)
        self.onehot = (iota((LANES, count), 0).astype(f32) == spot).astype(f32).astype(bf16)

    def row(self, blocks):
        return rows_sum(jnp.where(self.mask, dot(blocks.astype(bf16), self.onehot), 0.0))

    def blocks(self, row):
        return exact(dot_nt, jnp.where(self.mask, row, 0.0), self.onehot, 3)


def scratch_plan(dp, seq, length, width, rows):
    nz, owners, tokens = dp // 2, dp * seq, seq * length
    w = INNER // seq
    cw, groups, block = w + MAPS, tokens // GROUP, seq * rows
    plan = dict(
        XF=((tokens, width), bf16),
        CF=((tokens, width), bf16),
        WV=((width, w), bf16),
        WS=((width, SHARED), bf16),
        WG=((width, w), bf16),
        WO=((width, w), bf16),
        SM=((owners, 8, LANES), f32),
        XN=((tokens, width), bf16),
        NT=((width, tokens), bf16),
        CT=((width, tokens), bf16),
        INV=((tokens, LANES), f32),
        INM=((tokens, LANES), f32),
        GA=((8, width), f32),
        NG=((8, w), f32),
        CW=((8, cw), f32),
        EM=((LANES, w), bf16),
        CI=((8 + tokens, cw), f32),
        PRE=((tokens, cw), f32),
        DT=((tokens, LANES), f32),
        CAR=((groups, STATE, w), f32),
        RUN=((STATE, w), f32),
        SSD=((tokens, w), f32),
        GR=((tokens, w), f32),
        GT=((tokens, w), f32),
        MG=((tokens, w), f32),
        ST=((8, tokens), f32),
        EX=((seq - 1, 8, tokens), f32),
        SC=((8, tokens), f32),
        EC=((seq - 1, 8, tokens), f32),
        MX=((tokens, w), bf16),
        PG=((tokens, w), bf16),
        DY=((tokens, w), f32),
        PV=((tokens, w), bf16),
        PS=((tokens, SHARED), bf16),
        DP=((tokens + 8, cw), f32),
        OP=((tokens, width), bf16),
        OB=((seq - 1, length, width), bf16),
        NP=((tokens, width), bf16),
        NB=((seq - 1, length, width), bf16),
        CACC=((8, cw), f32),
        NACC=((8, w), f32),
        HACC=((8, LANES), f32),
        PACC=((8, width), f32),
    )
    for name, columns in (("O", w), ("G", w), ("V", w // 2), ("U", w // 2), ("S", SHARED)):
        size = block // 2 if name == "S" else block
        plan["G" + name] = ((dp * size, columns), bf16)
        for way in "RL":
            plan["Y" + way + name] = ((nz, size, columns), bf16)
            plan["A" + way + name] = ((nz - 1, size, columns), bf16)
        plan["T" + name] = ((size, columns), bf16)
        plan["F" + name] = ((seq, rows, columns), bf16)
    plan["QS"] = ((dp, block, SHARED), bf16)
    plan["QB"] = ((dp, block // 2, SHARED), bf16)
    plan["SH"] = ((rows, SHARED), bf16)
    plan["SEL"] = ((LANES, LANES), bf16)
    plan["HD"] = ((8, LANES), f32)
    tile = (8, LANES)
    plan["GM"] = ((owners,) + tile, f32)
    for way in "RL":
        plan["Y" + way + "M"] = ((nz, seq) + tile, f32)
        plan["A" + way + "M"] = ((nz - 1, seq) + tile, f32)
    plan["TM"] = ((seq,) + tile, f32)
    plan["FM"] = ((seq, 1) + tile, f32)
    return plan


def fused_kernel(dp, seq, names, sems, *refs):
    x_ref, cot_ref, inw_ref, outw_ref, small_ref, heads_ref = refs[:6]
    block_ref, ingrad_ref, inshare_ref, outshare_ref = refs[6:10]
    small_refs = refs[10:17]
    b = dict(zip(names, refs[17 : 17 + len(names)]))
    send, recv, own = refs[17 + len(names) :]
    site = Site(dp, seq, send, recv, own)
    nz, owners = dp // 2, dp * seq
    length, width = x_ref.shape
    rows = inw_ref.shape[0]
    tokens = seq * length
    groups = tokens // GROUP
    w = INNER // seq
    cw = w + MAPS
    pairs = w // LANES
    block_rows = seq * rows
    s = site.s

    def tok(g):
        return at(g * GROUP, GROUP, GROUP)

    def each_group(body):
        lax.fori_loop(0, groups, lambda g, c: (body(g), c)[1], 0)

    def columns(base):
        return lambda q: inw_ref.at[:, at(base + q * w, w, LANES)]

    sm = Spread(site, b["SM"], 1, lambda q: small_ref)
    wv = Spread(site, b["WV"], rows, columns(INNER))
    ws = Spread(site, b["WS"], rows, lambda q: b["SH"], True)
    wg = Spread(site, b["WG"], rows, columns(0))
    wo = Spread(site, b["WO"], rows, lambda q: outw_ref.at[:, at(q * w, w, LANES)])
    mine = at(s * length, length, length)
    xg = GroupCopy(site, lambda q: x_ref, lambda k: b["XF"].at[mine], True)
    cg = GroupCopy(site, lambda q: cot_ref, lambda k: b["CF"].at[mine], True)
    squares = GroupCopy(site, lambda q: b["ST"], lambda k: b["EX"].at[k - 1], False)
    crosses = GroupCopy(site, lambda q: b["SC"], lambda k: b["EC"].at[k - 1], False)
    pair_slot = site.take(1)

    def slices(name):
        return lambda q: b[name].at[at(q * length, length, length)]

    outs = GroupCopy(site, slices("OP"), lambda k: b["OB"].at[k - 1], False)
    grads = GroupCopy(site, slices("NP"), lambda k: b["NB"].at[k - 1], False)
    fo, fg, fv, fu, fs, fm = (
        Fold(
            site,
            b["G" + n],
            1 if n == "M" else rows,
            (b["YR" + n], b["YL" + n]),
            (b["AR" + n], b["AL" + n]),
            b["T" + n],
            b["F" + n],
            n == "S",
        )
        for n in "OGVUSM"
    )
    assert site.used == sems[0] and site.used_own == sems[1]

    b["SH"][:, pl.ds(0, MAPS)] = inw_ref[:, pl.ds(INNER + INNER, MAPS)]
    steps = inw_ref[:, pl.ds(INNER + CONV_CH, HEADS)].astype(f32)
    filler = jnp.zeros((rows, LANES - HEADS), f32)
    b["SH"][:, pl.ds(MAPS, LANES)] = jnp.concatenate((steps, filler), axis=1).astype(bf16)
    site.greet()
    for item in (sm.members, wv.members, ws.members):
        item.start()
    for item in (sm, wv, ws):
        item.begin()
    for item in (wg.members, wo.members):
        item.start()
    heads_here = w // HEAD_DIM
    head = lax.div(iota((LANES, w), 1), HEAD_DIM)
    b["EM"][...] = (iota((LANES, w), 0) == head).astype(f32).astype(bf16)
    lanes = iota((LANES, LANES), 1)
    picked = (iota((LANES, LANES), 0) == lanes + s * heads_here) & (lanes < heads_here)
    b["SEL"][...] = picked.astype(f32).astype(bf16)
    b["HD"][...] = exact(dot, heads_ref[...], b["SEL"][...], 3)
    b["HD"][pl.ds(1, 1), :] = jnp.where(
        iota((1, LANES), 1) < heads_here, -jnp.exp(b["HD"][pl.ds(1, 1), :]), 0.0
    )
    for name in ("CACC", "NACC", "HACC", "PACC"):
        b[name][...] = jnp.zeros_like(b[name])
    b["CI"][pl.ds(0, 8), :] = jnp.zeros((8, cw), f32)
    b["DP"][pl.ds(tokens, 8), :] = jnp.zeros((8, cw), f32)

    def norm_scale(g):
        value = b["XF"][tok(g), :].astype(f32)
        inverse = lax.rsqrt(lanes_sum(value * value) / width + epsilon)
        b["INV"][tok(g), :] = jnp.broadcast_to(inverse, (GROUP, LANES))

    def forward(items, hop):
        for item in items:
            item.forward(hop)

    first = (sm, wv, ws)
    forward(first, 1)
    wg.begin()
    xg.start()
    for hop in range(2, nz):
        forward(first, hop)
        wg.forward(hop - 1)
        if hop == 2:
            wo.begin()
    xg.wait()
    cg.start()
    each_group(norm_scale)
    sm.finish()

    lane = iota((1, width), 1)
    pre_table = lambda: Table(owners, lane, width // owners)
    norm_table = lambda: Table(owners, iota((1, w), 1) + s * w, INNER // owners)

    def conv_table():
        place = iota((1, cw), 1)
        channel = jnp.where(place < w, place + s * w, place - w + INNER)
        return Table(owners, channel, CONV_CH // owners)

    b["GA"][pl.ds(0, 1), :] = pre_table().row(b["SM"][:, 0, :])
    b["NG"][pl.ds(0, 1), :] = norm_table().row(b["SM"][:, 1, :])
    taps = conv_table()
    for k in range(CONV + 1):
        b["CW"][pl.ds(k, 1), :] = taps.row(b["SM"][:, 2 + k, :])

    def flip(source, target):
        def body(g):
            for c in range(0, width, LANES):
                part = b[source][tok(g), pl.ds(c, LANES)].astype(f32)
                b[target][pl.ds(c, LANES), tok(g)] = part.T.astype(bf16)

        each_group(body)

    def normalise(g):
        value = b["XF"][tok(g), :].astype(f32) * b["INV"][tok(g), pl.ds(0, 1)]
        b["XN"][tok(g), :] = (value * b["GA"][pl.ds(0, 1), :]).astype(bf16)

    each_group(normalise)
    flip("XN", "NT")
    wg.forward(nz - 1)
    wo.forward(1)
    wv.finish()
    ws.finish()

    def project(g):
        normed = b["XN"][tok(g), :]
        here = at(g * GROUP + 8, GROUP, 8)
        shared = dot(normed, b["WS"][...])
        b["CI"][here, pl.ds(0, w)] = dot(normed, b["WV"][...])
        b["CI"][here, pl.ds(w, MAPS)] = shared[:, :MAPS]
        b["DT"][tok(g), :] = exact(dot, shared[:, MAPS:], b["SEL"][...], 3)
        window = b["CI"][at(g * GROUP, GROUP + 8, 8), :]
        total = jnp.broadcast_to(b["CW"][pl.ds(CONV, 1), :], (GROUP, cw))
        for k in range(CONV):
            shift = 8 - (CONV - 1) + k
            total = total + b["CW"][pl.ds(k, 1), :] * window[shift : shift + GROUP]
        b["PRE"][tok(g), :] = total

    each_group(project)
    wo.forward(2)

    causal = iota((GROUP, GROUP), 0) >= iota((GROUP, GROUP), 1)
    low_half = iota((1, LANES), 1) < HEAD_DIM

    def expand(value):
        return exact(dot, value, b["EM"][...], 2)

    def per_head(value):
        return exact(dot_nt, value, b["EM"][...], 2)

    def halves(value):
        return jnp.concatenate(
            (jnp.where(low_half, value, 0.0), jnp.where(low_half, 0.0, value)), axis=0
        )

    def front(g):
        pre = b["PRE"][tok(g), :]
        out = pre * sigmoid(pre)
        bias, rate = b["HD"][pl.ds(0, 1), :], b["HD"][pl.ds(1, 1), :]
        raw = b["DT"][tok(g), :] + bias
        step = softplus(raw)
        lower = causal.astype(f32).astype(bf16)
        pieces = split(step * rate, 3)
        cumulative = dot(lower, pieces[2]) + dot(lower, pieces[1]) + dot(lower, pieces[0])
        return out[:, :w], out[:, w : w + STATE], out[:, w + STATE :], raw, step, cumulative

    def decays(cumulative, turned, j, backward):
        column = cumulative[:, j : j + 1]
        row = turned[j : j + 1, :]
        if backward:
            upper = iota((GROUP, GROUP), 0) <= iota((GROUP, GROUP), 1)
            return jnp.exp(jnp.where(upper, row - column, -10000.0))
        return jnp.exp(jnp.where(causal, column - row, -10000.0))

    b["RUN"][...] = jnp.zeros_like(b["RUN"])

    def ssd_forward(g):
        values, in_map, out_map, raw, step, cumulative = front(g)
        turned = cumulative.T
        last = cumulative[GROUP - 1 :, :]
        grown = jnp.exp(cumulative)
        grown_wide = expand(grown)
        carried = b["RUN"][...]
        b["CAR"][g] = carried
        scores = mm_nt(out_map, in_map)
        weighted = values * expand(step)
        skip = exact(dot, b["HD"][...], b["EM"][...], 3)[2:3, :]
        rest = mm(out_map, carried) * grown_wide + skip * values
        for p in range(pairs):
            part = slice(p * LANES, (p + 1) * LANES)
            mixing = jnp.concatenate(
                [scores * decays(cumulative, turned, 2 * p + i, False) for i in range(2)], axis=1
            )
            inner = mm(mixing, halves(weighted[:, part]))
            b["SSD"][tok(g), part] = inner + rest[:, part]
        ends = expand(jnp.exp(last - cumulative) * step)
        state = mm(in_map.T, values * ends)
        b["RUN"][...] = carried * grown_wide[GROUP - 1 :, :] + state

    def between(lists, g):
        for item, first, hops in lists:
            for i, hop in enumerate(hops):

                @pl.when(g == min(first + i, groups - 1))
                def _(item=item, hop=hop):
                    item.forward(hop)

    def ssd_step(g):
        ssd_forward(g)
        between(((wo, 0, range(3, nz)),), g)

    each_group(ssd_step)
    cg.wait()
    flip("CF", "CT")
    wg.finish()

    norm_gain = lambda: b["NG"][pl.ds(0, 1), :]

    def to_lanes(column):
        return jnp.broadcast_to(column, (GROUP, LANES)).T[:8, :]

    def summed(own, boxes, g):
        total = b[own][:, tok(g)]
        for k in range(seq - 1):
            total = total + b[boxes][k, :, tok(g)]
        return jnp.concatenate([total] * (LANES // 8), axis=0).T[:, 0:1]

    def gate(g):
        raw = dot(b["XN"][tok(g), :], b["WG"][...])
        gated = b["SSD"][tok(g), :] * (raw * sigmoid(raw))
        b["GR"][tok(g), :] = raw
        b["GT"][tok(g), :] = gated
        b["ST"][:, tok(g)] = to_lanes(lanes_sum(gated * gated))

    each_group(gate)
    squares.start()
    squares.wait()

    def mix(g):
        inverse = lax.rsqrt(summed("ST", "EX", g) / INNER + epsilon)
        unit = b["GT"][tok(g), :] * inverse
        b["GT"][tok(g), :] = unit
        b["INM"][tok(g), :] = jnp.broadcast_to(inverse, (GROUP, LANES))
        b["MX"][tok(g), :] = (unit * norm_gain()).astype(bf16)

    each_group(mix)

    def weight_grad(fold, left, right, first=0):
        def block(rows_here):
            columns_here = pl.ds(first, fold.grad.shape[1])
            product = dot(b[left][rows_here], b[right][:, columns_here])
            fold.grad[rows_here] = product.astype(bf16)

        def offset(i):
            farther = nz - (i + 1) // 2
            return farther * (2 * lax.rem(i, 2) - 1)

        def each(i, carry):
            block(fold.block(offset(i)))
            return carry

        block(fold.block(nz))
        fold.begin()
        lax.fori_loop(1, dp, each, 0)

    weight_grad(fo, "CT", "MX")
    wo.finish()

    def gate_grad(g):
        mixed_grad = dot(b["CF"][tok(g), :], b["WO"][...])
        unit = b["GT"][tok(g), :]
        b["NACC"][pl.ds(0, 1), :] += rows_sum(mixed_grad * unit)
        mixed_grad = mixed_grad * norm_gain()
        b["MG"][tok(g), :] = mixed_grad
        b["SC"][:, tok(g)] = to_lanes(lanes_sum(mixed_grad * unit))

    each_group(gate_grad)
    crosses.start()

    def out_product(g):
        b["OP"][tok(g), :] = dot_nt(b["MX"][tok(g), :], b["WO"][...]).astype(bf16)

    each_group(out_product)
    crosses.wait()
    fo.forward(1)

    def gate_back(g):
        cross = summed("SC", "EC", g) / INNER
        inverse = b["INM"][tok(g), pl.ds(0, 1)]
        raw = b["GR"][tok(g), :]
        gated_grad = inverse * (b["MG"][tok(g), :] - b["GT"][tok(g), :] * cross)
        sig = sigmoid(raw)
        b["DY"][tok(g), :] = gated_grad * (raw * sig)
        slope = sig * (1.0 + raw * (1.0 - sig))
        b["PG"][tok(g), :] = (gated_grad * b["SSD"][tok(g), :] * slope).astype(bf16)

    each_group(gate_back)
    weight_grad(fg, "NT", "PG")
    outs.start()

    b["RUN"][...] = jnp.zeros_like(b["RUN"])

    def ssd_backward(g):
        values, in_map, out_map, raw, step, cumulative = front(g)
        turned = cumulative.T
        last = cumulative[GROUP - 1 :, :]
        grown_wide = expand(jnp.exp(cumulative))
        step_wide = expand(step)
        weighted = values * step_wide
        skip = exact(dot, b["HD"][...], b["EM"][...], 3)[2:3, :]
        out_grad = b["DY"][tok(g), :]
        ssd = b["SSD"][tok(g), :]
        carried, after = b["CAR"][g], b["RUN"][...]
        rate = b["HD"][pl.ds(1, 1), :]

        b["NACC"][pl.ds(1, 1), :] += rows_sum(out_grad * values)
        cumul_grad = per_head(out_grad * (ssd - skip * values))
        grown_grad = out_grad * grown_wide
        ends = jnp.exp(last - cumulative)
        ends_wide = expand(ends * step)
        out_map_grad = mm_nt(grown_grad, carried)
        scaled_grad = mm(in_map, after)
        in_map_grad = mm_nt(values * ends_wide, after)
        ends_grad = per_head(scaled_grad * values)
        step_grad = ends_grad * ends
        ends_cumul = ends_grad * ends * step
        cumul_grad = cumul_grad - ends_cumul
        decay_sum = rows_sum(after * carried)
        decay_grad = per_head(jnp.broadcast_to(decay_sum, (8, w)))[0:1, :] * jnp.exp(last)
        last_grad = rows_sum(ends_cumul) + decay_grad
        b["RUN"][...] = mm(out_map.T, grown_grad) + after * grown_wide[GROUP - 1 :, :]
        scores_turned = mm_nt(in_map, out_map)
        scores_grad = jnp.zeros((GROUP, GROUP), f32)
        value_grads, step_parts = [], []
        for p in range(pairs):
            part = slice(p * LANES, (p + 1) * LANES)
            grads_here = halves(out_grad[:, part])
            mixing = jnp.concatenate(
                [scores_turned * decays(cumulative, turned, 2 * p + i, True) for i in range(2)],
                axis=1,
            )
            inner = mm(mixing, grads_here)
            step_parts.append(inner * values[:, part])
            value_grads.append(inner * step_wide[:, part])
            mixing_grad = mm_nt(grads_here, weighted[:, part])
            for i in range(2):
                scores_grad = scores_grad + (
                    decays(cumulative, turned, 2 * p + i, False)
                    * mixing_grad[i * GROUP : (i + 1) * GROUP]
                )
        inner_step = per_head(jnp.concatenate(step_parts, axis=1))
        step_grad = step_grad + inner_step
        cumul_grad = cumul_grad - inner_step * step
        values_grad = (
            jnp.concatenate(value_grads, axis=1) + scaled_grad * ends_wide + skip * out_grad
        )
        out_map_grad = out_map_grad + mm(scores_grad, in_map)
        in_map_grad = in_map_grad + mm(scores_grad.T, out_map)
        at_last = iota((GROUP, LANES), 0) == GROUP - 1
        cumul_grad = cumul_grad + jnp.where(at_last, last_grad, 0.0)
        upper = (iota((GROUP, GROUP), 0) <= iota((GROUP, GROUP), 1)).astype(f32).astype(bf16)
        pieces = split(cumul_grad, 3)
        rated_grad = dot(upper, pieces[2]) + dot(upper, pieces[1]) + dot(upper, pieces[0])
        step_grad = step_grad + rated_grad * rate
        b["HACC"][pl.ds(1, 1), :] += rows_sum(rated_grad * step * rate)
        raw_grad = step_grad * sigmoid(raw)
        b["HACC"][pl.ds(0, 1), :] += rows_sum(raw_grad)
        pre = b["PRE"][tok(g), :]
        sig = sigmoid(pre)
        conv_grad = jnp.concatenate((values_grad, in_map_grad, out_map_grad), axis=1)
        pre_grad = conv_grad * (sig * (1.0 + pre * (1.0 - sig)))
        b["DP"][tok(g), :] = pre_grad
        before = b["CI"][at(g * GROUP, GROUP + 8, 8), :]
        following = jnp.concatenate((pre_grad, b["DP"][at(g * GROUP + GROUP, 8, 8), :]), axis=0)
        total = None
        for k in range(CONV):
            shift = 8 - (CONV - 1) + k
            b["CACC"][pl.ds(k, 1), :] += rows_sum(pre_grad * before[shift : shift + GROUP])
            back = CONV - 1 - k
            term = b["CW"][pl.ds(k, 1), :] * following[back : back + GROUP]
            total = term if total is None else total + term
        b["CACC"][pl.ds(CONV, 1), :] += rows_sum(pre_grad)
        b["PV"][tok(g), :] = total[:, :w].astype(bf16)
        b["PS"][tok(g), :] = jnp.concatenate(
            (total[:, w:], exact(dot_nt, raw_grad, b["SEL"][...], 2)), axis=1
        ).astype(bf16)

    def ssd_back_step(g):
        ssd_backward(groups - 1 - g)
        between(((fo, 0, range(2, nz)), (fg, 0, range(1, nz))), g)

    each_group(ssd_back_step)

    weight_grad(fv, "NT", "PV")
    weight_grad(fu, "NT", "PV", w // 2)
    block = block_rows // 2

    def shared_block(d, carry):
        left = b["NT"][at(d * block_rows, block_rows, block_rows)]
        b["QS"][d] = dot(left, b["PS"][...]).astype(bf16)
        return carry

    lax.fori_loop(0, dp, shared_block, 0)
    mine_half = lax.rem(s, 2) * block
    pair = site.copy(
        b["QS"].at[:, at(block - mine_half, block, block)], b["QB"], pair_slot, site.twin()
    )
    pair.start()

    fo.finish()
    fg.finish()

    def normed_grad(g):
        total = (
            dot_nt(b["PV"][tok(g), :], b["WV"][...])
            + dot_nt(b["PG"][tok(g), :], b["WG"][...])
            + dot_nt(b["PS"][tok(g), :], b["WS"][...])
        )
        b["NP"][tok(g), :] = total.astype(bf16)
        unit = b["XF"][tok(g), :].astype(f32) * b["INV"][tok(g), pl.ds(0, 1)]
        b["PACC"][pl.ds(0, 1), :] += rows_sum(total * unit)

    each_group(normed_grad)
    grads.start()
    pair.wait_recv()

    def add_twin(d, carry):
        both = b["QS"][d, at(mine_half, block, block)].astype(f32) + b["QB"][d].astype(f32)
        b["GS"][at(d * block, block, block)] = both.astype(bf16)
        return carry

    lax.fori_loop(0, dp, add_twin, 0)
    fs.begin()
    b["GM"][:, 0, :] = pre_table().blocks(b["PACC"][pl.ds(0, 1), :])
    b["GM"][:, 1, :] = norm_table().blocks(b["NACC"][pl.ds(0, 1), :])
    taps = conv_table()
    for k in range(CONV + 1):
        b["GM"][:, 2 + k, :] = taps.blocks(b["CACC"][pl.ds(k, 1), :])
    skip_grad = per_head(jnp.broadcast_to(b["NACC"][pl.ds(1, 1), :], (8, w)))
    total = jnp.zeros((8, LANES), f32)
    kinds = (b["HACC"][pl.ds(0, 1), :], b["HACC"][pl.ds(1, 1), :], skip_grad[0:1, :])
    for i, row in enumerate(kinds):
        place = iota((LANES, LANES), 1) - s * heads_here - i * HEADS
        source = iota((LANES, LANES), 0)
        move = ((place == source) & (source < heads_here)).astype(f32).astype(bf16)
        total = total + exact(dot, jnp.broadcast_to(row, (8, LANES)), move, 3)
    b["GM"][:, 7, :] = jnp.broadcast_to(total[0:1, :], (owners, LANES))
    fm.begin()
    for hop in range(1, nz):
        forward((fv, fu, fs, fm), hop)
    outs.wait()
    total = x_ref[...].astype(f32) + b["OP"][mine, :].astype(f32)
    for k in range(seq - 1):
        total = total + b["OB"][k].astype(f32)
    block_ref[...] = total.astype(bf16)
    grads.wait()
    total = b["NP"][mine, :].astype(f32)
    for k in range(seq - 1):
        total = total + b["NB"][k].astype(f32)
    scaled = total * b["GA"][pl.ds(0, 1), :]
    inverse = b["INV"][mine, pl.ds(0, 1)]
    unit = x_ref[...].astype(f32) * inverse
    mean = lanes_sum(scaled * unit) / width
    ingrad_ref[...] = inverse * (scaled - unit * mean) + cot_ref[...].astype(f32)
    for item in (fv, fu, fs, fm):
        item.finish()
    for item in (fo, fg, fv, fu, fs, fm):
        item.members.wait()
    smalls, shared = b["FM"][0], None
    for q in range(seq):
        outshare_ref[:, pl.ds(q * w, w)] = b["FO"][q].astype(f32)
        inshare_ref[:, pl.ds(q * w, w)] = b["FG"][q].astype(f32)
        inshare_ref[:, pl.ds(INNER + q * w, w // 2)] = b["FV"][q].astype(f32)
        inshare_ref[:, pl.ds(INNER + q * w + w // 2, w // 2)] = b["FU"][q].astype(f32)
        if q > 0:
            smalls = smalls + b["FM"][q]
    for j in range(seq // 2):
        part = b["FS"][2 * j + s // (seq // 2)].astype(f32)
        shared = part if shared is None else shared + part
    inshare_ref[:, pl.ds(INNER + INNER, MAPS + HEADS)] = shared[:, : MAPS + HEADS]
    smalls = smalls[0]
    starts = ((0, 0), (1, 0), (2, 0), (6, 0), (7, 0), (7, HEADS), (7, 2 * HEADS))
    for ref, (top, left) in zip(small_refs, starts):
        ref[...] = smalls[top : top + ref.shape[0], left : left + ref.shape[1]]
    for drain in site.pending:
        drain()
    pair.wait_send()


def fused(x, cot, in_weight, out_weight, small, heads, dp, seq):
    length, width = x.shape
    rows, proj = in_weight.shape
    owners = dp * seq
    plan = scratch_plan(dp, seq, length, width, rows)
    names = tuple(plan)
    sems = (11 * (seq - 1 + dp) + 6 * (seq - 1) + dp + 1, 7)
    vmem = pl.BlockSpec(memory_space=pltpu.VMEM)
    return pl.pallas_call(
        functools.partial(fused_kernel, dp, seq, names, sems),
        out_shape=[
            jax.ShapeDtypeStruct((length, width), bf16),
            jax.ShapeDtypeStruct((length, width), f32),
            jax.ShapeDtypeStruct((rows, proj), f32),
            jax.ShapeDtypeStruct((rows, INNER), f32),
        ]
        + [
            jax.ShapeDtypeStruct(shape, f32)
            for shape in (
                (1, width // owners),
                (1, INNER // owners),
                (CONV, CONV_CH // owners),
                (1, CONV_CH // owners),
                (1, HEADS),
                (1, HEADS),
                (1, HEADS),
            )
        ],
        in_specs=[vmem] * 6,
        out_specs=[vmem] * 11,
        scratch_shapes=[pltpu.VMEM(*plan[name]) for name in names]
        + [
            pltpu.SemaphoreType.DMA((sems[0],)),
            pltpu.SemaphoreType.DMA((sems[0],)),
            pltpu.SemaphoreType.DMA((sems[1],)),
        ],
        compiler_params=pltpu.CompilerParams(
            collective_id=0, has_side_effects=True, vmem_limit_bytes=58 * 2**20
        ),
    )(x, cot, in_weight, out_weight, small, heads)


def place_kernel(count, *refs):
    copies = [
        pltpu.make_async_copy(refs[i], refs[count + i], refs[2 * count].at[i])
        for i in range(count)
    ]
    for copy in copies:
        copy.start()
    for copy in copies:
        copy.wait()


def placed(values):
    count = len(values)
    return pl.pallas_call(
        functools.partial(place_kernel, count),
        out_shape=[jax.ShapeDtypeStruct(value.shape, value.dtype) for value in values],
        in_specs=[pl.BlockSpec(memory_space=pltpu.VMEM)] * count,
        out_specs=[pl.BlockSpec(memory_space=pl.ANY)] * count,
        scratch_shapes=[pltpu.SemaphoreType.DMA((count,))],
    )(*values)


def fits(dp, seq, block_input, in_weight):
    seq_dev, length, width = block_input.shape
    rows = in_weight.shape[0]
    owners = dp * seq
    return (
        seq_dev == 1
        and dp % 2 == 0
        and dp >= 4
        and seq % 2 == 0
        and length % GROUP == 0
        and rows % 32 == 0
        and rows <= LANES
        and INNER % (seq * 2 * LANES) == 0
        and INNER % owners == 0
        and CONV_CH % owners == 0
        and CONV_CH // owners <= LANES
        and dp // 2 <= seq * length // GROUP + 1
    )


def spread_rows(values):
    total, first = None, 0
    for value in values:
        value = value.reshape(-1, value.shape[-1]).astype(f32)
        count, size = value.shape
        value = jnp.pad(value, ((first, 8 - first - count), (0, LANES - size)))
        total = value if total is None else total + value
        first += count
    return total


def on_device_fused(
    block_input,
    in_weight,
    out_weight,
    pre_gain,
    norm_gain,
    conv_weight,
    conv_bias,
    dt_bias,
    decay_log,
    skip_gain,
    cotangent,
):
    dp, seq = lax.axis_size("dp"), lax.axis_size("seq")
    small = spread_rows((pre_gain, norm_gain, conv_weight, conv_bias))[None]
    heads = spread_rows((dt_bias, decay_log, skip_gain))
    results = fused(
        block_input[0], cotangent[0], in_weight, out_weight.T, small, heads, dp, seq
    )
    block, in_grad, in_share, out_share, *smalls = placed(results)
    taps = smalls.pop(2)
    pre, norm, bias, dt, decay, skip = (value.reshape(-1) for value in smalls)
    return (
        block[None],
        in_grad[None],
        in_share,
        out_share.T,
        pre,
        norm,
        taps,
        bias,
        dt,
        decay,
        skip,
    )


def from_behind(value, axis, steps):
    count = lax.axis_size(axis)
    leading, last = (max(0, -steps), min(count, count - steps))
    return lax.ppermute(value, axis, [(source, source + steps) for source in range(leading, last)])


def convolve(padded, conv_weight, conv_bias):
    taps = conv_weight.shape[0]
    length = padded.shape[-2] - taps + 1
    total = conv_bias
    for index in range(taps):
        total = total + conv_weight[index] * lax.slice_in_dim(
            padded, index, index + length, axis=padded.ndim - 2
        )
    return total


def running_sum(value):
    length = value.shape[1]
    lower = (jnp.arange(length)[:, None] >= jnp.arange(length)[None, :]).astype(value.dtype)
    return jnp.einsum("ts,bsh->bth", lower, value, precision=lax.Precision.HIGHEST)


def carry_scan(state, decay, axis, sign):
    count = lax.axis_size(axis)
    within, within_decay = state, decay
    entering, entering_decay = None, None
    width = 1
    while width < count:
        moved = from_behind(within.astype(jnp.bfloat16), axis, sign * width).astype(jnp.float32)
        last = 2 * width >= count
        if not last or entering is None:
            moved_decay = from_behind(within_decay, axis, sign * width)
        if entering is None:
            entering, entering_decay = moved, moved_decay
        else:
            entering = entering + entering_decay[:, :, None, None] * moved
            if not last:
                entering_decay = entering_decay * moved_decay
        if not last:
            within = within + within_decay[:, :, None, None] * moved
            within_decay = within_decay * moved_decay
        width *= 2
    return jnp.zeros_like(state) if entering is None else entering


def front_fn(tail, rim, conv_weight, conv_bias, dt_bias, decay_log):
    conv_in = tail[..., :CONV_CH]
    dt_raw = tail[..., CONV_CH:]
    padded = jnp.concatenate([rim, conv_in], axis=-2)
    conv_out = jax.nn.silu(convolve(padded, conv_weight, conv_bias))
    leading = conv_out.shape[:-1]
    values = conv_out[..., :INNER].reshape(leading + (HEADS, HEAD_DIM))
    in_map = conv_out[..., INNER : INNER + STATE]
    out_map = conv_out[..., INNER + STATE :]
    step = jax.nn.softplus(dt_raw + dt_bias)
    cumulative = running_sum(step * -jnp.exp(decay_log))
    return (values, in_map, out_map, step, cumulative)


def group_state(values, in_map, step, cumulative):
    weights_end = jnp.exp(cumulative[-1][None, :] - cumulative) * step
    state = jnp.einsum("shp,sn->hpn", values * weights_end[:, :, None], in_map, precision=highest)
    return (state, jnp.exp(cumulative[-1]))


def group_output(values, in_map, out_map, step, cumulative, carried, skip_gain):
    length = values.shape[0]
    scores = jnp.dot(out_map, in_map.T, precision=highest)
    causal = jnp.arange(length)[:, None] >= jnp.arange(length)[None, :]
    spread = cumulative[:, None, :] - cumulative[None, :, :]
    decay = jnp.exp(jnp.where(causal[:, :, None], spread, -10000.0))
    mixing = scores[:, :, None] * decay * step[None, :, :]
    inner_part = jnp.einsum("tsh,shp->thp", mixing, values, precision=highest)
    carried_part = (
        jnp.einsum("tn,hpn->thp", out_map, carried, precision=highest)
        * jnp.exp(cumulative)[:, :, None]
    )
    return inner_part + carried_part + skip_gain[None, :, None] * values


def state_fn(values, in_map, step, cumulative):
    return jax.vmap(group_state)(values, in_map, step, cumulative)


def out_fn(values, in_map, out_map, step, cumulative, gate_raw, carried, skip_gain, norm_gain):
    ssd_out = jax.vmap(group_output, in_axes=(0, 0, 0, 0, 0, 0, None))(
        values, in_map, out_map, step, cumulative, carried, skip_gain
    )
    ssd_out = ssd_out.reshape(gate_raw.shape)
    gated = ssd_out * jax.nn.silu(gate_raw)
    inverse = lax.rsqrt(jnp.mean(gated * gated, axis=-1, keepdims=True) + epsilon)
    return gated * inverse * norm_gain


def by_rows(grad, owners):
    return grad.reshape(owners, -1)


def by_columns(grad, owners):
    rows = grad.shape[0]
    return jnp.transpose(grad.reshape(rows, owners, -1), (1, 0, 2)).reshape(owners, -1)


def on_device(
    block_input,
    in_weight,
    out_weight,
    pre_gain,
    norm_gain,
    conv_weight,
    conv_bias,
    dt_bias,
    decay_log,
    skip_gain,
    cotangent,
):
    seq_dev, length, width = block_input.shape
    dp, seq = lax.axis_size("dp"), lax.axis_size("seq")
    owners = dp * seq
    both = ("dp", "seq")
    if fits(dp, seq, block_input, in_weight):
        return on_device_fused(
            block_input,
            in_weight,
            out_weight,
            pre_gain,
            norm_gain,
            conv_weight,
            conv_bias,
            dt_bias,
            decay_log,
            skip_gain,
            cotangent,
        )
    small_parts = (pre_gain, norm_gain, conv_weight.reshape(-1), conv_bias)
    small_sizes = [part.size for part in small_parts]
    small = jnp.concatenate(small_parts)
    in_full = lax.all_gather(in_weight, both, axis=0, tiled=True)
    gate_w, tail_w = in_full[:, :INNER], in_full[:, INNER:]
    out_t = lax.all_gather(out_weight.T, both, axis=0, tiled=True)
    small_all = lax.all_gather(small, both, axis=0)
    pieces, start = [], 0
    for size in small_sizes:
        pieces.append(small_all[:, start : start + size])
        start += size
    pre_full, norm_full, conv_b_full = (pieces[i].reshape(-1) for i in (0, 1, 3))
    conv_w_full = jnp.transpose(pieces[2].reshape(owners, CONV, -1), (1, 0, 2)).reshape(CONV, -1)
    pre_float = pre_full.astype(jnp.float32)
    norm_float = norm_full.astype(jnp.float32)
    inputs = block_input.astype(jnp.float32)
    inv_pre = lax.rsqrt(jnp.mean(inputs * inputs, axis=-1, keepdims=True) + epsilon)
    normed = (inputs * inv_pre * pre_float).astype(jnp.bfloat16)
    flat_normed = normed.reshape(seq_dev * length, width)
    gate_raw = jnp.dot(flat_normed, gate_w, preferred_element_type=jnp.float32).reshape(
        seq_dev, length, -1
    )
    tail = jnp.dot(flat_normed, tail_w, preferred_element_type=jnp.float32).reshape(
        seq_dev, length, -1
    )
    conv_in = tail[:, length - (CONV - 1) :, :CONV_CH]
    rim = from_behind(conv_in, "seq", 1)
    front_out, front_pull = jax.vjp(
        front_fn,
        tail,
        rim,
        conv_w_full.astype(jnp.float32),
        conv_b_full.astype(jnp.float32),
        dt_bias,
        decay_log,
    )
    values, in_map, out_map, step, cumulative = front_out
    state_out, state_pull = jax.vjp(state_fn, values, in_map, step, cumulative)
    state, decay = state_out
    carried = carry_scan(state, decay, "seq", 1)
    mixed_float, out_pull = jax.vjp(
        out_fn, values, in_map, out_map, step, cumulative, gate_raw, carried, skip_gain, norm_float
    )
    mixed = mixed_float.astype(jnp.bfloat16)
    flat_mixed = mixed.reshape(seq_dev * length, INNER)
    block_output = (
        inputs
        + jnp.dot(flat_mixed, out_t.T, preferred_element_type=jnp.float32).reshape(
            seq_dev, length, width
        )
    ).astype(jnp.bfloat16)
    flat_grad = cotangent.reshape(seq_dev * length, width)
    mixed_grad = jnp.dot(flat_grad, out_t, preferred_element_type=jnp.float32).reshape(
        seq_dev, length, INNER
    )
    out_w_grad = jnp.dot(flat_grad.T, flat_mixed, preferred_element_type=jnp.float32)
    (
        values_a,
        in_map_a,
        out_map_grad,
        step_a,
        cumul_a,
        gate_grad,
        local_grad,
        skip_grad,
        norm_grad,
    ) = out_pull(mixed_grad)

    later_grad = carry_scan(local_grad, decay, "seq", -1)
    decay_grad = jnp.sum(later_grad * carried, axis=(2, 3))
    values_b, in_map_b, step_b, cumul_b = state_pull((later_grad, decay_grad))
    front_grads = front_pull(
        (
            values_a + values_b,
            in_map_a + in_map_b,
            out_map_grad,
            step_a + step_b,
            cumul_a + cumul_b,
        )
    )
    tail_float, rim_grad, conv_w_grad, conv_b_grad, dt_grad, decay_log_grad = front_grads
    returned = from_behind(rim_grad, "seq", -1)
    tail_float = tail_float + jnp.pad(returned, ((0, 0), (length - (CONV - 1), 0), (0, HEADS)))
    tail_grad = tail_float.astype(jnp.bfloat16).reshape(seq_dev * length, -1)
    gate_grad = gate_grad.astype(jnp.bfloat16).reshape(seq_dev * length, -1)
    gate_w_grad = jnp.dot(flat_normed.T, gate_grad, preferred_element_type=jnp.float32)
    tail_w_grad = jnp.dot(flat_normed.T, tail_grad, preferred_element_type=jnp.float32)
    normed_grad = (
        jnp.dot(gate_grad, gate_w.T, preferred_element_type=jnp.float32)
        + jnp.dot(tail_grad, tail_w.T, preferred_element_type=jnp.float32)
    ).reshape(seq_dev, length, width)
    pre_grad = jnp.sum(normed_grad * inputs * inv_pre, axis=(0, 1))
    scaled = normed_grad * pre_float
    unit = inputs * inv_pre
    input_grad = inv_pre * (
        scaled - unit * jnp.mean(scaled * unit, axis=-1, keepdims=True)
    ) + cotangent.astype(jnp.float32)
    small_grads = jnp.concatenate(
        (
            by_rows(pre_grad, owners),
            by_rows(norm_grad, owners),
            by_columns(conv_w_grad, owners),
            by_rows(conv_b_grad, owners),
        ),
        axis=1,
    )
    heads = jnp.concatenate((dt_grad, decay_log_grad, skip_grad))
    scatter = functools.partial(
        lax.psum_scatter, axis_name=both, scatter_dimension=0, tiled=True
    )
    in_share = scatter(jnp.concatenate((gate_w_grad, tail_w_grad), axis=1))
    out_share = scatter(out_w_grad).T
    small_share = scatter(small_grads)[0]
    heads = lax.psum(heads, both)
    shares, start = [], 0
    for size in small_sizes:
        shares.append(small_share[start : start + size])
        start += size
    pre_share, norm_share, conv_w_share, conv_b_share = shares
    conv_w_share = conv_w_share.reshape(CONV, -1)
    heads_total = (heads[:HEADS], heads[HEADS : 2 * HEADS], heads[2 * HEADS :])
    return (
        block_output,
        input_grad,
        in_share,
        out_share,
        pre_share,
        norm_share,
        conv_w_share,
        conv_b_share,
        heads_total[0],
        heads_total[1],
        heads_total[2],
    )


def solution(mesh):
    in_specs = (
        P("dp", "seq", None),
        P(("dp", "seq"), None),
        P(None, ("dp", "seq")),
        P(("dp", "seq")),
        P(("dp", "seq")),
        P(None, ("dp", "seq")),
        P(("dp", "seq")),
        P(),
        P(),
        P(),
        P("dp", "seq", None),
    )
    out_specs = (
        P("dp", "seq", None),
        P("dp", "seq", None),
        P(("dp", "seq"), None),
        P(None, ("dp", "seq")),
        P(("dp", "seq")),
        P(("dp", "seq")),
        P(None, ("dp", "seq")),
        P(("dp", "seq")),
        P(),
        P(),
        P(),
    )
    return jax.shard_map(
        on_device, mesh=mesh, in_specs=in_specs, out_specs=out_specs, check_vma=False
    )
```

```python
import functools

import jax
import jax.numpy as jnp
from jax import lax
from jax.experimental import pallas as pl
from jax.experimental.pallas import tpu as pltpu
from jax.sharding import PartitionSpec as P

HEADS = 32
HEAD_DIM = 64
STATE = 128
CONV = 4
GROUP = 128
INNER = 2048
CONV_CH = 2304
LANES = 128
MAPS = CONV_CH - INNER
SHARED = MAPS + LANES
RING_HOPS = 4


epsilon = 1e-05
highest = lax.Precision.HIGH
bf16 = jnp.bfloat16
f32 = jnp.float32


def at(start, size, multiple):
    return pl.ds(start if isinstance(start, int) else pl.multiple_of(start, multiple), size)


def remote(src, dst, send, recv, device):
    return pltpu.make_async_remote_copy(
        src_ref=src,
        dst_ref=dst,
        send_sem=send,
        recv_sem=recv,
        device_id=device,
        device_id_type=pl.DeviceIdType.MESH,
    )


class Site:
    def __init__(self, dp, seq, send, recv, own):
        self.nz, self.ns = dp // 2, seq
        self.d, self.s = lax.axis_index("dp"), lax.axis_index("seq")
        far, level = lax.rem(self.d, 2), self.d // 2
        self.dp, self.half = dp, dp // 2
        self.place = level + far * (dp - 1 - 2 * level)
        self.owner = self.d * seq + self.s
        self.send, self.recv, self.own = send, recv, own
        self.used, self.used_own = 0, 0
        self.pending = []

    def group(self, k):
        return (self.d, lax.rem(self.s + k, self.ns))

    def ring(self, offset):
        place = lax.rem(self.place + offset + 2 * self.dp, self.dp)
        far = place // self.nz
        level = place + far * (self.dp - 1 - 2 * place)
        return level * 2 + far

    def beside(self, way):
        return (self.ring(way), self.s)

    def twin(self):
        return (self.d, self.s + 1 - 2 * lax.rem(self.s, 2))

    def take(self, count):
        self.used += count
        return self.used - count

    def copy(self, src, dst, slot, device):
        return remote(src, dst, self.send.at[slot], self.recv.at[slot], device)

    def greet(self):
        barrier = pltpu.get_barrier_semaphore()
        partners = [self.group(k) for k in range(1, self.ns)]
        partners += [(lax.rem(self.d + k, self.dp), self.s) for k in range(1, self.dp)]
        for partner in partners:
            pl.semaphore_signal(
                barrier, inc=1, device_id=partner, device_id_type=pl.DeviceIdType.MESH
            )
        pl.semaphore_wait(barrier, len(partners))


class GroupCopy:
    def __init__(self, site, source, dest, local, wanted=None):
        self.site, self.source, self.dest, self.local = site, source, dest, local
        self.wanted = wanted
        self.base = site.take(site.ns - 1)
        if local:
            self.own = site.used_own
            site.used_own += 1
        site.pending.append(self.drain)

    def own_copy(self):
        site = self.site
        return pltpu.make_async_copy(self.source(site.s), self.dest(0), site.own.at[self.own])

    def copy(self, k):
        site = self.site
        member = lax.rem(site.s + k, site.ns)
        return site.copy(self.source(member), self.dest(k), self.base + k - 1, site.group(k))

    def each(self, act, sending):
        site = self.site
        for k in range(1, site.ns):
            if self.wanted is None:
                act(k)
                continue
            other = lax.rem(site.s + (k if sending else site.ns - k), site.ns)
            ends = (site.s, other) if sending else (other, site.s)
            pl.when(self.wanted(*ends))(functools.partial(act, k))

    def start(self):
        self.each(lambda k: self.copy(k).start(), True)
        if self.local:
            self.own_copy().start()

    def wait(self):
        if self.local:
            self.own_copy().wait()
        self.each(lambda k: self.copy(k).wait_recv(), False)

    def drain(self):
        self.each(lambda k: self.copy(k).wait_send(), True)


class Spread:
    def __init__(self, site, buf, rows, source, twins=False):
        self.site, self.buf, self.rows, self.source = site, buf, rows, source
        self.block_rows, self.twins = site.ns * rows, twins
        self.members = GroupCopy(
            site, source, lambda k: buf.at[at(site.owner * rows, rows, rows)], True
        )
        self.base = {way: site.take(site.half) for way in (1, -1)}
        self.twin_base = {way: site.take(site.half) for way in (1, -1)} if twins else None
        site.pending.append(self.drain)

    def block(self, way, offset, halved):
        size = self.block_rows
        start = self.site.ring(offset) * size
        if self.twins:
            size = size // 2
            start = start + lax.rem(self.site.s, 2) * size
        if halved:
            size = size // 2
            start = start if way > 0 else start + size
        return self.buf.at[at(start, size, size)]

    def copy(self, way, hop):
        site = self.site
        block = self.block(way, way * (1 - hop), hop == site.half)
        return site.copy(block, block, self.base[way] + hop - 1, site.beside(way))

    def twin_copy(self, way, hop):
        site = self.site
        block = self.block(way, -way * hop, hop == site.half)
        return site.copy(block, block, self.twin_base[way] + hop - 1, site.twin())

    def begin(self):
        self.members.wait()
        for way in (1, -1):
            self.copy(way, 1).start()

    def forward(self, hop):
        for way in (1, -1):
            self.copy(way, hop).wait_recv()
            self.copy(way, hop + 1).start()
            if self.twins:
                self.twin_copy(way, hop).start()

    def finish(self):
        last = self.site.half
        for way in (1, -1):
            self.copy(way, last).wait_recv()
            if self.twins:
                self.twin_copy(way, last).start()
        if self.twins:
            for way in (1, -1):
                for hop in range(1, last + 1):
                    self.twin_copy(way, hop).wait_recv()

    def drain(self):
        for way in (1, -1):
            for hop in range(1, self.site.half + 1):
                self.copy(way, hop).wait_send()
                if self.twins:
                    self.twin_copy(way, hop).wait_send()


class Fold:
    def __init__(self, site, grad, rows, boxes, sums, total, final, twins=False):
        self.site, self.grad, self.rows, self.twins = site, grad, rows, twins
        self.members_in = site.ns // 2 if twins else site.ns
        self.block_rows = self.members_in * rows
        self.boxes, self.sums = dict(zip((1, -1), boxes)), dict(zip((1, -1), sums))
        self.total, self.final = total, final
        self.base = {way: site.take(site.half) for way in (1, -1)}
        self.members = GroupCopy(
            site,
            lambda q: total.at[self.rows_for(q)],
            lambda k: final.at[site.s],
            False,
            (lambda a, q: lax.rem(a, 2) == q // self.members_in) if twins else None,
        )
        site.pending.append(self.drain)

    def rows_for(self, q):
        return at(lax.rem(q, self.members_in) * self.rows, self.rows, self.rows)

    def block(self, offset):
        return at(self.site.ring(offset) * self.block_rows, self.block_rows, self.block_rows)

    def copy(self, way, hop):
        site, size = self.site, self.block_rows // 2
        if hop == 1:
            shift = 0 if way > 0 else size
            source = self.grad.at[at(site.ring(way * site.half) * 2 * size + shift, size, size)]
            dest = self.boxes[way].at[0, pl.ds(shift, size)]
        else:
            source, dest = self.sums[way].at[hop - 2], self.boxes[way].at[hop - 1]
        return site.copy(source, dest, self.base[way] + hop - 1, site.beside(way))

    def begin(self):
        for way in (1, -1):
            self.copy(way, 1).start()

    def forward(self, hop):
        site, size = self.site, self.block_rows // 2
        for way in (1, -1):
            self.copy(way, hop).wait_recv()
            kept = self.grad[self.block(way * (site.half - hop))]
            box, sums = self.boxes[way], self.sums[way]
            if hop == 1:
                near, far = (slice(0, size), slice(size, None))[::way]
                both = kept[near].astype(f32) + box[0, near].astype(f32)
                sums[0, near] = both.astype(sums.dtype)
                sums[0, far] = kept[far]
            else:
                both = kept.astype(f32) + box[hop - 1].astype(f32)
                sums[hop - 1] = both.astype(sums.dtype)
            self.copy(way, hop + 1).start()

    def finish(self):
        site = self.site
        total = self.grad[self.block(0)].astype(f32)
        for way in (1, -1):
            self.copy(way, site.half).wait_recv()
            total = total + self.boxes[way][site.half - 1].astype(f32)
        self.total[...] = total.astype(self.total.dtype)
        self.members.start()
        self.final[site.s] = self.total[self.rows_for(site.s)]

    def drain(self):
        for way in (1, -1):
            for hop in range(1, self.site.half + 1):
                self.copy(way, hop).wait_send()


class Exchange:
    def __init__(self, site, table, boxes, total, final):
        self.site, self.table, self.boxes, self.total = site, table, boxes, total
        self.base = site.take(site.dp - 1)
        self.members = GroupCopy(
            site, lambda q: total.at[pl.ds(q, 1)], lambda k: final.at[site.s], False
        )
        self.final = final
        site.pending.append(self.drain)

    def copy(self, k):
        site = self.site
        other = lax.rem(site.d + k, site.dp)
        block = self.table.at[at(other * site.ns, site.ns, site.ns)]
        return site.copy(block, self.boxes.at[k - 1], self.base + k - 1, (other, site.s))

    def begin(self):
        for k in range(1, self.site.dp):
            self.copy(k).start()

    def finish(self):
        site = self.site
        total = self.table[at(site.d * site.ns, site.ns, site.ns)]
        for k in range(1, site.dp):
            self.copy(k).wait_recv()
            total = total + self.boxes[k - 1]
        self.total[...] = total
        self.members.start()
        self.final[site.s] = self.total[pl.ds(site.s, 1)]

    def drain(self):
        for k in range(1, self.site.dp):
            self.copy(k).wait_send()


def dot(a, b):
    return jnp.dot(a, b, preferred_element_type=f32)


def dot_nt(a, b):
    return lax.dot_general(a, b, (((1,), (1,)), ((), ())), preferred_element_type=f32)


def split(value, parts):
    pieces = []
    for _ in range(parts - 1):
        pieces.append(value.astype(bf16))
        value = value - pieces[-1].astype(f32)
    return pieces + [value.astype(bf16)]


def exact(product, value, onehot, parts):
    total = None
    for piece in split(value, parts)[::-1]:
        term = product(piece, onehot)
        total = term if total is None else total + term
    return total


def wide(product, a, b, passes):
    if passes == 1:
        return product(a.astype(bf16), b.astype(bf16))
    (a_hi, a_lo), (b_hi, b_lo) = split(a, 2), split(b, 2)
    total = product(a_hi, b_lo)
    if passes == 3:
        total = total + product(a_lo, b_hi)
    return total + product(a_hi, b_hi)


def mm(a, b, passes=3):
    return wide(dot, a, b, passes)


def mm_nt(a, b, passes=3):
    return wide(dot_nt, a, b, passes)


def iota(shape, axis):
    return lax.broadcasted_iota(jnp.int32, shape, axis)


def sigmoid(value):
    return 1.0 / (1.0 + jnp.exp(-value))


def softplus(value):
    small = jnp.exp(-jnp.abs(value))
    series = small * (1.0 - small * (0.5 - small * (1 / 3 - small * (0.25 - small * 0.2))))
    return jnp.maximum(value, 0.0) + jnp.where(small < 0.03, series, jnp.log(1.0 + small))


def rows_sum(value):
    return jnp.sum(value, axis=0, keepdims=True)


def lanes_sum(value):
    return jnp.sum(value, axis=1, keepdims=True)


class Table:
    def __init__(self, owners, channel, size):
        count = channel.shape[1]
        first = iota((owners, count), 0) * size
        place = channel - first
        self.mask = (place >= 0) & (place < size)
        spot = jnp.sum(jnp.where(self.mask, place.astype(f32), 0.0), axis=0, keepdims=True)
        self.onehot = (iota((LANES, count), 0).astype(f32) == spot).astype(f32).astype(bf16)

    def row(self, blocks):
        return rows_sum(jnp.where(self.mask, dot(blocks.astype(bf16), self.onehot), 0.0))

    def blocks(self, row):
        return exact(dot_nt, jnp.where(self.mask, row, 0.0), self.onehot, 3)


def scratch_plan(dp, seq, length, width, rows):
    nz, owners, tokens = dp // 2, dp * seq, seq * length
    w = INNER // seq
    cw, groups, block = w + MAPS, tokens // GROUP, seq * rows
    plan = dict(
        XF=((tokens, width), bf16),
        CF=((tokens, width), bf16),
        WV=((width, w), bf16),
        WS=((width, SHARED), bf16),
        WG=((width, w), bf16),
        WO=((width, w), bf16),
        SM=((owners, 8, LANES), f32),
        XN=((tokens, width), bf16),
        NT=((width, tokens), bf16),
        CT=((width, tokens), bf16),
        INV=((tokens, LANES), f32),
        INM=((tokens, LANES), f32),
        GA=((8, width), f32),
        NG=((8, w), f32),
        CW=((8, cw), f32),
        EM=((LANES, w), bf16),
        CI=((8 + tokens, cw), f32),
        PRE=((tokens, cw), f32),
        DT=((tokens, LANES), f32),
        CAR=((groups, STATE, w), f32),
        RUN=((STATE, w), f32),
        SSD=((tokens, w), f32),
        GR=((tokens, w), f32),
        GT=((tokens, w), f32),
        MG=((tokens, w), f32),
        ST=((8, tokens), f32),
        EX=((seq - 1, 8, tokens), f32),
        SC=((8, tokens), f32),
        EC=((seq - 1, 8, tokens), f32),
        MX=((tokens, w), bf16),
        PG=((tokens, w), bf16),
        DY=((tokens, w), f32),
        PV=((tokens, w), bf16),
        PS=((tokens, SHARED), bf16),
        DP=((tokens + 8, cw), f32),
        OP=((tokens, width), bf16),
        OB=((seq - 1, length, width), bf16),
        NP=((tokens, width), bf16),
        NB=((seq - 1, length, width), bf16),
        CACC=((8, cw), f32),
        NACC=((8, w), f32),
        HACC=((8, LANES), f32),
        PACC=((8, width), f32),
    )
    for name, columns in (("O", w), ("S", SHARED)) + tuple((n, w // 2) for n in "GHVU"):
        size = block // 2 if name == "S" else block
        plan["G" + name] = ((dp * size, columns), bf16)
        for way in "RL":
            plan["Y" + way + name] = ((nz, size, columns), bf16)
            plan["A" + way + name] = ((nz - 1, size, columns), bf16)
        plan["T" + name] = ((size, columns), bf16)
        plan["F" + name] = ((seq, rows, columns), bf16)
    plan["QS"] = ((dp, block, SHARED), bf16)
    plan["QB"] = ((dp, block // 2, SHARED), bf16)
    plan["SH"] = ((rows, SHARED), bf16)
    plan["SEL"] = ((LANES, LANES), bf16)
    plan["HD"] = ((8, LANES), f32)
    tile = (8, LANES)
    plan["GM"] = ((owners,) + tile, f32)
    plan["YM"] = ((dp - 1, seq) + tile, f32)
    plan["TM"] = ((seq,) + tile, f32)
    plan["FM"] = ((seq, 1) + tile, f32)
    return plan


def fused_kernel(dp, seq, names, sems, *refs):
    x_ref, cot_ref, inw_ref, outw_ref, small_ref, heads_ref = refs[:6]
    block_ref, ingrad_ref, inshare_ref, outshare_ref = refs[6:10]
    small_refs = refs[10:17]
    b = dict(zip(names, refs[17 : 17 + len(names)]))
    send, recv, own = refs[17 + len(names) :]
    site = Site(dp, seq, send, recv, own)
    nz, owners = dp // 2, dp * seq
    length, width = x_ref.shape
    rows = inw_ref.shape[0]
    tokens = seq * length
    groups = tokens // GROUP
    w = INNER // seq
    cw = w + MAPS
    pairs = w // LANES
    block_rows = seq * rows
    s = site.s

    def tok(g):
        return at(g * GROUP, GROUP, GROUP)

    def each_group(body):
        lax.fori_loop(0, groups, lambda g, c: (body(g), c)[1], 0)

    def columns(base):
        return lambda q: inw_ref.at[:, at(base + q * w, w, LANES)]

    sm = Spread(site, b["SM"], 1, lambda q: small_ref)
    wv = Spread(site, b["WV"], rows, columns(INNER))
    ws = Spread(site, b["WS"], rows, lambda q: b["SH"], True)
    wg = Spread(site, b["WG"], rows, columns(0))
    wo = Spread(site, b["WO"], rows, lambda q: outw_ref.at[:, at(q * w, w, LANES)])
    mine = at(s * length, length, length)
    xg = GroupCopy(site, lambda q: x_ref, lambda k: b["XF"].at[mine], True)
    cg = GroupCopy(site, lambda q: cot_ref, lambda k: b["CF"].at[mine], True)
    squares = GroupCopy(site, lambda q: b["ST"], lambda k: b["EX"].at[k - 1], False)
    crosses = GroupCopy(site, lambda q: b["SC"], lambda k: b["EC"].at[k - 1], False)
    pair_slot = site.take(1)

    def slices(name):
        return lambda q: b[name].at[at(q * length, length, length)]

    outs = GroupCopy(site, slices("OP"), lambda k: b["OB"].at[k - 1], False)
    grads = GroupCopy(site, slices("NP"), lambda k: b["NB"].at[k - 1], False)
    fo, fg, fh, fv, fu, fs = (
        Fold(
            site,
            b["G" + n],
            rows,
            (b["YR" + n], b["YL" + n]),
            (b["AR" + n], b["AL" + n]),
            b["T" + n],
            b["F" + n],
            n == "S",
        )
        for n in "OGHVUS"
    )
    fm = Exchange(site, b["GM"], b["YM"], b["TM"], b["FM"])
    assert site.used == sems[0] and site.used_own == sems[1]

    b["SH"][:, pl.ds(0, MAPS)] = inw_ref[:, pl.ds(INNER + INNER, MAPS)]
    steps = inw_ref[:, pl.ds(INNER + CONV_CH, HEADS)].astype(f32)
    filler = jnp.zeros((rows, LANES - HEADS), f32)
    b["SH"][:, pl.ds(MAPS, LANES)] = jnp.concatenate((steps, filler), axis=1).astype(bf16)
    site.greet()
    for item in (sm.members, wv.members, ws.members):
        item.start()
    for item in (sm, wv, ws):
        item.begin()
    for item in (wg.members, wo.members):
        item.start()
    heads_here = w // HEAD_DIM
    head = lax.div(iota((LANES, w), 1), HEAD_DIM)
    b["EM"][...] = (iota((LANES, w), 0) == head).astype(f32).astype(bf16)
    lanes = iota((LANES, LANES), 1)
    picked = (iota((LANES, LANES), 0) == lanes + s * heads_here) & (lanes < heads_here)
    b["SEL"][...] = picked.astype(f32).astype(bf16)
    b["HD"][...] = exact(dot, heads_ref[...], b["SEL"][...], 3)
    b["HD"][pl.ds(1, 1), :] = jnp.where(
        iota((1, LANES), 1) < heads_here, -jnp.exp(b["HD"][pl.ds(1, 1), :]), 0.0
    )
    for name in ("CACC", "NACC", "HACC", "PACC"):
        b[name][...] = jnp.zeros_like(b[name])
    b["CI"][pl.ds(0, 8), :] = jnp.zeros((8, cw), f32)
    b["DP"][pl.ds(tokens, 8), :] = jnp.zeros((8, cw), f32)

    def norm_scale(g):
        value = b["XF"][tok(g), :].astype(f32)
        inverse = lax.rsqrt(lanes_sum(value * value) / width + epsilon)
        b["INV"][tok(g), :] = jnp.broadcast_to(inverse, (GROUP, LANES))

    def forward(items, hop):
        for item in items:
            item.forward(hop)

    first = (sm, wv, ws)
    forward(first, 1)
    wg.begin()
    xg.start()
    for hop in range(2, nz):
        forward(first, hop)
        wg.forward(hop - 1)
        if hop == 2:
            wo.begin()
    xg.wait()
    cg.start()
    each_group(norm_scale)
    sm.finish()

    lane = iota((1, width), 1)
    pre_table = lambda: Table(owners, lane, width // owners)
    norm_table = lambda: Table(owners, iota((1, w), 1) + s * w, INNER // owners)

    def conv_table():
        place = iota((1, cw), 1)
        channel = jnp.where(place < w, place + s * w, place - w + INNER)
        return Table(owners, channel, CONV_CH // owners)

    b["GA"][pl.ds(0, 1), :] = pre_table().row(b["SM"][:, 0, :])
    b["NG"][pl.ds(0, 1), :] = norm_table().row(b["SM"][:, 1, :])
    taps = conv_table()
    for k in range(CONV + 1):
        b["CW"][pl.ds(k, 1), :] = taps.row(b["SM"][:, 2 + k, :])

    def flip(source, target):
        def body(g):
            for c in range(0, width, LANES):
                part = b[source][tok(g), pl.ds(c, LANES)].astype(f32)
                b[target][pl.ds(c, LANES), tok(g)] = part.T.astype(bf16)

        each_group(body)

    def normalise(g):
        value = b["XF"][tok(g), :].astype(f32) * b["INV"][tok(g), pl.ds(0, 1)]
        b["XN"][tok(g), :] = (value * b["GA"][pl.ds(0, 1), :]).astype(bf16)

    each_group(normalise)
    flip("XN", "NT")
    wg.forward(nz - 1)
    wo.forward(1)
    wv.finish()
    ws.finish()

    def project(g):
        normed = b["XN"][tok(g), :]
        here = at(g * GROUP + 8, GROUP, 8)
        shared = dot(normed, b["WS"][...])
        b["CI"][here, pl.ds(0, w)] = dot(normed, b["WV"][...])
        b["CI"][here, pl.ds(w, MAPS)] = shared[:, :MAPS]
        b["DT"][tok(g), :] = exact(dot, shared[:, MAPS:], b["SEL"][...], 3)
        window = b["CI"][at(g * GROUP, GROUP + 8, 8), :]
        total = jnp.broadcast_to(b["CW"][pl.ds(CONV, 1), :], (GROUP, cw))
        for k in range(CONV):
            shift = 8 - (CONV - 1) + k
            total = total + b["CW"][pl.ds(k, 1), :] * window[shift : shift + GROUP]
        b["PRE"][tok(g), :] = total

    each_group(project)
    wo.forward(2)

    causal = iota((GROUP, GROUP), 0) >= iota((GROUP, GROUP), 1)
    low_half = iota((1, LANES), 1) < HEAD_DIM

    def expand(value):
        return exact(dot, value, b["EM"][...], 2)

    def per_head(value):
        return exact(dot_nt, value, b["EM"][...], 2)

    def halves(value):
        return jnp.concatenate(
            (jnp.where(low_half, value, 0.0), jnp.where(low_half, 0.0, value)), axis=0
        )

    def front(g):
        pre = b["PRE"][tok(g), :]
        out = pre * sigmoid(pre)
        bias, rate = b["HD"][pl.ds(0, 1), :], b["HD"][pl.ds(1, 1), :]
        raw = b["DT"][tok(g), :] + bias
        step = softplus(raw)
        lower = causal.astype(f32).astype(bf16)
        pieces = split(step * rate, 3)
        cumulative = dot(lower, pieces[2]) + dot(lower, pieces[1]) + dot(lower, pieces[0])
        return out[:, :w], out[:, w : w + STATE], out[:, w + STATE :], raw, step, cumulative

    def decays(cumulative, turned, j, backward):
        column = cumulative[:, j : j + 1]
        row = turned[j : j + 1, :]
        if backward:
            upper = iota((GROUP, GROUP), 0) <= iota((GROUP, GROUP), 1)
            return jnp.exp(jnp.where(upper, row - column, -10000.0))
        return jnp.exp(jnp.where(causal, column - row, -10000.0))

    b["RUN"][...] = jnp.zeros_like(b["RUN"])

    def ssd_forward(g):
        values, in_map, out_map, raw, step, cumulative = front(g)
        turned = cumulative.T
        last = cumulative[GROUP - 1 :, :]
        grown = jnp.exp(cumulative)
        grown_wide = expand(grown)
        carried = b["RUN"][...]
        b["CAR"][g] = carried
        scores = mm_nt(out_map, in_map)
        weighted = values * expand(step)
        skip = exact(dot, b["HD"][...], b["EM"][...], 3)[2:3, :]
        rest = mm(out_map, carried) * grown_wide + skip * values
        for p in range(pairs):
            part = slice(p * LANES, (p + 1) * LANES)
            mixing = jnp.concatenate(
                [scores * decays(cumulative, turned, 2 * p + i, False) for i in range(2)], axis=1
            )
            inner = mm(mixing, halves(weighted[:, part]))
            b["SSD"][tok(g), part] = inner + rest[:, part]
        ends = expand(jnp.exp(last - cumulative) * step)
        state = mm(in_map.T, values * ends)
        b["RUN"][...] = carried * grown_wide[GROUP - 1 :, :] + state

    def between(lists, g):
        for item, first, hops in lists:
            for i, hop in enumerate(hops):

                @pl.when(g == min(first + i, groups - 1))
                def _(item=item, hop=hop):
                    item.forward(hop)

    def ssd_step(g):
        ssd_forward(g)
        between(((wo, 0, range(3, nz)),), g)

    each_group(ssd_step)
    wg.finish()

    norm_gain = lambda: b["NG"][pl.ds(0, 1), :]

    def to_lanes(column):
        return jnp.broadcast_to(column, (GROUP, LANES)).T[:8, :]

    def summed(own, boxes, g):
        total = b[own][:, tok(g)]
        for k in range(seq - 1):
            total = total + b[boxes][k, :, tok(g)]
        return jnp.concatenate([total] * (LANES // 8), axis=0).T[:, 0:1]

    def gate(g):
        raw = dot(b["XN"][tok(g), :], b["WG"][...])
        gated = b["SSD"][tok(g), :] * (raw * sigmoid(raw))
        b["GR"][tok(g), :] = raw
        b["GT"][tok(g), :] = gated
        b["ST"][:, tok(g)] = to_lanes(lanes_sum(gated * gated))

    each_group(gate)
    squares.start()
    cg.wait()
    flip("CF", "CT")
    squares.wait()

    def mix(g):
        inverse = lax.rsqrt(summed("ST", "EX", g) / INNER + epsilon)
        unit = b["GT"][tok(g), :] * inverse
        b["GT"][tok(g), :] = unit
        b["INM"][tok(g), :] = jnp.broadcast_to(inverse, (GROUP, LANES))
        b["MX"][tok(g), :] = (unit * norm_gain()).astype(bf16)

    each_group(mix)

    def weight_grad(fold, left, right, first=0):
        def block(rows_here):
            columns_here = pl.ds(first, fold.grad.shape[1])
            product = dot(b[left][rows_here], b[right][:, columns_here])
            fold.grad[rows_here] = product.astype(bf16)

        def offset(i):
            farther = nz - (i + 1) // 2
            return farther * (2 * lax.rem(i, 2) - 1)

        def each(i, carry):
            block(fold.block(offset(i)))
            return carry

        block(fold.block(nz))
        fold.begin()
        lax.fori_loop(1, dp, each, 0)

    weight_grad(fo, "CT", "MX")
    wo.finish()

    def gate_grad(g):
        mixed_grad = dot(b["CF"][tok(g), :], b["WO"][...])
        unit = b["GT"][tok(g), :]
        b["NACC"][pl.ds(0, 1), :] += rows_sum(mixed_grad * unit)
        mixed_grad = mixed_grad * norm_gain()
        b["MG"][tok(g), :] = mixed_grad
        b["SC"][:, tok(g)] = to_lanes(lanes_sum(mixed_grad * unit))

    each_group(gate_grad)
    crosses.start()
    fo.forward(1)

    def out_product(g):
        b["OP"][tok(g), :] = dot_nt(b["MX"][tok(g), :], b["WO"][...]).astype(bf16)

    each_group(out_product)
    crosses.wait()

    def gate_back(g):
        cross = summed("SC", "EC", g) / INNER
        inverse = b["INM"][tok(g), pl.ds(0, 1)]
        raw = b["GR"][tok(g), :]
        gated_grad = inverse * (b["MG"][tok(g), :] - b["GT"][tok(g), :] * cross)
        sig = sigmoid(raw)
        b["DY"][tok(g), :] = gated_grad * (raw * sig)
        slope = sig * (1.0 + raw * (1.0 - sig))
        b["PG"][tok(g), :] = (gated_grad * b["SSD"][tok(g), :] * slope).astype(bf16)

    each_group(gate_back)
    fo.forward(2)
    weight_grad(fg, "NT", "PG")
    weight_grad(fh, "NT", "PG", w // 2)
    b["GM"][:, 1, :] = norm_table().blocks(b["NACC"][pl.ds(0, 1), :])
    outs.start()

    b["RUN"][...] = jnp.zeros_like(b["RUN"])

    def ssd_backward(g, midway):
        values, in_map, out_map, raw, step, cumulative = front(g)
        turned = cumulative.T
        last = cumulative[GROUP - 1 :, :]
        grown_wide = expand(jnp.exp(cumulative))
        step_wide = expand(step)
        weighted = values * step_wide
        skip = exact(dot, b["HD"][...], b["EM"][...], 3)[2:3, :]
        out_grad = b["DY"][tok(g), :]
        ssd = b["SSD"][tok(g), :]
        carried, after = b["CAR"][g], b["RUN"][...]
        rate = b["HD"][pl.ds(1, 1), :]

        b["NACC"][pl.ds(1, 1), :] += rows_sum(out_grad * values)
        cumul_grad = per_head(out_grad * (ssd - skip * values))
        grown_grad = out_grad * grown_wide
        ends = jnp.exp(last - cumulative)
        ends_wide = expand(ends * step)
        out_map_grad = mm_nt(grown_grad, carried)
        scaled_grad = mm(in_map, after)
        in_map_grad = mm_nt(values * ends_wide, after)
        ends_grad = per_head(scaled_grad * values)
        step_grad = ends_grad * ends
        ends_cumul = ends_grad * ends * step
        cumul_grad = cumul_grad - ends_cumul
        decay_sum = rows_sum(after * carried)
        decay_grad = per_head(jnp.broadcast_to(decay_sum, (8, w)))[0:1, :] * jnp.exp(last)
        last_grad = rows_sum(ends_cumul) + decay_grad
        b["RUN"][...] = mm(out_map.T, grown_grad) + after * grown_wide[GROUP - 1 :, :]
        scores_turned = mm_nt(in_map, out_map)
        scores_grad = jnp.zeros((GROUP, GROUP), f32)
        value_grads, step_parts = [], []
        for p in range(pairs):
            part = slice(p * LANES, (p + 1) * LANES)
            if p == pairs // 2:
                midway()
            grads_here = halves(out_grad[:, part])
            mixing = jnp.concatenate(
                [scores_turned * decays(cumulative, turned, 2 * p + i, True) for i in range(2)],
                axis=1,
            )
            inner = mm(mixing, grads_here)
            step_parts.append(inner * values[:, part])
            value_grads.append(inner * step_wide[:, part])
            mixing_grad = mm_nt(grads_here, weighted[:, part])
            for i in range(2):
                scores_grad = scores_grad + (
                    decays(cumulative, turned, 2 * p + i, False)
                    * mixing_grad[i * GROUP : (i + 1) * GROUP]
                )
        inner_step = per_head(jnp.concatenate(step_parts, axis=1))
        step_grad = step_grad + inner_step
        cumul_grad = cumul_grad - inner_step * step
        values_grad = (
            jnp.concatenate(value_grads, axis=1) + scaled_grad * ends_wide + skip * out_grad
        )
        out_map_grad = out_map_grad + mm(scores_grad, in_map)
        in_map_grad = in_map_grad + mm(scores_grad.T, out_map)
        at_last = iota((GROUP, LANES), 0) == GROUP - 1
        cumul_grad = cumul_grad + jnp.where(at_last, last_grad, 0.0)
        upper = (iota((GROUP, GROUP), 0) <= iota((GROUP, GROUP), 1)).astype(f32).astype(bf16)
        pieces = split(cumul_grad, 3)
        rated_grad = dot(upper, pieces[2]) + dot(upper, pieces[1]) + dot(upper, pieces[0])
        step_grad = step_grad + rated_grad * rate
        b["HACC"][pl.ds(1, 1), :] += rows_sum(rated_grad * step * rate)
        raw_grad = step_grad * sigmoid(raw)
        b["HACC"][pl.ds(0, 1), :] += rows_sum(raw_grad)
        pre = b["PRE"][tok(g), :]
        sig = sigmoid(pre)
        conv_grad = jnp.concatenate((values_grad, in_map_grad, out_map_grad), axis=1)
        pre_grad = conv_grad * (sig * (1.0 + pre * (1.0 - sig)))
        b["DP"][tok(g), :] = pre_grad
        before = b["CI"][at(g * GROUP, GROUP + 8, 8), :]
        following = jnp.concatenate((pre_grad, b["DP"][at(g * GROUP + GROUP, 8, 8), :]), axis=0)
        total = None
        for k in range(CONV):
            shift = 8 - (CONV - 1) + k
            b["CACC"][pl.ds(k, 1), :] += rows_sum(pre_grad * before[shift : shift + GROUP])
            back = CONV - 1 - k
            term = b["CW"][pl.ds(k, 1), :] * following[back : back + GROUP]
            total = term if total is None else total + term
        b["CACC"][pl.ds(CONV, 1), :] += rows_sum(pre_grad)
        b["PV"][tok(g), :] = total[:, :w].astype(bf16)
        b["PS"][tok(g), :] = jnp.concatenate(
            (total[:, w:], exact(dot_nt, raw_grad, b["SEL"][...], 2)), axis=1
        ).astype(bf16)

    def ssd_back_step(g):
        steps = range(1, nz)
        midway = lambda: between(((fo, 0, steps[2:]), (fh, 1, steps)), g)
        ssd_backward(groups - 1 - g, midway)
        between(((fg, 0, steps),), g)

    each_group(ssd_back_step)

    block = block_rows // 2

    def shared_block(d, carry):
        left = b["NT"][at(d * block_rows, block_rows, block_rows)]
        b["QS"][d] = dot(left, b["PS"][...]).astype(bf16)
        return carry

    lax.fori_loop(0, dp, shared_block, 0)
    mine_half = lax.rem(s, 2) * block
    pair = site.copy(
        b["QS"].at[:, at(block - mine_half, block, block)], b["QB"], pair_slot, site.twin()
    )
    pair.start()

    weight_grad(fv, "NT", "PV")
    weight_grad(fu, "NT", "PV", w // 2)
    pair.wait_recv()

    def add_twin(d, carry):
        both = b["QS"][d, at(mine_half, block, block)].astype(f32) + b["QB"][d].astype(f32)
        b["GS"][at(d * block, block, block)] = both.astype(bf16)
        return carry

    lax.fori_loop(0, dp, add_twin, 0)
    fs.begin()
    for item in (fo, fg, fh):
        item.finish()
    forward((fv, fu), 1)

    def normed_grad(g):
        total = (
            dot_nt(b["PV"][tok(g), :], b["WV"][...])
            + dot_nt(b["PG"][tok(g), :], b["WG"][...])
            + dot_nt(b["PS"][tok(g), :], b["WS"][...])
        )
        b["NP"][tok(g), :] = total.astype(bf16)
        unit = b["XF"][tok(g), :].astype(f32) * b["INV"][tok(g), pl.ds(0, 1)]
        b["PACC"][pl.ds(0, 1), :] += rows_sum(total * unit)

    each_group(normed_grad)
    grads.start()
    forward((fs,), 1)
    forward((fv, fu), 2)
    b["GM"][:, 0, :] = pre_table().blocks(b["PACC"][pl.ds(0, 1), :])
    taps = conv_table()
    for k in range(CONV + 1):
        b["GM"][:, 2 + k, :] = taps.blocks(b["CACC"][pl.ds(k, 1), :])
    skip_grad = per_head(jnp.broadcast_to(b["NACC"][pl.ds(1, 1), :], (8, w)))
    total = jnp.zeros((8, LANES), f32)
    kinds = (b["HACC"][pl.ds(0, 1), :], b["HACC"][pl.ds(1, 1), :], skip_grad[0:1, :])
    for i, row in enumerate(kinds):
        place = iota((LANES, LANES), 1) - s * heads_here - i * HEADS
        source = iota((LANES, LANES), 0)
        move = ((place == source) & (source < heads_here)).astype(f32).astype(bf16)
        total = total + exact(dot, jnp.broadcast_to(row, (8, LANES)), move, 3)
    b["GM"][:, 7, :] = jnp.broadcast_to(total[0:1, :], (owners, LANES))
    fm.begin()
    forward((fs,), 2)
    forward((fv, fu), 3)
    forward((fs,), 3)
    outs.wait()
    total = x_ref[...].astype(f32) + b["OP"][mine, :].astype(f32)
    for k in range(seq - 1):
        total = total + b["OB"][k].astype(f32)
    block_ref[...] = total.astype(bf16)
    grads.wait()
    total = b["NP"][mine, :].astype(f32)
    for k in range(seq - 1):
        total = total + b["NB"][k].astype(f32)
    scaled = total * b["GA"][pl.ds(0, 1), :]
    inverse = b["INV"][mine, pl.ds(0, 1)]
    unit = x_ref[...].astype(f32) * inverse
    mean = lanes_sum(scaled * unit) / width
    ingrad_ref[...] = inverse * (scaled - unit * mean) + cot_ref[...].astype(f32)
    for item in (fm, fv, fu, fs):
        item.finish()
    for item in (fo, fg, fh, fv, fu, fs, fm):
        item.members.wait()
    smalls, shared = b["FM"][0], None
    for q in range(seq):
        outshare_ref[:, pl.ds(q * w, w)] = b["FO"][q].astype(f32)
        inshare_ref[:, pl.ds(q * w, w // 2)] = b["FG"][q].astype(f32)
        inshare_ref[:, pl.ds(q * w + w // 2, w // 2)] = b["FH"][q].astype(f32)
        inshare_ref[:, pl.ds(INNER + q * w, w // 2)] = b["FV"][q].astype(f32)
        inshare_ref[:, pl.ds(INNER + q * w + w // 2, w // 2)] = b["FU"][q].astype(f32)
        if q > 0:
            smalls = smalls + b["FM"][q]
    for j in range(seq // 2):
        part = b["FS"][2 * j + s // (seq // 2)].astype(f32)
        shared = part if shared is None else shared + part
    inshare_ref[:, pl.ds(INNER + INNER, MAPS + HEADS)] = shared[:, : MAPS + HEADS]
    smalls = smalls[0]
    starts = ((0, 0), (1, 0), (2, 0), (6, 0), (7, 0), (7, HEADS), (7, 2 * HEADS))
    for ref, (top, left) in zip(small_refs, starts):
        ref[...] = smalls[top : top + ref.shape[0], left : left + ref.shape[1]]
    for drain in site.pending:
        drain()
    pair.wait_send()


def fused(x, cot, in_weight, out_weight, small, heads, dp, seq):
    length, width = x.shape
    rows, proj = in_weight.shape
    owners = dp * seq
    plan = scratch_plan(dp, seq, length, width, rows)
    names = tuple(plan)
    sems = (11 * (seq - 1 + dp) + (dp - 1) + (seq - 1) + 6 * (seq - 1) + dp + 1, 7)
    vmem = pl.BlockSpec(memory_space=pltpu.VMEM)
    return pl.pallas_call(
        functools.partial(fused_kernel, dp, seq, names, sems),
        out_shape=[
            jax.ShapeDtypeStruct((length, width), bf16),
            jax.ShapeDtypeStruct((length, width), f32),
            jax.ShapeDtypeStruct((rows, proj), f32),
            jax.ShapeDtypeStruct((rows, INNER), f32),
        ]
        + [
            jax.ShapeDtypeStruct(shape, f32)
            for shape in (
                (1, width // owners),
                (1, INNER // owners),
                (CONV, CONV_CH // owners),
                (1, CONV_CH // owners),
                (1, HEADS),
                (1, HEADS),
                (1, HEADS),
            )
        ],
        in_specs=[vmem] * 6,
        out_specs=[vmem] * 11,
        scratch_shapes=[pltpu.VMEM(*plan[name]) for name in names]
        + [
            pltpu.SemaphoreType.DMA((sems[0],)),
            pltpu.SemaphoreType.DMA((sems[0],)),
            pltpu.SemaphoreType.DMA((sems[1],)),
        ],
        compiler_params=pltpu.CompilerParams(
            collective_id=0, has_side_effects=True, vmem_limit_bytes=58 * 2**20
        ),
    )(x, cot, in_weight, out_weight, small, heads)


def place_kernel(count, *refs):
    copies = [
        pltpu.make_async_copy(refs[i], refs[count + i], refs[2 * count].at[i])
        for i in range(count)
    ]
    for copy in copies:
        copy.start()
    for copy in copies:
        copy.wait()


def placed(values):
    count = len(values)
    return pl.pallas_call(
        functools.partial(place_kernel, count),
        out_shape=[jax.ShapeDtypeStruct(value.shape, value.dtype) for value in values],
        in_specs=[pl.BlockSpec(memory_space=pltpu.VMEM)] * count,
        out_specs=[pl.BlockSpec(memory_space=pl.ANY)] * count,
        scratch_shapes=[pltpu.SemaphoreType.DMA((count,))],
    )(*values)


def fits(dp, seq, block_input, in_weight):
    seq_dev, length, width = block_input.shape
    rows = in_weight.shape[0]
    owners = dp * seq
    return (
        seq_dev == 1
        and dp == 2 * RING_HOPS
        and seq % 2 == 0
        and length % GROUP == 0
        and rows % 32 == 0
        and rows <= LANES
        and INNER % (seq * 2 * LANES) == 0
        and INNER % owners == 0
        and CONV_CH % owners == 0
        and CONV_CH // owners <= LANES
        and dp // 2 <= seq * length // GROUP + 1
    )


def spread_rows(values):
    total, first = None, 0
    for value in values:
        value = value.reshape(-1, value.shape[-1]).astype(f32)
        count, size = value.shape
        value = jnp.pad(value, ((first, 8 - first - count), (0, LANES - size)))
        total = value if total is None else total + value
        first += count
    return total


def on_device_fused(
    block_input,
    in_weight,
    out_weight,
    pre_gain,
    norm_gain,
    conv_weight,
    conv_bias,
    dt_bias,
    decay_log,
    skip_gain,
    cotangent,
):
    dp, seq = lax.axis_size("dp"), lax.axis_size("seq")
    small = spread_rows((pre_gain, norm_gain, conv_weight, conv_bias))[None]
    heads = spread_rows((dt_bias, decay_log, skip_gain))
    results = fused(
        block_input[0], cotangent[0], in_weight, out_weight.T, small, heads, dp, seq
    )
    block, in_grad, in_share, out_share, *smalls = placed(results)
    taps = smalls.pop(2)
    pre, norm, bias, dt, decay, skip = (value.reshape(-1) for value in smalls)
    return (
        block[None],
        in_grad[None],
        in_share,
        out_share.T,
        pre,
        norm,
        taps,
        bias,
        dt,
        decay,
        skip,
    )


def from_behind(value, axis, steps):
    count = lax.axis_size(axis)
    leading, last = (max(0, -steps), min(count, count - steps))
    return lax.ppermute(value, axis, [(source, source + steps) for source in range(leading, last)])


def convolve(padded, conv_weight, conv_bias):
    taps = conv_weight.shape[0]
    length = padded.shape[-2] - taps + 1
    total = conv_bias
    for index in range(taps):
        total = total + conv_weight[index] * lax.slice_in_dim(
            padded, index, index + length, axis=padded.ndim - 2
        )
    return total


def running_sum(value):
    length = value.shape[1]
    lower = (jnp.arange(length)[:, None] >= jnp.arange(length)[None, :]).astype(value.dtype)
    return jnp.einsum("ts,bsh->bth", lower, value, precision=lax.Precision.HIGHEST)


def carry_scan(state, decay, axis, sign):
    count = lax.axis_size(axis)
    within, within_decay = state, decay
    entering, entering_decay = None, None
    width = 1
    while width < count:
        moved = from_behind(within.astype(jnp.bfloat16), axis, sign * width).astype(jnp.float32)
        last = 2 * width >= count
        if not last or entering is None:
            moved_decay = from_behind(within_decay, axis, sign * width)
        if entering is None:
            entering, entering_decay = moved, moved_decay
        else:
            entering = entering + entering_decay[:, :, None, None] * moved
            if not last:
                entering_decay = entering_decay * moved_decay
        if not last:
            within = within + within_decay[:, :, None, None] * moved
            within_decay = within_decay * moved_decay
        width *= 2
    return jnp.zeros_like(state) if entering is None else entering


def front_fn(tail, rim, conv_weight, conv_bias, dt_bias, decay_log):
    conv_in = tail[..., :CONV_CH]
    dt_raw = tail[..., CONV_CH:]
    padded = jnp.concatenate([rim, conv_in], axis=-2)
    conv_out = jax.nn.silu(convolve(padded, conv_weight, conv_bias))
    leading = conv_out.shape[:-1]
    values = conv_out[..., :INNER].reshape(leading + (HEADS, HEAD_DIM))
    in_map = conv_out[..., INNER : INNER + STATE]
    out_map = conv_out[..., INNER + STATE :]
    step = jax.nn.softplus(dt_raw + dt_bias)
    cumulative = running_sum(step * -jnp.exp(decay_log))
    return (values, in_map, out_map, step, cumulative)


def group_state(values, in_map, step, cumulative):
    weights_end = jnp.exp(cumulative[-1][None, :] - cumulative) * step
    state = jnp.einsum("shp,sn->hpn", values * weights_end[:, :, None], in_map, precision=highest)
    return (state, jnp.exp(cumulative[-1]))


def group_output(values, in_map, out_map, step, cumulative, carried, skip_gain):
    length = values.shape[0]
    scores = jnp.dot(out_map, in_map.T, precision=highest)
    causal = jnp.arange(length)[:, None] >= jnp.arange(length)[None, :]
    spread = cumulative[:, None, :] - cumulative[None, :, :]
    decay = jnp.exp(jnp.where(causal[:, :, None], spread, -10000.0))
    mixing = scores[:, :, None] * decay * step[None, :, :]
    inner_part = jnp.einsum("tsh,shp->thp", mixing, values, precision=highest)
    carried_part = (
        jnp.einsum("tn,hpn->thp", out_map, carried, precision=highest)
        * jnp.exp(cumulative)[:, :, None]
    )
    return inner_part + carried_part + skip_gain[None, :, None] * values


def state_fn(values, in_map, step, cumulative):
    return jax.vmap(group_state)(values, in_map, step, cumulative)


def out_fn(values, in_map, out_map, step, cumulative, gate_raw, carried, skip_gain, norm_gain):
    ssd_out = jax.vmap(group_output, in_axes=(0, 0, 0, 0, 0, 0, None))(
        values, in_map, out_map, step, cumulative, carried, skip_gain
    )
    ssd_out = ssd_out.reshape(gate_raw.shape)
    gated = ssd_out * jax.nn.silu(gate_raw)
    inverse = lax.rsqrt(jnp.mean(gated * gated, axis=-1, keepdims=True) + epsilon)
    return gated * inverse * norm_gain


def by_rows(grad, owners):
    return grad.reshape(owners, -1)


def by_columns(grad, owners):
    rows = grad.shape[0]
    return jnp.transpose(grad.reshape(rows, owners, -1), (1, 0, 2)).reshape(owners, -1)


def on_device(
    block_input,
    in_weight,
    out_weight,
    pre_gain,
    norm_gain,
    conv_weight,
    conv_bias,
    dt_bias,
    decay_log,
    skip_gain,
    cotangent,
):
    seq_dev, length, width = block_input.shape
    dp, seq = lax.axis_size("dp"), lax.axis_size("seq")
    owners = dp * seq
    both = ("dp", "seq")
    if fits(dp, seq, block_input, in_weight):
        return on_device_fused(
            block_input,
            in_weight,
            out_weight,
            pre_gain,
            norm_gain,
            conv_weight,
            conv_bias,
            dt_bias,
            decay_log,
            skip_gain,
            cotangent,
        )
    small_parts = (pre_gain, norm_gain, conv_weight.reshape(-1), conv_bias)
    small_sizes = [part.size for part in small_parts]
    small = jnp.concatenate(small_parts)
    in_full = lax.all_gather(in_weight, both, axis=0, tiled=True)
    gate_w, tail_w = in_full[:, :INNER], in_full[:, INNER:]
    out_t = lax.all_gather(out_weight.T, both, axis=0, tiled=True)
    small_all = lax.all_gather(small, both, axis=0)
    pieces, start = [], 0
    for size in small_sizes:
        pieces.append(small_all[:, start : start + size])
        start += size
    pre_full, norm_full, conv_b_full = (pieces[i].reshape(-1) for i in (0, 1, 3))
    conv_w_full = jnp.transpose(pieces[2].reshape(owners, CONV, -1), (1, 0, 2)).reshape(CONV, -1)
    pre_float = pre_full.astype(jnp.float32)
    norm_float = norm_full.astype(jnp.float32)
    inputs = block_input.astype(jnp.float32)
    inv_pre = lax.rsqrt(jnp.mean(inputs * inputs, axis=-1, keepdims=True) + epsilon)
    normed = (inputs * inv_pre * pre_float).astype(jnp.bfloat16)
    flat_normed = normed.reshape(seq_dev * length, width)
    gate_raw = jnp.dot(flat_normed, gate_w, preferred_element_type=jnp.float32).reshape(
        seq_dev, length, -1
    )
    tail = jnp.dot(flat_normed, tail_w, preferred_element_type=jnp.float32).reshape(
        seq_dev, length, -1
    )
    conv_in = tail[:, length - (CONV - 1) :, :CONV_CH]
    rim = from_behind(conv_in, "seq", 1)
    front_out, front_pull = jax.vjp(
        front_fn,
        tail,
        rim,
        conv_w_full.astype(jnp.float32),
        conv_b_full.astype(jnp.float32),
        dt_bias,
        decay_log,
    )
    values, in_map, out_map, step, cumulative = front_out
    state_out, state_pull = jax.vjp(state_fn, values, in_map, step, cumulative)
    state, decay = state_out
    carried = carry_scan(state, decay, "seq", 1)
    mixed_float, out_pull = jax.vjp(
        out_fn, values, in_map, out_map, step, cumulative, gate_raw, carried, skip_gain, norm_float
    )
    mixed = mixed_float.astype(jnp.bfloat16)
    flat_mixed = mixed.reshape(seq_dev * length, INNER)
    block_output = (
        inputs
        + jnp.dot(flat_mixed, out_t.T, preferred_element_type=jnp.float32).reshape(
            seq_dev, length, width
        )
    ).astype(jnp.bfloat16)
    flat_grad = cotangent.reshape(seq_dev * length, width)
    mixed_grad = jnp.dot(flat_grad, out_t, preferred_element_type=jnp.float32).reshape(
        seq_dev, length, INNER
    )
    out_w_grad = jnp.dot(flat_grad.T, flat_mixed, preferred_element_type=jnp.float32)
    (
        values_a,
        in_map_a,
        out_map_grad,
        step_a,
        cumul_a,
        gate_grad,
        local_grad,
        skip_grad,
        norm_grad,
    ) = out_pull(mixed_grad)

    later_grad = carry_scan(local_grad, decay, "seq", -1)
    decay_grad = jnp.sum(later_grad * carried, axis=(2, 3))
    values_b, in_map_b, step_b, cumul_b = state_pull((later_grad, decay_grad))
    front_grads = front_pull(
        (
            values_a + values_b,
            in_map_a + in_map_b,
            out_map_grad,
            step_a + step_b,
            cumul_a + cumul_b,
        )
    )
    tail_float, rim_grad, conv_w_grad, conv_b_grad, dt_grad, decay_log_grad = front_grads
    returned = from_behind(rim_grad, "seq", -1)
    tail_float = tail_float + jnp.pad(returned, ((0, 0), (length - (CONV - 1), 0), (0, HEADS)))
    tail_grad = tail_float.astype(jnp.bfloat16).reshape(seq_dev * length, -1)
    gate_grad = gate_grad.astype(jnp.bfloat16).reshape(seq_dev * length, -1)
    gate_w_grad = jnp.dot(flat_normed.T, gate_grad, preferred_element_type=jnp.float32)
    tail_w_grad = jnp.dot(flat_normed.T, tail_grad, preferred_element_type=jnp.float32)
    normed_grad = (
        jnp.dot(gate_grad, gate_w.T, preferred_element_type=jnp.float32)
        + jnp.dot(tail_grad, tail_w.T, preferred_element_type=jnp.float32)
    ).reshape(seq_dev, length, width)
    pre_grad = jnp.sum(normed_grad * inputs * inv_pre, axis=(0, 1))
    scaled = normed_grad * pre_float
    unit = inputs * inv_pre
    input_grad = inv_pre * (
        scaled - unit * jnp.mean(scaled * unit, axis=-1, keepdims=True)
    ) + cotangent.astype(jnp.float32)
    small_grads = jnp.concatenate(
        (
            by_rows(pre_grad, owners),
            by_rows(norm_grad, owners),
            by_columns(conv_w_grad, owners),
            by_rows(conv_b_grad, owners),
        ),
        axis=1,
    )
    heads = jnp.concatenate((dt_grad, decay_log_grad, skip_grad))
    scatter = functools.partial(
        lax.psum_scatter, axis_name=both, scatter_dimension=0, tiled=True
    )
    in_share = scatter(jnp.concatenate((gate_w_grad, tail_w_grad), axis=1))
    out_share = scatter(out_w_grad).T
    small_share = scatter(small_grads)[0]
    heads = lax.psum(heads, both)
    shares, start = [], 0
    for size in small_sizes:
        shares.append(small_share[start : start + size])
        start += size
    pre_share, norm_share, conv_w_share, conv_b_share = shares
    conv_w_share = conv_w_share.reshape(CONV, -1)
    heads_total = (heads[:HEADS], heads[HEADS : 2 * HEADS], heads[2 * HEADS :])
    return (
        block_output,
        input_grad,
        in_share,
        out_share,
        pre_share,
        norm_share,
        conv_w_share,
        conv_b_share,
        heads_total[0],
        heads_total[1],
        heads_total[2],
    )


def solution(mesh):
    in_specs = (
        P("dp", "seq", None),
        P(("dp", "seq"), None),
        P(None, ("dp", "seq")),
        P(("dp", "seq")),
        P(("dp", "seq")),
        P(None, ("dp", "seq")),
        P(("dp", "seq")),
        P(),
        P(),
        P(),
        P("dp", "seq", None),
    )
    out_specs = (
        P("dp", "seq", None),
        P("dp", "seq", None),
        P(("dp", "seq"), None),
        P(None, ("dp", "seq")),
        P(("dp", "seq")),
        P(("dp", "seq")),
        P(None, ("dp", "seq")),
        P(("dp", "seq")),
        P(),
        P(),
        P(),
    )
    return jax.shard_map(
        on_device, mesh=mesh, in_specs=in_specs, out_specs=out_specs, check_vma=False
    )
```

```python
import functools

import jax
import jax.numpy as jnp
from jax import lax
from jax.experimental import pallas as pl
from jax.experimental.pallas import tpu as pltpu
from jax.sharding import PartitionSpec as P

HEADS = 32
HEAD_DIM = 64
STATE = 128
CONV = 4
GROUP = 128
INNER = 2048
CONV_CH = 2304
LANES = 128
MAPS = CONV_CH - INNER
SHARED = MAPS + LANES
RING_HOPS = 4


epsilon = 1e-05
highest = lax.Precision.HIGH
bf16 = jnp.bfloat16
f32 = jnp.float32


def at(start, size, multiple):
    return pl.ds(start if isinstance(start, int) else pl.multiple_of(start, multiple), size)


def remote(src, dst, send, recv, device):
    return pltpu.make_async_remote_copy(
        src_ref=src,
        dst_ref=dst,
        send_sem=send,
        recv_sem=recv,
        device_id=device,
        device_id_type=pl.DeviceIdType.MESH,
    )


class Site:
    def __init__(self, dp, seq, send, recv, own):
        self.nz, self.ns = dp // 2, seq
        self.d, self.s = lax.axis_index("dp"), lax.axis_index("seq")
        far, level = lax.rem(self.d, 2), self.d // 2
        self.dp, self.half = dp, dp // 2
        self.place = level + far * (dp - 1 - 2 * level)
        self.owner = self.d * seq + self.s
        self.send, self.recv, self.own = send, recv, own
        self.used, self.used_own = 0, 0
        self.pending = []

    def group(self, k):
        return (self.d, lax.rem(self.s + k, self.ns))

    def ring(self, offset):
        place = lax.rem(self.place + offset + 2 * self.dp, self.dp)
        far = place // self.nz
        level = place + far * (self.dp - 1 - 2 * place)
        return level * 2 + far

    def beside(self, way):
        return (self.ring(way), self.s)

    def twin(self):
        return (self.d, self.s + 1 - 2 * lax.rem(self.s, 2))

    def take(self, count):
        self.used += count
        return self.used - count

    def copy(self, src, dst, slot, device):
        return remote(src, dst, self.send.at[slot], self.recv.at[slot], device)

    def greet(self):
        barrier = pltpu.get_barrier_semaphore()
        partners = [self.group(k) for k in range(1, self.ns)]
        partners += [(lax.rem(self.d + k, self.dp), self.s) for k in range(1, self.dp)]
        for partner in partners:
            pl.semaphore_signal(
                barrier, inc=1, device_id=partner, device_id_type=pl.DeviceIdType.MESH
            )
        pl.semaphore_wait(barrier, len(partners))


class GroupCopy:
    def __init__(self, site, source, dest, local, wanted=None):
        self.site, self.source, self.dest, self.local = site, source, dest, local
        self.wanted = wanted
        self.base = site.take(site.ns - 1)
        if local:
            self.own = site.used_own
            site.used_own += 1
        site.pending.append(self.drain)

    def own_copy(self):
        site = self.site
        return pltpu.make_async_copy(self.source(site.s), self.dest(0), site.own.at[self.own])

    def copy(self, k):
        site = self.site
        member = lax.rem(site.s + k, site.ns)
        return site.copy(self.source(member), self.dest(k), self.base + k - 1, site.group(k))

    def each(self, act, sending):
        site = self.site
        for k in range(1, site.ns):
            if self.wanted is None:
                act(k)
                continue
            other = lax.rem(site.s + (k if sending else site.ns - k), site.ns)
            ends = (site.s, other) if sending else (other, site.s)
            pl.when(self.wanted(*ends))(functools.partial(act, k))

    def start(self):
        self.each(lambda k: self.copy(k).start(), True)
        if self.local:
            self.own_copy().start()

    def wait(self):
        if self.local:
            self.own_copy().wait()
        self.each(lambda k: self.copy(k).wait_recv(), False)

    def drain(self):
        self.each(lambda k: self.copy(k).wait_send(), True)


class Spread:
    def __init__(self, site, buf, rows, source, twins=False):
        self.site, self.buf, self.rows, self.source = site, buf, rows, source
        self.block_rows, self.twins = site.ns * rows, twins
        self.members = GroupCopy(
            site, source, lambda k: buf.at[at(site.owner * rows, rows, rows)], True
        )
        self.base = {way: site.take(site.half) for way in (1, -1)}
        self.twin_base = {way: site.take(site.half) for way in (1, -1)} if twins else None
        site.pending.append(self.drain)

    def block(self, way, offset, halved):
        size = self.block_rows
        start = self.site.ring(offset) * size
        if self.twins:
            size = size // 2
            start = start + lax.rem(self.site.s, 2) * size
        if halved:
            size = size // 2
            start = start if way > 0 else start + size
        return self.buf.at[at(start, size, size)]

    def copy(self, way, hop):
        site = self.site
        block = self.block(way, way * (1 - hop), hop == site.half)
        return site.copy(block, block, self.base[way] + hop - 1, site.beside(way))

    def twin_copy(self, way, hop):
        site = self.site
        block = self.block(way, -way * hop, hop == site.half)
        return site.copy(block, block, self.twin_base[way] + hop - 1, site.twin())

    def begin(self):
        self.members.wait()
        for way in (1, -1):
            self.copy(way, 1).start()

    def forward(self, hop):
        for way in (1, -1):
            self.copy(way, hop).wait_recv()
            self.copy(way, hop + 1).start()
            if self.twins:
                self.twin_copy(way, hop).start()

    def finish(self):
        last = self.site.half
        for way in (1, -1):
            self.copy(way, last).wait_recv()
            if self.twins:
                self.twin_copy(way, last).start()
        if self.twins:
            for way in (1, -1):
                for hop in range(1, last + 1):
                    self.twin_copy(way, hop).wait_recv()

    def drain(self):
        for way in (1, -1):
            for hop in range(1, self.site.half + 1):
                self.copy(way, hop).wait_send()
                if self.twins:
                    self.twin_copy(way, hop).wait_send()


class Fold:
    def __init__(self, site, grad, rows, boxes, sums, total, final, twins=False):
        self.site, self.grad, self.rows, self.twins = site, grad, rows, twins
        self.members_in = site.ns // 2 if twins else site.ns
        self.block_rows = self.members_in * rows
        self.boxes, self.sums = dict(zip((1, -1), boxes)), dict(zip((1, -1), sums))
        self.total, self.final = total, final
        self.base = {way: site.take(site.half) for way in (1, -1)}
        self.members = GroupCopy(
            site,
            lambda q: total.at[self.rows_for(q)],
            lambda k: final.at[site.s],
            False,
            (lambda a, q: lax.rem(a, 2) == q // self.members_in) if twins else None,
        )
        site.pending.append(self.drain)

    def rows_for(self, q):
        return at(lax.rem(q, self.members_in) * self.rows, self.rows, self.rows)

    def block(self, offset):
        return at(self.site.ring(offset) * self.block_rows, self.block_rows, self.block_rows)

    def copy(self, way, hop):
        site, size = self.site, self.block_rows // 2
        if hop == 1:
            shift = 0 if way > 0 else size
            source = self.grad.at[at(site.ring(way * site.half) * 2 * size + shift, size, size)]
            dest = self.boxes[way].at[0, pl.ds(shift, size)]
        else:
            source, dest = self.sums[way].at[hop - 2], self.boxes[way].at[hop - 1]
        return site.copy(source, dest, self.base[way] + hop - 1, site.beside(way))

    def begin(self):
        for way in (1, -1):
            self.copy(way, 1).start()

    def forward(self, hop):
        site, size = self.site, self.block_rows // 2
        for way in (1, -1):
            self.copy(way, hop).wait_recv()
            kept = self.grad[self.block(way * (site.half - hop))]
            box, sums = self.boxes[way], self.sums[way]
            if hop == 1:
                near, far = (slice(0, size), slice(size, None))[::way]
                both = kept[near].astype(f32) + box[0, near].astype(f32)
                sums[0, near] = both.astype(sums.dtype)
                sums[0, far] = kept[far]
            else:
                both = kept.astype(f32) + box[hop - 1].astype(f32)
                sums[hop - 1] = both.astype(sums.dtype)
            self.copy(way, hop + 1).start()

    def finish(self):
        site = self.site
        total = self.grad[self.block(0)].astype(f32)
        for way in (1, -1):
            self.copy(way, site.half).wait_recv()
            total = total + self.boxes[way][site.half - 1].astype(f32)
        self.total[...] = total.astype(self.total.dtype)
        self.members.start()
        self.final[site.s] = self.total[self.rows_for(site.s)]

    def drain(self):
        for way in (1, -1):
            for hop in range(1, self.site.half + 1):
                self.copy(way, hop).wait_send()


class Exchange:
    def __init__(self, site, table, boxes, total, final):
        self.site, self.table, self.boxes, self.total = site, table, boxes, total
        self.base = site.take(site.dp - 1)
        self.members = GroupCopy(
            site, lambda q: total.at[pl.ds(q, 1)], lambda k: final.at[site.s], False
        )
        self.final = final
        site.pending.append(self.drain)

    def copy(self, k):
        site = self.site
        other = lax.rem(site.d + k, site.dp)
        block = self.table.at[at(other * site.ns, site.ns, site.ns)]
        return site.copy(block, self.boxes.at[k - 1], self.base + k - 1, (other, site.s))

    def begin(self):
        for k in range(1, self.site.dp):
            self.copy(k).start()

    def finish(self):
        site = self.site
        total = self.table[at(site.d * site.ns, site.ns, site.ns)]
        for k in range(1, site.dp):
            self.copy(k).wait_recv()
            total = total + self.boxes[k - 1]
        self.total[...] = total
        self.members.start()
        self.final[site.s] = self.total[pl.ds(site.s, 1)]

    def drain(self):
        for k in range(1, self.site.dp):
            self.copy(k).wait_send()


def dot(a, b):
    return jnp.dot(a, b, preferred_element_type=f32)


def dot_nt(a, b):
    return lax.dot_general(a, b, (((1,), (1,)), ((), ())), preferred_element_type=f32)


def split(value, parts):
    pieces = []
    for _ in range(parts - 1):
        pieces.append(value.astype(bf16))
        value = value - pieces[-1].astype(f32)
    return pieces + [value.astype(bf16)]


def exact(product, value, onehot, parts):
    total = None
    for piece in split(value, parts)[::-1]:
        term = product(piece, onehot)
        total = term if total is None else total + term
    return total


def wide(product, a, b, passes):
    if passes == 1:
        return product(a.astype(bf16), b.astype(bf16))
    (a_hi, a_lo), (b_hi, b_lo) = split(a, 2), split(b, 2)
    total = product(a_hi, b_lo)
    if passes == 3:
        total = total + product(a_lo, b_hi)
    return total + product(a_hi, b_hi)


def mm(a, b, passes=3):
    return wide(dot, a, b, passes)


def mm_nt(a, b, passes=3):
    return wide(dot_nt, a, b, passes)


def iota(shape, axis):
    return lax.broadcasted_iota(jnp.int32, shape, axis)


def sigmoid(value):
    return 1.0 / (1.0 + jnp.exp(-value))


def softplus(value):
    small = jnp.exp(-jnp.abs(value))
    series = small * (1.0 - small * (0.5 - small * (1 / 3 - small * (0.25 - small * 0.2))))
    return jnp.maximum(value, 0.0) + jnp.where(small < 0.03, series, jnp.log(1.0 + small))


def rows_sum(value):
    return jnp.sum(value, axis=0, keepdims=True)


def lanes_sum(value):
    return jnp.sum(value, axis=1, keepdims=True)


class Table:
    def __init__(self, owners, channel, size):
        count = channel.shape[1]
        first = iota((owners, count), 0) * size
        place = channel - first
        self.mask = (place >= 0) & (place < size)
        spot = jnp.sum(jnp.where(self.mask, place.astype(f32), 0.0), axis=0, keepdims=True)
        self.onehot = (iota((LANES, count), 0).astype(f32) == spot).astype(f32).astype(bf16)

    def row(self, blocks):
        return rows_sum(jnp.where(self.mask, dot(blocks.astype(bf16), self.onehot), 0.0))

    def blocks(self, row):
        return exact(dot_nt, jnp.where(self.mask, row, 0.0), self.onehot, 3)


def scratch_plan(dp, seq, length, width, rows):
    nz, owners, tokens = dp // 2, dp * seq, seq * length
    w = INNER // seq
    cw, groups, block = w + MAPS, tokens // GROUP, seq * rows
    plan = dict(
        XF=((tokens, width), bf16),
        CF=((tokens, width), bf16),
        WV=((width, w), bf16),
        WS=((width, SHARED), bf16),
        WG=((width, w), bf16),
        WO=((width, w), bf16),
        SM=((owners, 8, LANES), f32),
        XN=((tokens, width), bf16),
        NT=((width, tokens), bf16),
        CT=((width, tokens), bf16),
        INV=((tokens, LANES), f32),
        INM=((tokens, LANES), f32),
        GA=((8, width), f32),
        NG=((8, w), f32),
        CW=((8, cw), f32),
        EM=((LANES, w), bf16),
        CI=((8 + tokens, cw), f32),
        PRE=((tokens, cw), f32),
        DT=((tokens, LANES), f32),
        CAR=((groups, STATE, w), f32),
        RUN=((STATE, w), f32),
        SSD=((tokens, w), f32),
        GR=((tokens, w), f32),
        GT=((tokens, w), f32),
        MG=((tokens, w), f32),
        ST=((8, tokens), f32),
        EX=((seq - 1, 8, tokens), f32),
        SC=((8, tokens), f32),
        EC=((seq - 1, 8, tokens), f32),
        MX=((tokens, w), bf16),
        PG=((tokens, w), bf16),
        DY=((tokens, w), f32),
        PV=((tokens, w), bf16),
        PS=((tokens, SHARED), bf16),
        DP=((tokens + 8, cw), f32),
        OP=((tokens, width), bf16),
        OB=((seq - 1, length, width), bf16),
        NP=((tokens, width), bf16),
        NB=((seq - 1, length, width), bf16),
        CACC=((8, cw), f32),
        NACC=((8, w), f32),
        HACC=((8, LANES), f32),
        PACC=((8, width), f32),
    )
    for name, columns in (("O", w), ("S", SHARED)) + tuple((n, w // 2) for n in "GHVU"):
        size = block // 2 if name == "S" else block
        plan["G" + name] = ((dp * size, columns), bf16)
        for way in "RL":
            plan["Y" + way + name] = ((nz, size, columns), bf16)
            plan["A" + way + name] = ((nz - 1, size, columns), bf16)
        plan["T" + name] = ((size, columns), bf16)
        plan["F" + name] = ((seq, rows, columns), bf16)
    plan["QS"] = ((dp, block, SHARED), bf16)
    plan["QB"] = ((dp, block // 2, SHARED), bf16)
    plan["SH"] = ((rows, SHARED), bf16)
    plan["SEL"] = ((LANES, LANES), bf16)
    plan["HD"] = ((8, LANES), f32)
    tile = (8, LANES)
    plan["GM"] = ((owners,) + tile, f32)
    plan["YM"] = ((dp - 1, seq) + tile, f32)
    plan["TM"] = ((seq,) + tile, f32)
    plan["FM"] = ((seq, 1) + tile, f32)
    return plan


def fused_kernel(dp, seq, names, sems, *refs):
    x_ref, cot_ref, inw_ref, outw_ref, small_ref, heads_ref = refs[:6]
    block_ref, ingrad_ref, inshare_ref, outshare_ref = refs[6:10]
    small_refs = refs[10:17]
    b = dict(zip(names, refs[17 : 17 + len(names)]))
    send, recv, own = refs[17 + len(names) :]
    site = Site(dp, seq, send, recv, own)
    nz, owners = dp // 2, dp * seq
    length, width = x_ref.shape
    rows = inw_ref.shape[0]
    tokens = seq * length
    groups = tokens // GROUP
    w = INNER // seq
    cw = w + MAPS
    pairs = w // LANES
    block_rows = seq * rows
    s = site.s

    def tok(g):
        return at(g * GROUP, GROUP, GROUP)

    def each_group(body):
        lax.fori_loop(0, groups, lambda g, c: (body(g), c)[1], 0)

    def columns(base):
        return lambda q: inw_ref.at[:, at(base + q * w, w, LANES)]

    sm = Spread(site, b["SM"], 1, lambda q: small_ref)
    wv = Spread(site, b["WV"], rows, columns(INNER))
    ws = Spread(site, b["WS"], rows, lambda q: b["SH"], True)
    wg = Spread(site, b["WG"], rows, columns(0))
    wo = Spread(site, b["WO"], rows, lambda q: outw_ref.at[:, at(q * w, w, LANES)])
    mine = at(s * length, length, length)
    xg = GroupCopy(site, lambda q: x_ref, lambda k: b["XF"].at[mine], True)
    cg = GroupCopy(site, lambda q: cot_ref, lambda k: b["CF"].at[mine], True)
    squares = GroupCopy(site, lambda q: b["ST"], lambda k: b["EX"].at[k - 1], False)
    crosses = GroupCopy(site, lambda q: b["SC"], lambda k: b["EC"].at[k - 1], False)
    pair_slot = site.take(1)

    def slices(name):
        return lambda q: b[name].at[at(q * length, length, length)]

    outs = GroupCopy(site, slices("OP"), lambda k: b["OB"].at[k - 1], False)
    grads = GroupCopy(site, slices("NP"), lambda k: b["NB"].at[k - 1], False)
    fo, fg, fh, fv, fu, fs = (
        Fold(
            site,
            b["G" + n],
            rows,
            (b["YR" + n], b["YL" + n]),
            (b["AR" + n], b["AL" + n]),
            b["T" + n],
            b["F" + n],
            n == "S",
        )
        for n in "OGHVUS"
    )
    fm = Exchange(site, b["GM"], b["YM"], b["TM"], b["FM"])
    assert site.used == sems[0] and site.used_own == sems[1]

    b["SH"][:, pl.ds(0, MAPS)] = inw_ref[:, pl.ds(INNER + INNER, MAPS)]
    steps = inw_ref[:, pl.ds(INNER + CONV_CH, HEADS)].astype(f32)
    filler = jnp.zeros((rows, LANES - HEADS), f32)
    b["SH"][:, pl.ds(MAPS, LANES)] = jnp.concatenate((steps, filler), axis=1).astype(bf16)
    site.greet()
    for item in (sm.members, wv.members, ws.members):
        item.start()
    for item in (sm, wv, ws):
        item.begin()
    for item in (wg.members, wo.members):
        item.start()
    heads_here = w // HEAD_DIM
    head = lax.div(iota((LANES, w), 1), HEAD_DIM)
    b["EM"][...] = (iota((LANES, w), 0) == head).astype(f32).astype(bf16)
    lanes = iota((LANES, LANES), 1)
    picked = (iota((LANES, LANES), 0) == lanes + s * heads_here) & (lanes < heads_here)
    b["SEL"][...] = picked.astype(f32).astype(bf16)
    b["HD"][...] = exact(dot, heads_ref[...], b["SEL"][...], 3)
    b["HD"][pl.ds(1, 1), :] = jnp.where(
        iota((1, LANES), 1) < heads_here, -jnp.exp(b["HD"][pl.ds(1, 1), :]), 0.0
    )
    for name in ("CACC", "NACC", "HACC", "PACC"):
        b[name][...] = jnp.zeros_like(b[name])
    b["CI"][pl.ds(0, 8), :] = jnp.zeros((8, cw), f32)
    b["DP"][pl.ds(tokens, 8), :] = jnp.zeros((8, cw), f32)

    def norm_scale(g):
        value = b["XF"][tok(g), :].astype(f32)
        inverse = lax.rsqrt(lanes_sum(value * value) / width + epsilon)
        b["INV"][tok(g), :] = jnp.broadcast_to(inverse, (GROUP, LANES))

    def forward(items, hop):
        for item in items:
            item.forward(hop)

    first = (sm, wv, ws)
    forward(first, 1)
    wg.begin()
    xg.start()
    for hop in range(2, nz):
        forward(first, hop)
        wg.forward(hop - 1)
        if hop == 2:
            wo.begin()
    xg.wait()
    cg.start()
    each_group(norm_scale)
    sm.finish()

    lane = iota((1, width), 1)
    pre_table = lambda: Table(owners, lane, width // owners)
    norm_table = lambda: Table(owners, iota((1, w), 1) + s * w, INNER // owners)

    def conv_table():
        place = iota((1, cw), 1)
        channel = jnp.where(place < w, place + s * w, place - w + INNER)
        return Table(owners, channel, CONV_CH // owners)

    b["GA"][pl.ds(0, 1), :] = pre_table().row(b["SM"][:, 0, :])
    b["NG"][pl.ds(0, 1), :] = norm_table().row(b["SM"][:, 1, :])
    taps = conv_table()
    for k in range(CONV + 1):
        b["CW"][pl.ds(k, 1), :] = taps.row(b["SM"][:, 2 + k, :])

    def flip(source, target):
        def body(g):
            for c in range(0, width, LANES):
                part = b[source][tok(g), pl.ds(c, LANES)].astype(f32)
                b[target][pl.ds(c, LANES), tok(g)] = part.T.astype(bf16)

        each_group(body)

    def normalise(g):
        value = b["XF"][tok(g), :].astype(f32) * b["INV"][tok(g), pl.ds(0, 1)]
        b["XN"][tok(g), :] = (value * b["GA"][pl.ds(0, 1), :]).astype(bf16)

    each_group(normalise)
    flip("XN", "NT")
    wg.forward(nz - 1)
    wo.forward(1)
    wv.finish()
    ws.finish()

    def project(g):
        normed = b["XN"][tok(g), :]
        here = at(g * GROUP + 8, GROUP, 8)
        shared = dot(normed, b["WS"][...])
        b["CI"][here, pl.ds(0, w)] = dot(normed, b["WV"][...])
        b["CI"][here, pl.ds(w, MAPS)] = shared[:, :MAPS]
        b["DT"][tok(g), :] = exact(dot, shared[:, MAPS:], b["SEL"][...], 3)
        window = b["CI"][at(g * GROUP, GROUP + 8, 8), :]
        total = jnp.broadcast_to(b["CW"][pl.ds(CONV, 1), :], (GROUP, cw))
        for k in range(CONV):
            shift = 8 - (CONV - 1) + k
            total = total + b["CW"][pl.ds(k, 1), :] * window[shift : shift + GROUP]
        b["PRE"][tok(g), :] = total

    each_group(project)
    wo.forward(2)

    causal = iota((GROUP, GROUP), 0) >= iota((GROUP, GROUP), 1)
    low_half = iota((1, LANES), 1) < HEAD_DIM

    def expand(value):
        return exact(dot, value, b["EM"][...], 2)

    def per_head(value):
        return exact(dot_nt, value, b["EM"][...], 2)

    def halves(value):
        return jnp.concatenate(
            (jnp.where(low_half, value, 0.0), jnp.where(low_half, 0.0, value)), axis=0
        )

    def front(g):
        pre = b["PRE"][tok(g), :]
        out = pre * sigmoid(pre)
        bias, rate = b["HD"][pl.ds(0, 1), :], b["HD"][pl.ds(1, 1), :]
        raw = b["DT"][tok(g), :] + bias
        step = softplus(raw)
        lower = causal.astype(f32).astype(bf16)
        pieces = split(step * rate, 3)
        cumulative = dot(lower, pieces[2]) + dot(lower, pieces[1]) + dot(lower, pieces[0])
        return out[:, :w], out[:, w : w + STATE], out[:, w + STATE :], raw, step, cumulative

    def decays(cumulative, turned, j, backward):
        column = cumulative[:, j : j + 1]
        row = turned[j : j + 1, :]
        if backward:
            upper = iota((GROUP, GROUP), 0) <= iota((GROUP, GROUP), 1)
            return jnp.exp(jnp.where(upper, row - column, -10000.0))
        return jnp.exp(jnp.where(causal, column - row, -10000.0))

    b["RUN"][...] = jnp.zeros_like(b["RUN"])

    def ssd_forward(g):
        values, in_map, out_map, raw, step, cumulative = front(g)
        turned = cumulative.T
        last = cumulative[GROUP - 1 :, :]
        grown = jnp.exp(cumulative)
        grown_wide = expand(grown)
        carried = b["RUN"][...]
        b["CAR"][g] = carried
        scores = mm_nt(out_map, in_map)
        weighted = values * expand(step)
        skip = exact(dot, b["HD"][...], b["EM"][...], 3)[2:3, :]
        rest = mm(out_map, carried) * grown_wide + skip * values
        for p in range(pairs):
            part = slice(p * LANES, (p + 1) * LANES)
            mixing = jnp.concatenate(
                [scores * decays(cumulative, turned, 2 * p + i, False) for i in range(2)], axis=1
            )
            inner = mm(mixing, halves(weighted[:, part]))
            b["SSD"][tok(g), part] = inner + rest[:, part]
        ends = expand(jnp.exp(last - cumulative) * step)
        state = mm(in_map.T, values * ends)
        b["RUN"][...] = carried * grown_wide[GROUP - 1 :, :] + state

    def between(lists, g):
        for item, first, hops in lists:
            for i, hop in enumerate(hops):

                @pl.when(g == min(first + i, groups - 1))
                def _(item=item, hop=hop):
                    item.forward(hop)

    def ssd_step(g):
        ssd_forward(g)
        between(((wo, 0, range(3, nz)),), g)

    each_group(ssd_step)
    wg.finish()

    norm_gain = lambda: b["NG"][pl.ds(0, 1), :]

    def to_lanes(column):
        return jnp.broadcast_to(column, (GROUP, LANES)).T[:8, :]

    def summed(own, boxes, g):
        total = b[own][:, tok(g)]
        for k in range(seq - 1):
            total = total + b[boxes][k, :, tok(g)]
        return jnp.concatenate([total] * (LANES // 8), axis=0).T[:, 0:1]

    def gate(g):
        raw = dot(b["XN"][tok(g), :], b["WG"][...])
        gated = b["SSD"][tok(g), :] * (raw * sigmoid(raw))
        b["GR"][tok(g), :] = raw
        b["GT"][tok(g), :] = gated
        b["ST"][:, tok(g)] = to_lanes(lanes_sum(gated * gated))

    each_group(gate)
    squares.start()
    cg.wait()
    flip("CF", "CT")
    squares.wait()

    def mix(g):
        inverse = lax.rsqrt(summed("ST", "EX", g) / INNER + epsilon)
        unit = b["GT"][tok(g), :] * inverse
        b["GT"][tok(g), :] = unit
        b["INM"][tok(g), :] = jnp.broadcast_to(inverse, (GROUP, LANES))
        b["MX"][tok(g), :] = (unit * norm_gain()).astype(bf16)

    each_group(mix)

    def weight_grad(fold, left, right, first=0):
        def block(rows_here):
            columns_here = pl.ds(first, fold.grad.shape[1])
            product = dot(b[left][rows_here], b[right][:, columns_here])
            fold.grad[rows_here] = product.astype(bf16)

        def offset(i):
            farther = nz - (i + 1) // 2
            return farther * (2 * lax.rem(i, 2) - 1)

        def each(i, carry):
            block(fold.block(offset(i)))
            return carry

        block(fold.block(nz))
        fold.begin()
        lax.fori_loop(1, dp, each, 0)

    weight_grad(fo, "CT", "MX")
    wo.finish()

    def gate_grad(g):
        mixed_grad = dot(b["CF"][tok(g), :], b["WO"][...])
        unit = b["GT"][tok(g), :]
        b["NACC"][pl.ds(0, 1), :] += rows_sum(mixed_grad * unit)
        mixed_grad = mixed_grad * norm_gain()
        b["MG"][tok(g), :] = mixed_grad
        b["SC"][:, tok(g)] = to_lanes(lanes_sum(mixed_grad * unit))

    each_group(gate_grad)
    crosses.start()
    fo.forward(1)

    def out_product(g):
        b["OP"][tok(g), :] = dot_nt(b["MX"][tok(g), :], b["WO"][...]).astype(bf16)

    each_group(out_product)
    crosses.wait()

    def gate_back(g):
        cross = summed("SC", "EC", g) / INNER
        inverse = b["INM"][tok(g), pl.ds(0, 1)]
        raw = b["GR"][tok(g), :]
        gated_grad = inverse * (b["MG"][tok(g), :] - b["GT"][tok(g), :] * cross)
        sig = sigmoid(raw)
        b["DY"][tok(g), :] = gated_grad * (raw * sig)
        slope = sig * (1.0 + raw * (1.0 - sig))
        b["PG"][tok(g), :] = (gated_grad * b["SSD"][tok(g), :] * slope).astype(bf16)

    each_group(gate_back)
    fo.forward(2)
    weight_grad(fg, "NT", "PG")
    weight_grad(fh, "NT", "PG", w // 2)
    b["GM"][:, 1, :] = norm_table().blocks(b["NACC"][pl.ds(0, 1), :])
    outs.start()

    b["RUN"][...] = jnp.zeros_like(b["RUN"])

    def ssd_backward(g, midway):
        values, in_map, out_map, raw, step, cumulative = front(g)
        turned = cumulative.T
        last = cumulative[GROUP - 1 :, :]
        grown_wide = expand(jnp.exp(cumulative))
        step_wide = expand(step)
        weighted = values * step_wide
        skip = exact(dot, b["HD"][...], b["EM"][...], 3)[2:3, :]
        out_grad = b["DY"][tok(g), :]
        ssd = b["SSD"][tok(g), :]
        carried, after = b["CAR"][g], b["RUN"][...]
        rate = b["HD"][pl.ds(1, 1), :]

        b["NACC"][pl.ds(1, 1), :] += rows_sum(out_grad * values)
        cumul_grad = per_head(out_grad * (ssd - skip * values))
        grown_grad = out_grad * grown_wide
        ends = jnp.exp(last - cumulative)
        ends_wide = expand(ends * step)
        out_map_grad = mm_nt(grown_grad, carried)
        scaled_grad = mm(in_map, after)
        in_map_grad = mm_nt(values * ends_wide, after)
        ends_grad = per_head(scaled_grad * values)
        step_grad = ends_grad * ends
        ends_cumul = ends_grad * ends * step
        cumul_grad = cumul_grad - ends_cumul
        decay_sum = rows_sum(after * carried)
        decay_grad = per_head(jnp.broadcast_to(decay_sum, (8, w)))[0:1, :] * jnp.exp(last)
        last_grad = rows_sum(ends_cumul) + decay_grad
        b["RUN"][...] = mm(out_map.T, grown_grad) + after * grown_wide[GROUP - 1 :, :]
        scores_turned = mm_nt(in_map, out_map)
        scores_grad = jnp.zeros((GROUP, GROUP), f32)
        value_grads, step_parts = [], []
        for p in range(pairs):
            part = slice(p * LANES, (p + 1) * LANES)
            if p == pairs // 2:
                midway()
            grads_here = halves(out_grad[:, part])
            mixing = jnp.concatenate(
                [scores_turned * decays(cumulative, turned, 2 * p + i, True) for i in range(2)],
                axis=1,
            )
            inner = mm(mixing, grads_here)
            step_parts.append(inner * values[:, part])
            value_grads.append(inner * step_wide[:, part])
            mixing_grad = mm_nt(grads_here, weighted[:, part])
            for i in range(2):
                scores_grad = scores_grad + (
                    decays(cumulative, turned, 2 * p + i, False)
                    * mixing_grad[i * GROUP : (i + 1) * GROUP]
                )
        inner_step = per_head(jnp.concatenate(step_parts, axis=1))
        step_grad = step_grad + inner_step
        cumul_grad = cumul_grad - inner_step * step
        values_grad = (
            jnp.concatenate(value_grads, axis=1) + scaled_grad * ends_wide + skip * out_grad
        )
        out_map_grad = out_map_grad + mm(scores_grad, in_map)
        in_map_grad = in_map_grad + mm(scores_grad.T, out_map)
        at_last = iota((GROUP, LANES), 0) == GROUP - 1
        cumul_grad = cumul_grad + jnp.where(at_last, last_grad, 0.0)
        upper = (iota((GROUP, GROUP), 0) <= iota((GROUP, GROUP), 1)).astype(f32).astype(bf16)
        pieces = split(cumul_grad, 3)
        rated_grad = dot(upper, pieces[2]) + dot(upper, pieces[1]) + dot(upper, pieces[0])
        step_grad = step_grad + rated_grad * rate
        b["HACC"][pl.ds(1, 1), :] += rows_sum(rated_grad * step * rate)
        raw_grad = step_grad * sigmoid(raw)
        b["HACC"][pl.ds(0, 1), :] += rows_sum(raw_grad)
        pre = b["PRE"][tok(g), :]
        sig = sigmoid(pre)
        conv_grad = jnp.concatenate((values_grad, in_map_grad, out_map_grad), axis=1)
        pre_grad = conv_grad * (sig * (1.0 + pre * (1.0 - sig)))
        b["DP"][tok(g), :] = pre_grad
        before = b["CI"][at(g * GROUP, GROUP + 8, 8), :]
        following = jnp.concatenate((pre_grad, b["DP"][at(g * GROUP + GROUP, 8, 8), :]), axis=0)
        total = None
        for k in range(CONV):
            shift = 8 - (CONV - 1) + k
            b["CACC"][pl.ds(k, 1), :] += rows_sum(pre_grad * before[shift : shift + GROUP])
            back = CONV - 1 - k
            term = b["CW"][pl.ds(k, 1), :] * following[back : back + GROUP]
            total = term if total is None else total + term
        b["CACC"][pl.ds(CONV, 1), :] += rows_sum(pre_grad)
        b["PV"][tok(g), :] = total[:, :w].astype(bf16)
        b["PS"][tok(g), :] = jnp.concatenate(
            (total[:, w:], exact(dot_nt, raw_grad, b["SEL"][...], 2)), axis=1
        ).astype(bf16)

    def ssd_back_step(g):
        steps = range(1, nz)
        midway = lambda: between(((fo, 0, steps[2:]), (fh, 1, steps)), g)
        ssd_backward(groups - 1 - g, midway)
        between(((fg, 0, steps),), g)

    each_group(ssd_back_step)

    weight_grad(fv, "NT", "PV")
    weight_grad(fu, "NT", "PV", w // 2)
    block = block_rows // 2

    def shared_block(d, carry):
        left = b["NT"][at(d * block_rows, block_rows, block_rows)]
        b["QS"][d] = dot(left, b["PS"][...]).astype(bf16)
        return carry

    lax.fori_loop(0, dp, shared_block, 0)
    mine_half = lax.rem(s, 2) * block
    pair = site.copy(
        b["QS"].at[:, at(block - mine_half, block, block)], b["QB"], pair_slot, site.twin()
    )
    pair.start()

    pair.wait_recv()

    def add_twin(d, carry):
        both = b["QS"][d, at(mine_half, block, block)].astype(f32) + b["QB"][d].astype(f32)
        b["GS"][at(d * block, block, block)] = both.astype(bf16)
        return carry

    lax.fori_loop(0, dp, add_twin, 0)
    fs.begin()
    for item in (fo, fg, fh):
        item.finish()
    forward((fv, fu), 1)

    def normed_grad(g):
        total = (
            dot_nt(b["PV"][tok(g), :], b["WV"][...])
            + dot_nt(b["PG"][tok(g), :], b["WG"][...])
            + dot_nt(b["PS"][tok(g), :], b["WS"][...])
        )
        b["NP"][tok(g), :] = total.astype(bf16)
        unit = b["XF"][tok(g), :].astype(f32) * b["INV"][tok(g), pl.ds(0, 1)]
        b["PACC"][pl.ds(0, 1), :] += rows_sum(total * unit)

    each_group(normed_grad)
    grads.start()
    forward((fs,), 1)
    forward((fv, fu), 2)
    b["GM"][:, 0, :] = pre_table().blocks(b["PACC"][pl.ds(0, 1), :])
    taps = conv_table()
    for k in range(CONV + 1):
        b["GM"][:, 2 + k, :] = taps.blocks(b["CACC"][pl.ds(k, 1), :])
    skip_grad = per_head(jnp.broadcast_to(b["NACC"][pl.ds(1, 1), :], (8, w)))
    total = jnp.zeros((8, LANES), f32)
    kinds = (b["HACC"][pl.ds(0, 1), :], b["HACC"][pl.ds(1, 1), :], skip_grad[0:1, :])
    for i, row in enumerate(kinds):
        place = iota((LANES, LANES), 1) - s * heads_here - i * HEADS
        source = iota((LANES, LANES), 0)
        move = ((place == source) & (source < heads_here)).astype(f32).astype(bf16)
        total = total + exact(dot, jnp.broadcast_to(row, (8, LANES)), move, 3)
    b["GM"][:, 7, :] = jnp.broadcast_to(total[0:1, :], (owners, LANES))
    fm.begin()
    forward((fs,), 2)
    forward((fv, fu), 3)
    forward((fs,), 3)
    outs.wait()
    total = x_ref[...].astype(f32) + b["OP"][mine, :].astype(f32)
    for k in range(seq - 1):
        total = total + b["OB"][k].astype(f32)
    block_ref[...] = total.astype(bf16)
    grads.wait()
    total = b["NP"][mine, :].astype(f32)
    for k in range(seq - 1):
        total = total + b["NB"][k].astype(f32)
    scaled = total * b["GA"][pl.ds(0, 1), :]
    inverse = b["INV"][mine, pl.ds(0, 1)]
    unit = x_ref[...].astype(f32) * inverse
    mean = lanes_sum(scaled * unit) / width
    ingrad_ref[...] = inverse * (scaled - unit * mean) + cot_ref[...].astype(f32)
    for item in (fm, fv, fu, fs):
        item.finish()
    for item in (fo, fg, fh, fv, fu, fs, fm):
        item.members.wait()
    smalls, shared = b["FM"][0], None
    for q in range(seq):
        outshare_ref[:, pl.ds(q * w, w)] = b["FO"][q].astype(f32)
        inshare_ref[:, pl.ds(q * w, w // 2)] = b["FG"][q].astype(f32)
        inshare_ref[:, pl.ds(q * w + w // 2, w // 2)] = b["FH"][q].astype(f32)
        inshare_ref[:, pl.ds(INNER + q * w, w // 2)] = b["FV"][q].astype(f32)
        inshare_ref[:, pl.ds(INNER + q * w + w // 2, w // 2)] = b["FU"][q].astype(f32)
        if q > 0:
            smalls = smalls + b["FM"][q]
    for j in range(seq // 2):
        part = b["FS"][2 * j + s // (seq // 2)].astype(f32)
        shared = part if shared is None else shared + part
    inshare_ref[:, pl.ds(INNER + INNER, MAPS + HEADS)] = shared[:, : MAPS + HEADS]
    smalls = smalls[0]
    starts = ((0, 0), (1, 0), (2, 0), (6, 0), (7, 0), (7, HEADS), (7, 2 * HEADS))
    for ref, (top, left) in zip(small_refs, starts):
        ref[...] = smalls[top : top + ref.shape[0], left : left + ref.shape[1]]
    for drain in site.pending:
        drain()
    pair.wait_send()


def fused(x, cot, in_weight, out_weight, small, heads, dp, seq):
    length, width = x.shape
    rows, proj = in_weight.shape
    owners = dp * seq
    plan = scratch_plan(dp, seq, length, width, rows)
    names = tuple(plan)
    sems = (11 * (seq - 1 + dp) + (dp - 1) + (seq - 1) + 6 * (seq - 1) + dp + 1, 7)
    vmem = pl.BlockSpec(memory_space=pltpu.VMEM)
    return pl.pallas_call(
        functools.partial(fused_kernel, dp, seq, names, sems),
        out_shape=[
            jax.ShapeDtypeStruct((length, width), bf16),
            jax.ShapeDtypeStruct((length, width), f32),
            jax.ShapeDtypeStruct((rows, proj), f32),
            jax.ShapeDtypeStruct((rows, INNER), f32),
        ]
        + [
            jax.ShapeDtypeStruct(shape, f32)
            for shape in (
                (1, width // owners),
                (1, INNER // owners),
                (CONV, CONV_CH // owners),
                (1, CONV_CH // owners),
                (1, HEADS),
                (1, HEADS),
                (1, HEADS),
            )
        ],
        in_specs=[vmem] * 6,
        out_specs=[vmem] * 11,
        scratch_shapes=[pltpu.VMEM(*plan[name]) for name in names]
        + [
            pltpu.SemaphoreType.DMA((sems[0],)),
            pltpu.SemaphoreType.DMA((sems[0],)),
            pltpu.SemaphoreType.DMA((sems[1],)),
        ],
        compiler_params=pltpu.CompilerParams(
            collective_id=0, has_side_effects=True, vmem_limit_bytes=58 * 2**20
        ),
    )(x, cot, in_weight, out_weight, small, heads)


def place_kernel(count, *refs):
    copies = [
        pltpu.make_async_copy(refs[i], refs[count + i], refs[2 * count].at[i])
        for i in range(count)
    ]
    for copy in copies:
        copy.start()
    for copy in copies:
        copy.wait()


def placed(values):
    count = len(values)
    return pl.pallas_call(
        functools.partial(place_kernel, count),
        out_shape=[jax.ShapeDtypeStruct(value.shape, value.dtype) for value in values],
        in_specs=[pl.BlockSpec(memory_space=pltpu.VMEM)] * count,
        out_specs=[pl.BlockSpec(memory_space=pl.ANY)] * count,
        scratch_shapes=[pltpu.SemaphoreType.DMA((count,))],
    )(*values)


def fits(dp, seq, block_input, in_weight):
    seq_dev, length, width = block_input.shape
    rows = in_weight.shape[0]
    owners = dp * seq
    return (
        seq_dev == 1
        and dp == 2 * RING_HOPS
        and seq % 2 == 0
        and length % GROUP == 0
        and rows % 32 == 0
        and rows <= LANES
        and INNER % (seq * 2 * LANES) == 0
        and INNER % owners == 0
        and CONV_CH % owners == 0
        and CONV_CH // owners <= LANES
        and dp // 2 <= seq * length // GROUP + 1
    )


def spread_rows(values):
    total, first = None, 0
    for value in values:
        value = value.reshape(-1, value.shape[-1]).astype(f32)
        count, size = value.shape
        value = jnp.pad(value, ((first, 8 - first - count), (0, LANES - size)))
        total = value if total is None else total + value
        first += count
    return total


def on_device_fused(
    block_input,
    in_weight,
    out_weight,
    pre_gain,
    norm_gain,
    conv_weight,
    conv_bias,
    dt_bias,
    decay_log,
    skip_gain,
    cotangent,
):
    dp, seq = lax.axis_size("dp"), lax.axis_size("seq")
    small = spread_rows((pre_gain, norm_gain, conv_weight, conv_bias))[None]
    heads = spread_rows((dt_bias, decay_log, skip_gain))
    results = fused(
        block_input[0], cotangent[0], in_weight, out_weight.T, small, heads, dp, seq
    )
    block, in_grad, in_share, out_share, *smalls = placed(results)
    taps = smalls.pop(2)
    pre, norm, bias, dt, decay, skip = (value.reshape(-1) for value in smalls)
    return (
        block[None],
        in_grad[None],
        in_share,
        out_share.T,
        pre,
        norm,
        taps,
        bias,
        dt,
        decay,
        skip,
    )


def from_behind(value, axis, steps):
    count = lax.axis_size(axis)
    leading, last = (max(0, -steps), min(count, count - steps))
    return lax.ppermute(value, axis, [(source, source + steps) for source in range(leading, last)])


def convolve(padded, conv_weight, conv_bias):
    taps = conv_weight.shape[0]
    length = padded.shape[-2] - taps + 1
    total = conv_bias
    for index in range(taps):
        total = total + conv_weight[index] * lax.slice_in_dim(
            padded, index, index + length, axis=padded.ndim - 2
        )
    return total


def running_sum(value):
    length = value.shape[1]
    lower = (jnp.arange(length)[:, None] >= jnp.arange(length)[None, :]).astype(value.dtype)
    return jnp.einsum("ts,bsh->bth", lower, value, precision=lax.Precision.HIGHEST)


def carry_scan(state, decay, axis, sign):
    count = lax.axis_size(axis)
    within, within_decay = state, decay
    entering, entering_decay = None, None
    width = 1
    while width < count:
        moved = from_behind(within.astype(jnp.bfloat16), axis, sign * width).astype(jnp.float32)
        last = 2 * width >= count
        if not last or entering is None:
            moved_decay = from_behind(within_decay, axis, sign * width)
        if entering is None:
            entering, entering_decay = moved, moved_decay
        else:
            entering = entering + entering_decay[:, :, None, None] * moved
            if not last:
                entering_decay = entering_decay * moved_decay
        if not last:
            within = within + within_decay[:, :, None, None] * moved
            within_decay = within_decay * moved_decay
        width *= 2
    return jnp.zeros_like(state) if entering is None else entering


def front_fn(tail, rim, conv_weight, conv_bias, dt_bias, decay_log):
    conv_in = tail[..., :CONV_CH]
    dt_raw = tail[..., CONV_CH:]
    padded = jnp.concatenate([rim, conv_in], axis=-2)
    conv_out = jax.nn.silu(convolve(padded, conv_weight, conv_bias))
    leading = conv_out.shape[:-1]
    values = conv_out[..., :INNER].reshape(leading + (HEADS, HEAD_DIM))
    in_map = conv_out[..., INNER : INNER + STATE]
    out_map = conv_out[..., INNER + STATE :]
    step = jax.nn.softplus(dt_raw + dt_bias)
    cumulative = running_sum(step * -jnp.exp(decay_log))
    return (values, in_map, out_map, step, cumulative)


def group_state(values, in_map, step, cumulative):
    weights_end = jnp.exp(cumulative[-1][None, :] - cumulative) * step
    state = jnp.einsum("shp,sn->hpn", values * weights_end[:, :, None], in_map, precision=highest)
    return (state, jnp.exp(cumulative[-1]))


def group_output(values, in_map, out_map, step, cumulative, carried, skip_gain):
    length = values.shape[0]
    scores = jnp.dot(out_map, in_map.T, precision=highest)
    causal = jnp.arange(length)[:, None] >= jnp.arange(length)[None, :]
    spread = cumulative[:, None, :] - cumulative[None, :, :]
    decay = jnp.exp(jnp.where(causal[:, :, None], spread, -10000.0))
    mixing = scores[:, :, None] * decay * step[None, :, :]
    inner_part = jnp.einsum("tsh,shp->thp", mixing, values, precision=highest)
    carried_part = (
        jnp.einsum("tn,hpn->thp", out_map, carried, precision=highest)
        * jnp.exp(cumulative)[:, :, None]
    )
    return inner_part + carried_part + skip_gain[None, :, None] * values


def state_fn(values, in_map, step, cumulative):
    return jax.vmap(group_state)(values, in_map, step, cumulative)


def out_fn(values, in_map, out_map, step, cumulative, gate_raw, carried, skip_gain, norm_gain):
    ssd_out = jax.vmap(group_output, in_axes=(0, 0, 0, 0, 0, 0, None))(
        values, in_map, out_map, step, cumulative, carried, skip_gain
    )
    ssd_out = ssd_out.reshape(gate_raw.shape)
    gated = ssd_out * jax.nn.silu(gate_raw)
    inverse = lax.rsqrt(jnp.mean(gated * gated, axis=-1, keepdims=True) + epsilon)
    return gated * inverse * norm_gain


def by_rows(grad, owners):
    return grad.reshape(owners, -1)


def by_columns(grad, owners):
    rows = grad.shape[0]
    return jnp.transpose(grad.reshape(rows, owners, -1), (1, 0, 2)).reshape(owners, -1)


def on_device(
    block_input,
    in_weight,
    out_weight,
    pre_gain,
    norm_gain,
    conv_weight,
    conv_bias,
    dt_bias,
    decay_log,
    skip_gain,
    cotangent,
):
    seq_dev, length, width = block_input.shape
    dp, seq = lax.axis_size("dp"), lax.axis_size("seq")
    owners = dp * seq
    both = ("dp", "seq")
    if fits(dp, seq, block_input, in_weight):
        return on_device_fused(
            block_input,
            in_weight,
            out_weight,
            pre_gain,
            norm_gain,
            conv_weight,
            conv_bias,
            dt_bias,
            decay_log,
            skip_gain,
            cotangent,
        )
    small_parts = (pre_gain, norm_gain, conv_weight.reshape(-1), conv_bias)
    small_sizes = [part.size for part in small_parts]
    small = jnp.concatenate(small_parts)
    in_full = lax.all_gather(in_weight, both, axis=0, tiled=True)
    gate_w, tail_w = in_full[:, :INNER], in_full[:, INNER:]
    out_t = lax.all_gather(out_weight.T, both, axis=0, tiled=True)
    small_all = lax.all_gather(small, both, axis=0)
    pieces, start = [], 0
    for size in small_sizes:
        pieces.append(small_all[:, start : start + size])
        start += size
    pre_full, norm_full, conv_b_full = (pieces[i].reshape(-1) for i in (0, 1, 3))
    conv_w_full = jnp.transpose(pieces[2].reshape(owners, CONV, -1), (1, 0, 2)).reshape(CONV, -1)
    pre_float = pre_full.astype(jnp.float32)
    norm_float = norm_full.astype(jnp.float32)
    inputs = block_input.astype(jnp.float32)
    inv_pre = lax.rsqrt(jnp.mean(inputs * inputs, axis=-1, keepdims=True) + epsilon)
    normed = (inputs * inv_pre * pre_float).astype(jnp.bfloat16)
    flat_normed = normed.reshape(seq_dev * length, width)
    gate_raw = jnp.dot(flat_normed, gate_w, preferred_element_type=jnp.float32).reshape(
        seq_dev, length, -1
    )
    tail = jnp.dot(flat_normed, tail_w, preferred_element_type=jnp.float32).reshape(
        seq_dev, length, -1
    )
    conv_in = tail[:, length - (CONV - 1) :, :CONV_CH]
    rim = from_behind(conv_in, "seq", 1)
    front_out, front_pull = jax.vjp(
        front_fn,
        tail,
        rim,
        conv_w_full.astype(jnp.float32),
        conv_b_full.astype(jnp.float32),
        dt_bias,
        decay_log,
    )
    values, in_map, out_map, step, cumulative = front_out
    state_out, state_pull = jax.vjp(state_fn, values, in_map, step, cumulative)
    state, decay = state_out
    carried = carry_scan(state, decay, "seq", 1)
    mixed_float, out_pull = jax.vjp(
        out_fn, values, in_map, out_map, step, cumulative, gate_raw, carried, skip_gain, norm_float
    )
    mixed = mixed_float.astype(jnp.bfloat16)
    flat_mixed = mixed.reshape(seq_dev * length, INNER)
    block_output = (
        inputs
        + jnp.dot(flat_mixed, out_t.T, preferred_element_type=jnp.float32).reshape(
            seq_dev, length, width
        )
    ).astype(jnp.bfloat16)
    flat_grad = cotangent.reshape(seq_dev * length, width)
    mixed_grad = jnp.dot(flat_grad, out_t, preferred_element_type=jnp.float32).reshape(
        seq_dev, length, INNER
    )
    out_w_grad = jnp.dot(flat_grad.T, flat_mixed, preferred_element_type=jnp.float32)
    (
        values_a,
        in_map_a,
        out_map_grad,
        step_a,
        cumul_a,
        gate_grad,
        local_grad,
        skip_grad,
        norm_grad,
    ) = out_pull(mixed_grad)

    later_grad = carry_scan(local_grad, decay, "seq", -1)
    decay_grad = jnp.sum(later_grad * carried, axis=(2, 3))
    values_b, in_map_b, step_b, cumul_b = state_pull((later_grad, decay_grad))
    front_grads = front_pull(
        (
            values_a + values_b,
            in_map_a + in_map_b,
            out_map_grad,
            step_a + step_b,
            cumul_a + cumul_b,
        )
    )
    tail_float, rim_grad, conv_w_grad, conv_b_grad, dt_grad, decay_log_grad = front_grads
    returned = from_behind(rim_grad, "seq", -1)
    tail_float = tail_float + jnp.pad(returned, ((0, 0), (length - (CONV - 1), 0), (0, HEADS)))
    tail_grad = tail_float.astype(jnp.bfloat16).reshape(seq_dev * length, -1)
    gate_grad = gate_grad.astype(jnp.bfloat16).reshape(seq_dev * length, -1)
    gate_w_grad = jnp.dot(flat_normed.T, gate_grad, preferred_element_type=jnp.float32)
    tail_w_grad = jnp.dot(flat_normed.T, tail_grad, preferred_element_type=jnp.float32)
    normed_grad = (
        jnp.dot(gate_grad, gate_w.T, preferred_element_type=jnp.float32)
        + jnp.dot(tail_grad, tail_w.T, preferred_element_type=jnp.float32)
    ).reshape(seq_dev, length, width)
    pre_grad = jnp.sum(normed_grad * inputs * inv_pre, axis=(0, 1))
    scaled = normed_grad * pre_float
    unit = inputs * inv_pre
    input_grad = inv_pre * (
        scaled - unit * jnp.mean(scaled * unit, axis=-1, keepdims=True)
    ) + cotangent.astype(jnp.float32)
    small_grads = jnp.concatenate(
        (
            by_rows(pre_grad, owners),
            by_rows(norm_grad, owners),
            by_columns(conv_w_grad, owners),
            by_rows(conv_b_grad, owners),
        ),
        axis=1,
    )
    heads = jnp.concatenate((dt_grad, decay_log_grad, skip_grad))
    scatter = functools.partial(
        lax.psum_scatter, axis_name=both, scatter_dimension=0, tiled=True
    )
    in_share = scatter(jnp.concatenate((gate_w_grad, tail_w_grad), axis=1))
    out_share = scatter(out_w_grad).T
    small_share = scatter(small_grads)[0]
    heads = lax.psum(heads, both)
    shares, start = [], 0
    for size in small_sizes:
        shares.append(small_share[start : start + size])
        start += size
    pre_share, norm_share, conv_w_share, conv_b_share = shares
    conv_w_share = conv_w_share.reshape(CONV, -1)
    heads_total = (heads[:HEADS], heads[HEADS : 2 * HEADS], heads[2 * HEADS :])
    return (
        block_output,
        input_grad,
        in_share,
        out_share,
        pre_share,
        norm_share,
        conv_w_share,
        conv_b_share,
        heads_total[0],
        heads_total[1],
        heads_total[2],
    )


def solution(mesh):
    in_specs = (
        P("dp", "seq", None),
        P(("dp", "seq"), None),
        P(None, ("dp", "seq")),
        P(("dp", "seq")),
        P(("dp", "seq")),
        P(None, ("dp", "seq")),
        P(("dp", "seq")),
        P(),
        P(),
        P(),
        P("dp", "seq", None),
    )
    out_specs = (
        P("dp", "seq", None),
        P("dp", "seq", None),
        P(("dp", "seq"), None),
        P(None, ("dp", "seq")),
        P(("dp", "seq")),
        P(("dp", "seq")),
        P(None, ("dp", "seq")),
        P(("dp", "seq")),
        P(),
        P(),
        P(),
    )
    return jax.shard_map(
        on_device, mesh=mesh, in_specs=in_specs, out_specs=out_specs, check_vma=False
    )
```
